128 devices in a mesh: row: 8 (over x, core), col: 16 (over y, z).
Axes of the slice: x: 4, y: 4, z: 4, core: 2. Of those that a mesh axis runs over, the one named last changes fastest.
Arguments:
- parent_front: float32 [16384, 16384], P('row', 'col'), as said below
- child_panels: float32 [8, 4096, 512], P('row', 'col'), may hold values from -6 to 6
- child_inverses: float32 [8, 512, 512], P('row'), as said below
- parent_index: int32 [8, 16], replicated, may hold values from 2 to 63, as said below
Outputs:
- panel: float32 [16384, 512], P('row')
- schur: float32 [16384, 16384], P('row', 'col')
The draws below stay inside these ranges and needn't reach their ends.
Inputs may be any that keep to these rules, and one draw needn't show every extreme that they name: `parent_index`: entry (g, u) names the parent tile that receives tile row and tile column u of child g's update. Seen in blocks of 4 consecutive tiles, each child names every block exactly once, and at a given u the children name different blocks. No entry names one of the first 2 tiles. `parent_front`: Symmetric. In its leading 2 * 256 rows and columns, each diagonal entry is positive and exceeds the sum of magnitudes of the other entries of its row within that block. `child_inverses`: each matrix is lower triangular with a positive diagonal.
All inputs are finite; a program needn't handle non-finite values.
Results may differ from the reference program's by a relative error of at most 0.0003.
Values sent between devices are 32-bit elements; how exact they have to be, the bound alone decides.
A program may use at most 128 MiB of HBM per device.

```python
import jax
import jax.numpy as jnp
from jax import lax

TILE = 256
CW = 512
PCT = 4
NSP = 2
CHILDREN = 8
UT = 16
UC = 4096
PT = 64
FP = 16384


def draw_parent_front(key, part):
    key_values = jax.random.fold_in(key, 0)
    key_gain = jax.random.fold_in(key, 2)
    key_lead = jax.random.fold_in(key, 3)
    raw_values = jax.random.uniform(key_values, (FP, FP), jnp.float32, -1.0, 1.0)
    lead_raw = jax.random.uniform(key_lead, (FP, FP), jnp.float32, 0.0, 1.0)
    lead_raw = 0.5 * (lead_raw + lead_raw.T)
    coupling = 4.0 / 3.0
    lead_values = coupling * (0.5 + 0.5 * lead_raw)
    entry_top = 1.0
    symmetric = 0.5 * (raw_values + raw_values.T)
    lead_size = NSP * TILE
    positions = jnp.arange(FP)
    in_lead = positions < lead_size
    lift = 0.5 * jnp.sqrt(entry_top * lead_size)
    crossing = jnp.logical_xor(in_lead[:, None], in_lead[None, :])
    symmetric = symmetric * jnp.where(crossing, lift, 1.0)
    in_block = in_lead[:, None] & in_lead[None, :]
    off_diag = (positions[:, None] != positions[None, :]).astype(jnp.float32)
    symmetric = jnp.where(in_block, lead_values * off_diag, symmetric)
    extra_gain = jax.random.uniform(key_gain, (FP,), jnp.float32, 1.1, 2.0)
    diagonal = jnp.where(in_lead, extra_gain * coupling * (lead_size - 1.0), 0.0)
    return symmetric + jnp.diag(diagonal)


def draw_child_inverses(key, part):
    key_off, key_diag = jax.random.split(key, 2)
    off_diag = jax.random.normal(key_off, (CHILDREN, CW, CW), jnp.float32) / CW
    diagonal = jnp.exp(jax.random.uniform(key_diag, (CHILDREN, CW), jnp.float32, jnp.log(0.5), jnp.log(2.0))) / jnp.sqrt(1.0 * CW)
    rows_ids = jnp.arange(CW)[:, None]
    cols_ids = jnp.arange(CW)[None, :]
    lower_mask = (rows_ids > cols_ids).astype(jnp.float32)
    identity = (rows_ids == cols_ids).astype(jnp.float32)
    return off_diag * lower_mask[None] + diagonal[:, :, None] * identity[None]


def draw_parent_index(key, part):
    key_shift, key_inner, key_low = jax.random.split(key, 3)
    offsets = jax.random.permutation(key_shift, UT)[:CHILDREN]
    block_ids = (jnp.arange(UT)[None, :] + offsets[:, None]) % UT
    inner_ids = jax.random.randint(key_inner, (CHILDREN, UT), 0, PCT)
    low_ids = NSP + jax.random.randint(key_low, (CHILDREN, UT), 0, PCT - NSP)
    first_child = (jnp.arange(CHILDREN) == 0)[:, None]
    low_ids = jnp.where(first_child, NSP, low_ids)
    inner_ids = jnp.where(first_child & (block_ids == UT - 1), PCT - 1, inner_ids)
    inner_ids = jnp.where(block_ids == 0, low_ids, inner_ids)
    return (block_ids * PCT + inner_ids).astype(jnp.int32)


def level_of(stream_key, dims, shards, least, top_value):
    def one(axis_at, parts):
        heights = jax.random.uniform(jax.random.fold_in(jax.random.fold_in(stream_key, 6), axis_at), (parts,), jnp.float32, least / len(shards), top_value / len(shards))
        return jnp.repeat(jnp.exp(heights), dims[axis_at] // parts).reshape((-1,) + (1,) * (len(dims) - axis_at - 1))

    factor_of = one(*shards[0])
    for cut in shards[1:]:
        factor_of = factor_of * one(*cut)
    return factor_of


def scatter_about(rng, dims, scale, most, cuts=(), kind=jnp.bfloat16):
    drawn = jax.random.normal(rng, dims, jnp.float32) * scale
    if len(cuts) > 0:
        drawn = level_of(rng, dims, cuts, -0.22, 0.18) * drawn
    return jnp.clip(drawn, min=-most, max=most).astype(kind)


def setup_inputs(seed: int = 0) -> dict:
    keys = jax.random.split(jax.random.key(seed), 5)
    parent_front = draw_parent_front(jax.random.fold_in(keys[4], 71), 0)
    child_panels = scatter_about(keys[1], (CHILDREN, UC, CW), 1.0, 6.0, ((0, 8), (1, 16)), jnp.float32)
    child_inverses = draw_child_inverses(jax.random.fold_in(keys[4], 71), 0)
    parent_index = draw_parent_index(jax.random.fold_in(keys[4], 71), 0)
    return dict(parent_front=parent_front, child_panels=child_panels, child_inverses=child_inverses, parent_index=parent_index)


def product(matrix_a, matrix_b):
    return jnp.dot(matrix_a.astype(jnp.float32), matrix_b.astype(jnp.float32), precision=lax.Precision.HIGHEST, preferred_element_type=jnp.float32)

def reference(parent_front, child_panels, child_inverses, parent_index):
    tile_grid = parent_front.reshape(PT, TILE, PT, TILE).transpose(0, 2, 1, 3)
    for child_index in range(CHILDREN):
        factor_rows = product(child_panels[child_index], child_inverses[child_index].T)
        update = product(factor_rows, factor_rows.T)
        update = update.reshape(UT, TILE, UT, TILE).transpose(0, 2, 1, 3)
        target = parent_index[child_index].astype(jnp.int32)
        tile_grid = tile_grid.at[target[:, None], target[None, :]].add(-update)
    work_matrix = tile_grid.transpose(0, 2, 1, 3).reshape(FP, FP)
    identity = jnp.eye(TILE, dtype=jnp.float32)
    tile_of_row = jnp.arange(FP) // TILE
    columns = []
    for step in range(NSP):
        offset = step * TILE
        pivot_tile = jnp.linalg.cholesky(work_matrix[offset:offset + TILE, offset:offset + TILE])
        inverse = lax.linalg.triangular_solve(pivot_tile, identity, left_side=True, lower=True)
        column = product(work_matrix[:, offset:offset + TILE], inverse.T)
        column = jnp.where(tile_of_row[:, None] < step, jnp.zeros_like(column), column)
        column = column.at[offset:offset + TILE].set(pivot_tile)
        work_matrix = work_matrix - product(column, column.T)
        columns.append(column)
    return (jnp.concatenate(columns, axis=1), work_matrix)
```

```python
import jax
import jax.numpy as jnp
from jax import lax
from jax.experimental import pallas as pl
from jax.experimental.pallas import tpu as pltpu
from jax.sharding import PartitionSpec as P

TILE = 256
CW = 512
PCT = 4
NSP = 2
ROWS = 8
COLS = 16
SIDE = 4
RT = 8
LEAD = NSP * TILE
PANEL_ROWS = RT * TILE
COL_WIDTH = PCT * TILE
TREE_CHUNKS = 8
MESH = pl.DeviceIdType.MESH
F32 = jnp.float32
BF16 = jnp.bfloat16


def product(matrix_a, matrix_b):
    return jnp.dot(
        matrix_a, matrix_b, precision=lax.Precision.HIGHEST, preferred_element_type=F32
    )


def product_rows(matrix_a, matrix_b):
    return lax.dot_general(
        matrix_a,
        matrix_b,
        (((1,), (1,)), ((), ())),
        precision=lax.Precision.HIGHEST,
        preferred_element_type=F32,
    )


def halves(value):
    high = value.astype(BF16)
    low = (value - high.astype(F32)).astype(BF16)
    return high, low


def three_pass(pair_a, pair_b, contract):
    def one(left, right):
        return lax.dot_general(left, right, (contract, ((), ())), preferred_element_type=F32)

    return one(pair_a[0], pair_b[0]) + (one(pair_a[0], pair_b[1]) + one(pair_a[1], pair_b[0]))


def wrap(value):
    return lax.rem(value + 2 * SIDE, SIDE)


def gather_kernel(
    own_ref, front_ref, all_ref, pan_ref, top_ref, lead_ref, send_sem, recv_sem, local_sem
):
    row = lax.axis_index("row")
    col = lax.axis_index("col")
    place_y = col // SIDE
    place_z = lax.rem(col, SIDE)
    chip = row // 2
    core = lax.rem(row, 2)
    counter = [0]

    def fresh():
        counter[0] += 1
        return counter[0] - 1

    def at(step_y, step_z):
        return wrap(place_y + step_y) * SIDE + wrap(place_z + step_z)

    def remote(src, dst, send, recv, to_row, to_col):
        return pltpu.make_async_remote_copy(
            src_ref=src,
            dst_ref=dst,
            send_sem=send_sem.at[send],
            recv_sem=recv_sem.at[recv],
            device_id=(to_row, to_col),
            device_id_type=MESH,
        )

    barrier = pltpu.get_barrier_semaphore()
    greeted = [
        (row, at(1, 0)),
        (row, at(-1, 0)),
        (row, at(0, 1)),
        (row, at(0, -1)),
        (row + 1 - 2 * core, col),
        (lax.rem(row + 2, ROWS), col),
        (lax.rem(row + 6, ROWS), col),
    ]
    for who in greeted:
        pl.semaphore_signal(barrier, inc=1, device_id=who, device_id_type=MESH)
    pl.semaphore_wait(barrier, len(greeted))

    started = []
    keep_own = pltpu.make_async_copy(own_ref, all_ref.at[col], local_sem.at[0])
    keep_own.start()

    def ring_events(half):
        if half == 0:
            place = lambda i, j: at(j, i)
        else:
            place = lambda i, j: at(i, j)
        base = half * 128
        sem = {}

        def key(*name):
            if name not in sem:
                sem[name] = fresh()
            return sem[name]

        def rows_of(part):
            if part == 0:
                return pl.ds(base, 128)
            return pl.ds(base, 64) if part == 1 else pl.ds(base + 64, 64)

        def make(i, j, part, to_i, to_j, name):
            source = own_ref if (i, j) == (0, 0) else all_ref.at[place(i, j)]
            return remote(
                source.at[rows_of(part)],
                all_ref.at[place(i, j), rows_of(part)],
                key(*name),
                key(*name),
                row,
                place(to_i, to_j),
            )

        pending = {}

        def go(name, *args):
            copy = make(*args, name)
            copy.start()
            pending[name] = copy
            started.append((copy, None))

        def arrived(name):
            pending[name].wait_recv()

        def quarter(d):
            return 1 if d == 1 else 2

        def first():
            for d in (1, -1):
                go(("a", d), 0, 0, 0, d, 0)

        def second():
            for e in (1, -1):
                go(("b", 0, e), 0, 0, 0, 0, e)

        def near(d):
            arrived(("a", d))
            go(("af", d), -d, 0, quarter(d), d, 0)
            for e in (1, -1):
                go(("b", -d, e), -d, 0, 0, 0, e)

        def far():
            arrived(("af", 1))
            arrived(("af", -1))
            for e in (1, -1):
                go(("b", 2, e), 2, 0, 0, 0, e)

        def cross(i):
            for e in (1, -1):
                arrived(("b", i, e))
                go(("bf", i, e), i, -e, quarter(e), 0, e)

        def last(i):
            for e in (1, -1):
                arrived(("bf", i, e))

        return first, second, near, far, cross, last

    root = col == 0
    trees = []
    for along_z, sign in ((True, 1), (True, -1), (False, 1), (False, -1)):
        place_a = wrap(sign * (place_z if along_z else place_y))
        place_b = wrap(sign * (place_y if along_z else place_z))
        to_a = at(0, sign) if along_z else at(sign, 0)
        to_b = at(sign, 0) if along_z else at(0, sign)
        send_a = ((place_b == 0) & (place_a < 3)) | ((place_b >= 1) & (place_a == 3))
        send_b = (place_a >= 1) & (place_b < 3)
        trees.append((to_a, to_b, send_a, send_b))

    def tree_event(tree, chunk):
        to_a, to_b, send_a, send_b = trees[tree]
        index_a, index_b = fresh(), fresh()
        size = LEAD // TREE_CHUNKS
        block = pan_ref.at[pl.ds(tree * LEAD + chunk * size, size)]
        copy_a = remote(block, block, index_a, index_a, row, to_a)
        copy_b = remote(block, block, index_b, index_a, row, to_b)

        def run():
            @pl.when(jnp.logical_not(root))
            def _():
                copy_a.wait_recv()

            @pl.when(send_a)
            def _():
                copy_a.start()

            @pl.when(send_b)
            def _():
                copy_b.start()

        started.append((copy_a, send_a))
        started.append((copy_b, send_b))
        return run

    def row_event(block):
        index_p, index_u, index_d = fresh(), fresh(), fresh()

        def build(part):
            return (
                remote(block, block, index_p, index_p, row + 1, col),
                remote(block, block, index_u, index_p, lax.rem(row + 2, ROWS), col),
                remote(block, block, index_d, index_p, lax.rem(row + 6, ROWS), col),
            )

        def run(part):
            partner, up, down = build(part)
            send_p = core == 0
            send_u = (core == 0) & ((chip == 0) | ((chip == 1) if part == 0 else (chip < 0)))
            send_d = (core == 0) & ((chip == 0) | ((chip == 3) if part == 1 else (chip < 0)))

            @pl.when(row != 0)
            def _():
                partner.wait_recv()

            for copy, flag in ((up, send_u), (down, send_d), (partner, send_p)):

                @pl.when(flag)
                def _(copy=copy):
                    copy.start()

                started.append((copy, flag))

        return run

    load_panel = pltpu.make_async_copy(
        front_ref.at[:, pl.ds(0, LEAD)], pan_ref, local_sem.at[1]
    )
    load_top = pltpu.make_async_copy(front_ref.at[pl.ds(0, LEAD)], top_ref, local_sem.at[2])

    @pl.when(root)
    def _():
        load_panel.start()

    @pl.when(row == 0)
    def _():
        load_top.start()

    z_ring = ring_events(0)
    y_ring = ring_events(1)
    for ring in (z_ring, y_ring):
        ring[0]()
    for ring in (z_ring, y_ring):
        ring[1]()

    @pl.when(root)
    def _():
        load_panel.wait()

    @pl.when(row == 0)
    def _():
        load_top.wait()

    tops = [row_event(top_ref.at[pl.ds(h * TILE, TILE)]) for h in range(2)]
    leads = [row_event(lead_ref.at[pl.ds(h * TILE, TILE)]) for h in range(2)]
    chunk_events = [
        [tree_event(tree, chunk) for tree in range(4)] for chunk in range(TREE_CHUNKS)
    ]

    def tree_round(chunk):
        for run in chunk_events[chunk]:
            run()

    ring_steps = []
    for d in (1, -1):
        for ring in (z_ring, y_ring):
            ring_steps.append((ring[2], d))
    for i in (0,):
        for ring in (z_ring, y_ring):
            ring_steps.append((ring[4], i))
    for ring in (z_ring, y_ring):
        ring_steps.append((ring[3],))
    for i in (1, -1, 2):
        for ring in (z_ring, y_ring):
            ring_steps.append((ring[4], i))
    for i in (0, 1, -1, 2):
        for ring in (z_ring, y_ring):
            ring_steps.append((ring[5], i))
    done_top = [False, False]

    def run_top(h):
        tops[h](h)

    for number, step in enumerate(ring_steps):
        if number == 0:
            run_top(0)
        if number == 6:
            run_top(1)
        step[0](*step[1:])
        if number >= 2 and number % 2 == 0 and (number - 2) // 2 < TREE_CHUNKS:
            tree_round((number - 2) // 2)
    for chunk in range(TREE_CHUNKS):
        if 2 + 2 * chunk >= len(ring_steps):
            tree_round(chunk)
    move_lead = pltpu.make_async_copy(pan_ref.at[pl.ds(0, LEAD)], lead_ref, local_sem.at[3])

    @pl.when(row == 0)
    def _():
        move_lead.start()
        move_lead.wait()

    for h in range(2):
        leads[h](h)
    keep_own.wait()
    for copy, flag in started:
        if flag is None:
            copy.wait_send()
        else:

            @pl.when(flag)
            def _(copy=copy):
                copy.wait_send()


def gather_all(own_factor, front):
    anywhere = pl.BlockSpec(memory_space=pl.ANY)
    vmem = pl.BlockSpec(memory_space=pltpu.VMEM)
    return pl.pallas_call(
        gather_kernel,
        out_shape=(
            jax.ShapeDtypeStruct((COLS, TILE, CW), F32),
            jax.ShapeDtypeStruct((PANEL_ROWS, LEAD), F32),
            jax.ShapeDtypeStruct((LEAD, COL_WIDTH), F32),
            jax.ShapeDtypeStruct((LEAD, LEAD), F32),
        ),
        in_specs=[vmem, anywhere],
        out_specs=(vmem, vmem, vmem, vmem),
        scratch_shapes=[
            pltpu.SemaphoreType.DMA((128,)),
            pltpu.SemaphoreType.DMA((128,)),
            pltpu.SemaphoreType.DMA((4,)),
        ],
        compiler_params=pltpu.CompilerParams(
            collective_id=0, has_side_effects=True, vmem_limit_bytes=40 * 2**20
        ),
        name="gather",
    )(own_factor, front)


def tiles_kernel(order_ref, left_ref, right_ref, out_ref):
    out_ref[0] = three_pass(halves(left_ref[0]), halves(right_ref[0]), ((1,), (1,)))


def update_tiles(order, factors):
    return pl.pallas_call(
        tiles_kernel,
        out_shape=jax.ShapeDtypeStruct((COLS, TILE, TILE), F32),
        grid_spec=pltpu.PrefetchScalarGridSpec(
            num_scalar_prefetch=1,
            grid=(COLS,),
            in_specs=[
                pl.BlockSpec((1, TILE, CW), lambda i, order: (order[i], 0, 0)),
                pl.BlockSpec((1, TILE, CW), lambda i, order: (order[COLS], 0, 0)),
            ],
            out_specs=pl.BlockSpec((1, TILE, TILE), lambda i, order: (i, 0, 0)),
        ),
        cost_estimate=pl.CostEstimate(
            flops=6 * COLS * TILE * TILE * CW, bytes_accessed=12 * 2**20, transcendentals=0
        ),
        name="tiles",
    )(order, factors, factors)


def schur_kernel(rows_ref, cols_ref, front_ref, panel_ref, top_ref, tiles_ref, out_ref):
    step = pl.program_id(0)
    out_ref[...] = front_ref[...] - three_pass(
        halves(panel_ref[...]), halves(top_ref[...]), ((1,), (0,))
    )
    block = step // PCT
    for child in range(ROWS):

        @pl.when(rows_ref[child, block] == step)
        def _(child=child):
            start = pl.multiple_of(cols_ref[child] * TILE, TILE)
            out_ref[:, pl.ds(start, TILE)] -= tiles_ref[child, 0]


def schur_update(row_places, col_places, front, panel, top, tiles):
    return pl.pallas_call(
        schur_kernel,
        out_shape=jax.ShapeDtypeStruct((PANEL_ROWS, COL_WIDTH), F32),
        grid_spec=pltpu.PrefetchScalarGridSpec(
            num_scalar_prefetch=2,
            grid=(RT,),
            in_specs=[
                pl.BlockSpec((TILE, COL_WIDTH), lambda i, *_: (i, 0)),
                pl.BlockSpec((TILE, LEAD), lambda i, *_: (i, 0)),
                pl.BlockSpec((LEAD, COL_WIDTH), lambda i, *_: (0, 0)),
                pl.BlockSpec((ROWS, 1, TILE, TILE), lambda i, *_: (0, i // PCT, 0, 0)),
            ],
            out_specs=pl.BlockSpec((TILE, COL_WIDTH), lambda i, *_: (i, 0)),
        ),
        cost_estimate=pl.CostEstimate(
            flops=6 * PANEL_ROWS * COL_WIDTH * LEAD,
            bytes_accessed=26 * 2**20,
            transcendentals=0,
        ),
        name="schur",
    )(row_places, col_places, front, panel, top, tiles)


def per_device(parent_front, child_panels, child_inverses, parent_index):
    here_row = lax.axis_index("row")
    here_col = lax.axis_index("col")
    own_factor = product_rows(child_panels[0], child_inverses[0])
    factors, panel, top, lead = gather_all(own_factor, parent_front)

    block_of = parent_index // PCT
    my_blocks = lax.dynamic_index_in_dim(block_of, here_row, 0, keepdims=False)
    ids = jnp.arange(COLS, dtype=jnp.int32)
    wanted = jnp.concatenate([ids, here_col[None].astype(jnp.int32)])
    order = jnp.sum(jnp.where(my_blocks[None, :] == wanted[:, None], ids[None, :], 0), axis=1)
    outgoing = update_tiles(order, factors).reshape(ROWS, 2, TILE, TILE)
    tiles = lax.all_to_all(outgoing, "row", split_axis=0, concat_axis=0, tiled=True)

    row_blocks = 2 * here_row + jnp.arange(2, dtype=jnp.int32)
    row_places = (
        jnp.sum(
            jnp.where(
                block_of[:, None, :] == row_blocks[None, :, None], parent_index[:, None, :], 0
            ),
            axis=2,
        )
        - here_row * RT
    )
    col_places = (
        jnp.sum(jnp.where(block_of == here_col, parent_index, 0), axis=1) - here_col * PCT
    )

    identity = jnp.eye(TILE, dtype=F32)
    pivot_0 = jnp.linalg.cholesky(lead[:TILE, :TILE])
    inverse_0 = lax.linalg.triangular_solve(pivot_0, identity, left_side=True, lower=True)
    below = product_rows(lead[TILE:, :TILE], inverse_0)
    pivot_1 = jnp.linalg.cholesky(lead[TILE:, TILE:] - product_rows(below, below))
    inverse_1 = lax.linalg.triangular_solve(pivot_1, identity, left_side=True, lower=True)

    tile_row = here_row * RT + jnp.arange(PANEL_ROWS) // TILE
    panel_0 = product_rows(panel[:, :TILE], inverse_0)
    panel_1 = product_rows(panel[:, TILE:] - product_rows(panel_0, below), inverse_1)
    first = here_row == 0
    panel_0 = panel_0.at[:TILE].set(jnp.where(first, pivot_0, panel_0[:TILE]))
    panel_1 = panel_1.at[:TILE].set(jnp.where(first, 0.0, panel_1[:TILE]))
    panel_1 = panel_1.at[TILE:LEAD].set(jnp.where(first, pivot_1, panel_1[TILE:LEAD]))
    panel_out = jnp.concatenate([panel_0, panel_1], axis=1)

    top_0 = product(inverse_0, top[:TILE])
    top_1 = product(inverse_1, top[TILE:] - product(below, top_0))
    first = here_col == 0
    top_0 = top_0.at[:, :TILE].set(jnp.where(first, pivot_0.T, top_0[:, :TILE]))
    top_1 = top_1.at[:, :TILE].set(jnp.where(first, 0.0, top_1[:, :TILE]))
    top_1 = top_1.at[:, TILE:LEAD].set(jnp.where(first, pivot_1.T, top_1[:, TILE:LEAD]))
    top_out = jnp.concatenate([top_0, top_1], axis=0)

    schur = schur_update(
        row_places.astype(jnp.int32),
        col_places.astype(jnp.int32),
        parent_front,
        panel_out,
        top_out,
        tiles,
    )
    return (panel_out, schur)


def solution(mesh):
    placed = (P("row", "col"), P("row", "col", None), P("row", None, None), P())
    return jax.shard_map(
        per_device,
        mesh=mesh,
        in_specs=placed,
        out_specs=(P("row", None), P("row", "col")),
        check_vma=False,
    )
```

```python
import jax
import jax.numpy as jnp
from jax import lax
from jax.experimental import pallas as pl
from jax.experimental.pallas import tpu as pltpu
from jax.sharding import PartitionSpec as P

TILE = 256
CW = 512
PCT = 4
NSP = 2
ROWS = 8
COLS = 16
SIDE = 4
RT = 8
LEAD = NSP * TILE
PANEL_ROWS = RT * TILE
COL_WIDTH = PCT * TILE
SLICE = LEAD // COLS
TOP_PIECES = 8
TOP_OVERLAP = 8
MESH = pl.DeviceIdType.MESH
F32 = jnp.float32
BF16 = jnp.bfloat16


def product(matrix_a, matrix_b):
    return jnp.dot(
        matrix_a, matrix_b, precision=lax.Precision.HIGHEST, preferred_element_type=F32
    )


def product_rows(matrix_a, matrix_b):
    return lax.dot_general(
        matrix_a,
        matrix_b,
        (((1,), (1,)), ((), ())),
        precision=lax.Precision.HIGHEST,
        preferred_element_type=F32,
    )


def halves(value):
    high = value.astype(BF16)
    low = (value - high.astype(F32)).astype(BF16)
    return high, low


def three_pass(pair_a, pair_b, contract):
    def one(left, right):
        return lax.dot_general(left, right, (contract, ((), ())), preferred_element_type=F32)

    return one(pair_a[0], pair_b[0]) + (one(pair_a[0], pair_b[1]) + one(pair_a[1], pair_b[0]))


def wrap(value):
    return lax.rem(value + 2 * SIDE, SIDE)


def gather_kernel(own_ref, front_ref, all_ref, pan_ref, top_ref, send_sem, recv_sem, local_sem):
    row = lax.axis_index("row")
    col = lax.axis_index("col")
    place_y = col // SIDE
    place_z = lax.rem(col, SIDE)
    chip = row // 2
    core = lax.rem(row, 2)
    counter = [0]

    def fresh(count=1):
        counter[0] += count
        return counter[0] - count

    def at(step_y, step_z):
        return wrap(place_y + step_y) * SIDE + wrap(place_z + step_z)

    def remote(src, dst, send, recv, to_row, to_col):
        return pltpu.make_async_remote_copy(
            src_ref=src,
            dst_ref=dst,
            send_sem=send_sem.at[send],
            recv_sem=recv_sem.at[recv],
            device_id=(to_row, to_col),
            device_id_type=MESH,
        )

    load_top = pltpu.make_async_copy(front_ref.at[pl.ds(0, LEAD)], top_ref, local_sem.at[0])

    @pl.when(row == 0)
    def _():
        load_top.start()

    keep_own = pltpu.make_async_copy(own_ref, all_ref.at[col], local_sem.at[1])
    keep_own.start()

    barrier = pltpu.get_barrier_semaphore()
    greeted = [(row, lax.rem(col + k, COLS)) for k in range(1, COLS)]
    greeted += [
        (row + 1 - 2 * core, col),
        (lax.rem(row + 2, ROWS), col),
        (lax.rem(row + 6, ROWS), col),
    ]
    for who in greeted:
        pl.semaphore_signal(barrier, inc=1, device_id=who, device_id_type=MESH)
    pl.semaphore_wait(barrier, len(greeted))

    started = []

    def ring(half, piece, own):
        if half == 0:
            place = lambda i, j: at(j, i)
        else:
            place = lambda i, j: at(i, j)
        sem = {}

        def key(name):
            if name not in sem:
                sem[name] = fresh()
            return sem[name]

        pending = {}

        def go(name, i, j, part, to_i, to_j):
            source = own if (i, j) == (0, 0) else piece(place(i, j), half, part)
            copy = remote(
                source,
                piece(place(i, j), half, part),
                key(name),
                key(name),
                row,
                place(to_i, to_j),
            )
            copy.start()
            pending[name] = copy
            started.append((copy, None))

        def arrived(name):
            pending[name].wait_recv()

        def quarter(d):
            return 1 if d == 1 else 2

        def first():
            for d in (1, -1):
                go(("a", d), 0, 0, 0, d, 0)

        def second():
            for e in (1, -1):
                go(("b", 0, e), 0, 0, 0, 0, e)

        def near(d):
            arrived(("a", d))
            go(("af", d), -d, 0, quarter(d), d, 0)
            for e in (1, -1):
                go(("b", -d, e), -d, 0, 0, 0, e)

        def far():
            arrived(("af", 1))
            arrived(("af", -1))
            for e in (1, -1):
                go(("b", 2, e), 2, 0, 0, 0, e)

        def cross(i):
            for e in (1, -1):
                arrived(("b", i, e))
                go(("bf", i, e), i, -e, quarter(e), 0, e)

        def last(i):
            for e in (1, -1):
                arrived(("bf", i, e))

        return first, second, near, far, cross, last

    def ring_steps(rings):
        def each(index, *args):
            return [lambda r=r: r[index](*args) for r in rings]

        steps = each(0) + each(1) + each(2, 1) + each(2, -1) + each(4, 0) + each(3)
        for i in (1, -1, 2):
            steps += each(4, i)
        for i in (0, 1, -1, 2):
            steps += each(5, i)
        return steps

    def factor_piece(slot, half, part):
        if part == 0:
            return all_ref.at[slot, pl.ds(half * 128, 128)]
        return all_ref.at[slot, pl.ds(half * 128 + 64 * (part - 1), 64)]

    def panel_piece(slot, half, part):
        if part == 0:
            return pan_ref.at[half, pl.ds(slot * SLICE, SLICE)]
        size = SLICE // 2
        return pan_ref.at[half, pl.ds(slot * SLICE + size * (part - 1), size)]

    factor_rings = [ring(h, factor_piece, own_ref.at[pl.ds(h * 128, 128)]) for h in range(2)]
    panel_rings = [ring(h, panel_piece, panel_piece(col, h, 0)) for h in range(2)]

    top_size = LEAD // TOP_PIECES
    half_pieces = TOP_PIECES // 2
    top_recv = fresh(TOP_PIECES)
    top_next = fresh(TOP_PIECES)
    top_side = fresh(TOP_PIECES)

    def top_copies(piece, way):
        block = top_ref.at[pl.ds(piece * top_size, top_size)]
        onward = lax.rem(row + (2 if way == 1 else 6), ROWS)
        return (
            remote(block, block, top_next + piece, top_recv + piece, onward, col),
            remote(block, block, top_side + piece, top_recv + piece, row + 1 - 2 * core, col),
        )

    def top_step(number):
        for way in (1, -1):
            depth = chip if way == 1 else lax.rem(SIDE - chip, SIDE)
            count = number - depth - core
            piece = 2 * count + (0 if way == 1 else 1)

            @pl.when((count >= 0) & (count < half_pieces))
            def _(piece=piece, way=way, depth=depth):
                onward, side = top_copies(piece, way)

                @pl.when(row != 0)
                def _():
                    side.wait_recv()

                @pl.when((core == 0) & (depth < SIDE - 1))
                def _():
                    onward.start()

                @pl.when(core == 0)
                def _():
                    side.start()

    def top_drain(number):
        for way in (1, -1):
            depth = chip if way == 1 else lax.rem(SIDE - chip, SIDE)
            onward, side = top_copies(2 * number + (0 if way == 1 else 1), way)

            @pl.when((core == 0) & (depth < SIDE - 1))
            def _():
                onward.wait_send()

            @pl.when(core == 0)
            def _():
                side.wait_send()

    spread = []
    for half in range(2):
        spread.append((half, 2 * row + half, pl.ds(0, COL_WIDTH), pl.ds(0, COL_WIDTH)))
        spread.append((half, 0, pl.ds(half * TILE, TILE), pl.ds(COL_WIDTH, TILE)))
    spread_recv = [fresh() for _ in spread]
    spread_send = [fresh(COLS) for _ in spread]

    def spread_copy(index, step):
        half, _, lanes, to_lanes = spread[index]
        to_col = lax.rem(col + step, COLS)
        rows = pl.ds(to_col * SLICE, SLICE)
        return remote(
            top_ref.at[rows, lanes],
            pan_ref.at[half, rows, to_lanes],
            spread_send[index] + step,
            spread_recv[index],
            row,
            to_col,
        )

    def spread_start(index):
        half, holder, lanes, to_lanes = spread[index]
        rows = pl.ds(col * SLICE, SLICE)

        @pl.when(col == holder)
        def _():
            keep = pltpu.make_async_copy(
                top_ref.at[rows, lanes], pan_ref.at[half, rows, to_lanes], local_sem.at[2 + index]
            )
            keep.start()

            @pl.loop(1, COLS)
            def _(step):
                spread_copy(index, step).start()

            keep.wait()

    def spread_wait(index):
        @pl.when(col != spread[index][1])
        def _():
            spread_copy(index, 1).wait_recv()

    def spread_drain(index):
        @pl.when(col == spread[index][1])
        def _():
            @pl.loop(1, COLS)
            def _(step):
                spread_copy(index, step).wait_send()

    factor_steps = ring_steps(factor_rings)
    panel_steps = ring_steps(panel_rings)
    for run in factor_steps[:4]:
        run()

    @pl.when(row == 0)
    def _():
        load_top.wait()

    top_steps = half_pieces + SIDE
    for number in range(top_steps):
        top_step(number)
        if 4 + number < TOP_OVERLAP:
            factor_steps[4 + number]()
    for number in (1, 3, 0, 2):
        spread_start(number)
    for run in factor_steps[TOP_OVERLAP:]:
        run()
    for number in range(len(spread)):
        spread_wait(number)
    for run in panel_steps:
        run()
    keep_own.wait()
    for copy, _ in started:
        copy.wait_send()
    for number in range(half_pieces):
        top_drain(number)
    for number in range(len(spread)):
        spread_drain(number)


def gather_all(own_factor, front):
    anywhere = pl.BlockSpec(memory_space=pl.ANY)
    vmem = pl.BlockSpec(memory_space=pltpu.VMEM)
    return pl.pallas_call(
        gather_kernel,
        out_shape=(
            jax.ShapeDtypeStruct((COLS, TILE, CW), F32),
            jax.ShapeDtypeStruct((2, LEAD, COL_WIDTH + TILE), F32),
            jax.ShapeDtypeStruct((LEAD, COL_WIDTH), F32),
        ),
        in_specs=[vmem, anywhere],
        out_specs=(vmem, vmem, vmem),
        scratch_shapes=[
            pltpu.SemaphoreType.DMA((192,)),
            pltpu.SemaphoreType.DMA((192,)),
            pltpu.SemaphoreType.DMA((6,)),
        ],
        compiler_params=pltpu.CompilerParams(
            collective_id=0, has_side_effects=True, vmem_limit_bytes=40 * 2**20
        ),
        name="gather",
    )(own_factor, front)


BLOCK = 128
GROUP = 8
GROUPS = BLOCK // GROUP


def eliminate(block_ref, upper_ref, inverse_ref):
    lanes = lax.broadcasted_iota(jnp.int32, (GROUP, BLOCK), 1)
    sublanes = lax.broadcasted_iota(jnp.int32, (GROUP, BLOCK), 0)
    left = [block_ref[GROUP * g : GROUP * (g + 1), :] for g in range(GROUPS)]
    right = [jnp.where(lanes == sublanes + GROUP * g, 1.0, 0.0) for g in range(GROUPS)]
    for j in range(BLOCK):
        g, s = j // GROUP, j % GROUP
        pivot_row = jnp.broadcast_to(left[g][s : s + 1, :], (GROUP, BLOCK))
        right_row = jnp.broadcast_to(right[g][s : s + 1, :], (GROUP, BLOCK))
        recip = 1.0 / jnp.broadcast_to(pivot_row[:, j : j + 1], (GROUP, BLOCK))
        for i in range(g, GROUPS):
            ratio = jnp.broadcast_to(left[i][:, j : j + 1], (GROUP, BLOCK)) * recip
            if i == g:
                if s == GROUP - 1:
                    continue
                ratio = jnp.where(sublanes > s, ratio, 0.0)
            left[i] = left[i] - ratio * pivot_row
            right[i] = right[i] - ratio * right_row
    for g in range(GROUPS):
        on_diag = lanes == sublanes + GROUP * g
        scale = 1.0 / jnp.sqrt(jnp.sum(jnp.where(on_diag, left[g], 0.0), axis=1, keepdims=True))
        upper = jnp.where(lanes >= sublanes + GROUP * g, left[g] * scale, 0.0)
        upper_ref[GROUP * g : GROUP * (g + 1), :] = upper
        inverse_ref[GROUP * g : GROUP * (g + 1), :] = right[g] * scale


def panel_kernel(
    pan_ref, top_ref, panel_ref, cols_ref, block_ref, upper_ref, inv_ref, side_ref, low_ref,
    work_ref, full_ref,
):
    row = lax.axis_index("row")
    col = lax.axis_index("col")
    lead = [pan_ref.at[h, :, pl.ds(COL_WIDTH, TILE)] for h in range(2)]
    near = slice(0, BLOCK)
    away = slice(BLOCK, TILE)

    def join_inverse(tile):
        first, second, side = inv_ref[2 * tile], inv_ref[2 * tile + 1], side_ref[tile]
        full_ref[tile, near, near] = first
        full_ref[tile, near, away] = jnp.zeros((BLOCK, BLOCK), F32)
        full_ref[tile, away, near] = -product(second, product(side, first))
        full_ref[tile, away, away] = second

    def second_half(tile, below, corner):
        side = product_rows(below, inv_ref[2 * tile])
        side_ref[tile] = side
        block_ref[...] = corner - product_rows(side, side)

    def body(number, carry):
        @pl.when(number == 0)
        def _():
            block_ref[...] = lead[0][near, near]

        @pl.when(number == 1)
        def _():
            second_half(0, lead[0][away, near], lead[0][away, away])

        @pl.when(number == 2)
        def _():
            join_inverse(0)
            low = product_rows(lead[0][TILE:, :], full_ref[0])
            low_ref[...] = low
            work_ref[...] = lead[1][TILE:, :] - product_rows(low, low)
            block_ref[...] = work_ref[near, near]

        @pl.when(number == 3)
        def _():
            second_half(1, work_ref[away, near], work_ref[away, away])

        eliminate(block_ref, upper_ref.at[number], inv_ref.at[number])
        return carry

    lax.fori_loop(0, 4, body, 0)
    join_inverse(1)

    inverses = [halves(full_ref[t]) for t in range(2)]
    low = halves(low_ref[...])

    def chunk(source, lanes):
        first = three_pass(inverses[0], halves(source[:TILE, lanes]), ((1,), (0,)))
        rest = source[TILE:, lanes] - three_pass(low, halves(first), ((1,), (0,)))
        return first, three_pass(inverses[1], halves(rest), ((1,), (0,)))

    @pl.loop(0, PCT)
    def _(part):
        lanes = pl.ds(pl.multiple_of(part * TILE, TILE), TILE)
        first, second = chunk(top_ref, lanes)
        cols_ref[:TILE, lanes] = first
        cols_ref[TILE:, lanes] = second

    @pl.loop(0, RT)
    def _(part):
        lanes = pl.ds(pl.multiple_of(lax.rem(part, PCT) * TILE, TILE), TILE)
        rows = pl.ds(pl.multiple_of(part * TILE, TILE), TILE)
        first, second = chunk(pan_ref.at[part // PCT], lanes)
        panel_ref[rows, :TILE] = first.T
        panel_ref[rows, TILE:] = second.T

    blank = jnp.zeros((BLOCK, BLOCK), F32)

    @pl.when(col == 0)
    def _():
        for t in range(2):
            for r, c, value in (
                (0, 0, upper_ref[2 * t]),
                (0, 1, side_ref[t].T),
                (1, 0, blank),
                (1, 1, upper_ref[2 * t + 1]),
            ):
                r0, c0 = t * TILE + r * BLOCK, t * TILE + c * BLOCK
                cols_ref[r0 : r0 + BLOCK, c0 : c0 + BLOCK] = value
        cols_ref[TILE:, :TILE] = jnp.zeros((TILE, TILE), F32)

    @pl.when(row == 0)
    def _():
        for t in range(2):
            for r, c, value in (
                (0, 0, upper_ref[2 * t].T),
                (0, 1, blank),
                (1, 0, side_ref[t]),
                (1, 1, upper_ref[2 * t + 1].T),
            ):
                r0, c0 = t * TILE + r * BLOCK, t * TILE + c * BLOCK
                panel_ref[r0 : r0 + BLOCK, c0 : c0 + BLOCK] = value
        panel_ref[:TILE, TILE:] = jnp.zeros((TILE, TILE), F32)


def factor_panel(pan, top):
    vmem = pl.BlockSpec(memory_space=pltpu.VMEM)
    return pl.pallas_call(
        panel_kernel,
        out_shape=(
            jax.ShapeDtypeStruct((PANEL_ROWS, LEAD), F32),
            jax.ShapeDtypeStruct((LEAD, COL_WIDTH), F32),
        ),
        in_specs=[vmem, vmem],
        out_specs=(vmem, vmem),
        scratch_shapes=[
            pltpu.VMEM((BLOCK, BLOCK), F32),
            pltpu.VMEM((4, BLOCK, BLOCK), F32),
            pltpu.VMEM((4, BLOCK, BLOCK), F32),
            pltpu.VMEM((2, BLOCK, BLOCK), F32),
            pltpu.VMEM((TILE, TILE), F32),
            pltpu.VMEM((TILE, TILE), F32),
            pltpu.VMEM((2, TILE, TILE), F32),
        ],
        compiler_params=pltpu.CompilerParams(vmem_limit_bytes=40 * 2**20),
        cost_estimate=pl.CostEstimate(
            flops=60 * 10**9, bytes_accessed=14 * 2**20, transcendentals=0
        ),
        name="panel",
    )(pan, top)


def tiles_kernel(order_ref, left_ref, right_ref, out_ref):
    out_ref[0] = three_pass(halves(left_ref[0]), halves(right_ref[0]), ((1,), (1,)))


def update_tiles(order, factors):
    return pl.pallas_call(
        tiles_kernel,
        out_shape=jax.ShapeDtypeStruct((COLS, TILE, TILE), F32),
        grid_spec=pltpu.PrefetchScalarGridSpec(
            num_scalar_prefetch=1,
            grid=(COLS,),
            in_specs=[
                pl.BlockSpec((1, TILE, CW), lambda i, order: (order[i], 0, 0)),
                pl.BlockSpec((1, TILE, CW), lambda i, order: (order[COLS], 0, 0)),
            ],
            out_specs=pl.BlockSpec((1, TILE, TILE), lambda i, order: (i, 0, 0)),
        ),
        cost_estimate=pl.CostEstimate(
            flops=6 * COLS * TILE * TILE * CW, bytes_accessed=12 * 2**20, transcendentals=0
        ),
        name="tiles",
    )(order, factors, factors)


def schur_kernel(rows_ref, cols_ref, front_ref, panel_ref, top_ref, tiles_ref, out_ref):
    step = pl.program_id(0)
    out_ref[...] = front_ref[...] - three_pass(
        halves(panel_ref[...]), halves(top_ref[...]), ((1,), (0,))
    )
    block = step // PCT
    for child in range(ROWS):

        @pl.when(rows_ref[child, block] == step)
        def _(child=child):
            start = pl.multiple_of(cols_ref[child] * TILE, TILE)
            out_ref[:, pl.ds(start, TILE)] -= tiles_ref[child, 0]


def schur_update(row_places, col_places, front, panel, top, tiles):
    return pl.pallas_call(
        schur_kernel,
        out_shape=jax.ShapeDtypeStruct((PANEL_ROWS, COL_WIDTH), F32),
        grid_spec=pltpu.PrefetchScalarGridSpec(
            num_scalar_prefetch=2,
            grid=(RT,),
            in_specs=[
                pl.BlockSpec((TILE, COL_WIDTH), lambda i, *_: (i, 0)),
                pl.BlockSpec((TILE, LEAD), lambda i, *_: (i, 0)),
                pl.BlockSpec((LEAD, COL_WIDTH), lambda i, *_: (0, 0)),
                pl.BlockSpec((ROWS, 1, TILE, TILE), lambda i, *_: (0, i // PCT, 0, 0)),
            ],
            out_specs=pl.BlockSpec((TILE, COL_WIDTH), lambda i, *_: (i, 0)),
        ),
        cost_estimate=pl.CostEstimate(
            flops=6 * PANEL_ROWS * COL_WIDTH * LEAD,
            bytes_accessed=26 * 2**20,
            transcendentals=0,
        ),
        name="schur",
    )(row_places, col_places, front, panel, top, tiles)


def per_device(parent_front, child_panels, child_inverses, parent_index):
    here_row = lax.axis_index("row")
    here_col = lax.axis_index("col")
    own_factor = product_rows(child_panels[0], child_inverses[0])
    factors, panel, top = gather_all(own_factor, parent_front)

    block_of = parent_index // PCT
    my_blocks = lax.dynamic_index_in_dim(block_of, here_row, 0, keepdims=False)
    ids = jnp.arange(COLS, dtype=jnp.int32)
    wanted = jnp.concatenate([ids, here_col[None].astype(jnp.int32)])
    order = jnp.sum(jnp.where(my_blocks[None, :] == wanted[:, None], ids[None, :], 0), axis=1)
    outgoing = update_tiles(order, factors).reshape(ROWS, 2, TILE, TILE)
    tiles = lax.all_to_all(outgoing, "row", split_axis=0, concat_axis=0, tiled=True)

    row_blocks = 2 * here_row + jnp.arange(2, dtype=jnp.int32)
    row_places = (
        jnp.sum(
            jnp.where(
                block_of[:, None, :] == row_blocks[None, :, None], parent_index[:, None, :], 0
            ),
            axis=2,
        )
        - here_row * RT
    )
    col_places = (
        jnp.sum(jnp.where(block_of == here_col, parent_index, 0), axis=1) - here_col * PCT
    )

    panel_out, top_out = factor_panel(panel, top)
    schur = schur_update(
        row_places.astype(jnp.int32),
        col_places.astype(jnp.int32),
        parent_front,
        panel_out,
        top_out,
        tiles,
    )
    return (panel_out, schur)


def solution(mesh):
    placed = (P("row", "col"), P("row", "col", None), P("row", None, None), P())
    return jax.shard_map(
        per_device,
        mesh=mesh,
        in_specs=placed,
        out_specs=(P("row", None), P("row", "col")),
        check_vma=False,
    )
```

```python
import jax
import jax.numpy as jnp
from jax import lax
from jax.experimental import pallas as pl
from jax.experimental.pallas import tpu as pltpu
from jax.sharding import PartitionSpec as P

TILE = 256
CW = 512
PCT = 4
NSP = 2
ROWS = 8
COLS = 16
SIDE = 4
RT = 8
LEAD = NSP * TILE
PANEL_ROWS = RT * TILE
COL_WIDTH = PCT * TILE
SLICE = LEAD // COLS
TOP_PIECES = 8
TOP_OVERLAP = 8
MESH = pl.DeviceIdType.MESH
F32 = jnp.float32
BF16 = jnp.bfloat16


def product(matrix_a, matrix_b):
    return jnp.dot(
        matrix_a, matrix_b, precision=lax.Precision.HIGHEST, preferred_element_type=F32
    )


def product_rows(matrix_a, matrix_b):
    return lax.dot_general(
        matrix_a,
        matrix_b,
        (((1,), (1,)), ((), ())),
        precision=lax.Precision.HIGHEST,
        preferred_element_type=F32,
    )


def halves(value):
    high = value.astype(BF16)
    low = (value - high.astype(F32)).astype(BF16)
    return high, low


def three_pass(pair_a, pair_b, contract):
    def one(left, right):
        return lax.dot_general(left, right, (contract, ((), ())), preferred_element_type=F32)

    return one(pair_a[0], pair_b[0]) + (one(pair_a[0], pair_b[1]) + one(pair_a[1], pair_b[0]))


def wrap(value):
    return lax.rem(value + 2 * SIDE, SIDE)


def gather_kernel(own_ref, front_ref, all_ref, pan_ref, top_ref, send_sem, recv_sem, local_sem):
    row = lax.axis_index("row")
    col = lax.axis_index("col")
    place_y = col // SIDE
    place_z = lax.rem(col, SIDE)
    chip = row // 2
    core = lax.rem(row, 2)
    counter = [0]

    def fresh(count=1):
        counter[0] += count
        return counter[0] - count

    def at(step_y, step_z):
        return wrap(place_y + step_y) * SIDE + wrap(place_z + step_z)

    def remote(src, dst, send, recv, to_row, to_col):
        return pltpu.make_async_remote_copy(
            src_ref=src,
            dst_ref=dst,
            send_sem=send_sem.at[send],
            recv_sem=recv_sem.at[recv],
            device_id=(to_row, to_col),
            device_id_type=MESH,
        )

    load_top = pltpu.make_async_copy(front_ref.at[pl.ds(0, LEAD)], top_ref, local_sem.at[0])

    @pl.when(row == 0)
    def _():
        load_top.start()

    keep_own = pltpu.make_async_copy(own_ref, all_ref.at[col], local_sem.at[1])
    keep_own.start()

    barrier = pltpu.get_barrier_semaphore()
    greeted = [(row, lax.rem(col + k, COLS)) for k in range(1, COLS)]
    greeted += [
        (row + 1 - 2 * core, col),
        (lax.rem(row + 2, ROWS), col),
        (lax.rem(row + 6, ROWS), col),
    ]
    for who in greeted:
        pl.semaphore_signal(barrier, inc=1, device_id=who, device_id_type=MESH)
    pl.semaphore_wait(barrier, len(greeted))

    started = []

    def ring(half, piece, own):
        if half == 0:
            place = lambda i, j: at(j, i)
        else:
            place = lambda i, j: at(i, j)
        sem = {}

        def key(name):
            if name not in sem:
                sem[name] = fresh()
            return sem[name]

        pending = {}

        def go(name, i, j, part, to_i, to_j):
            source = own if (i, j) == (0, 0) else piece(place(i, j), half, part)
            copy = remote(
                source,
                piece(place(i, j), half, part),
                key(name),
                key(name),
                row,
                place(to_i, to_j),
            )
            copy.start()
            pending[name] = copy
            started.append((copy, None))

        def arrived(name):
            pending[name].wait_recv()

        def quarter(d):
            return 1 if d == 1 else 2

        def first():
            for d in (1, -1):
                go(("a", d), 0, 0, 0, d, 0)

        def second():
            for e in (1, -1):
                go(("b", 0, e), 0, 0, 0, 0, e)

        def near(d):
            arrived(("a", d))
            go(("af", d), -d, 0, quarter(d), d, 0)
            for e in (1, -1):
                go(("b", -d, e), -d, 0, 0, 0, e)

        def far():
            arrived(("af", 1))
            arrived(("af", -1))
            for e in (1, -1):
                go(("b", 2, e), 2, 0, 0, 0, e)

        def cross(i):
            for e in (1, -1):
                arrived(("b", i, e))
                go(("bf", i, e), i, -e, quarter(e), 0, e)

        def last(i):
            for e in (1, -1):
                arrived(("bf", i, e))

        return first, second, near, far, cross, last

    def ring_steps(rings):
        def each(index, *args):
            return [lambda r=r: r[index](*args) for r in rings]

        steps = each(0) + each(1) + each(2, 1) + each(2, -1) + each(4, 0) + each(3)
        for i in (1, -1, 2):
            steps += each(4, i)
        for i in (0, 1, -1, 2):
            steps += each(5, i)
        return steps

    def factor_piece(slot, half, part):
        if part == 0:
            return all_ref.at[slot, pl.ds(half * 128, 128)]
        return all_ref.at[slot, pl.ds(half * 128 + 64 * (part - 1), 64)]

    def panel_piece(slot, half, part):
        if part == 0:
            return pan_ref.at[half, pl.ds(slot * SLICE, SLICE)]
        size = SLICE // 2
        return pan_ref.at[half, pl.ds(slot * SLICE + size * (part - 1), size)]

    factor_rings = [ring(h, factor_piece, own_ref.at[pl.ds(h * 128, 128)]) for h in range(2)]
    panel_rings = [ring(h, panel_piece, panel_piece(col, h, 0)) for h in range(2)]

    top_size = LEAD // TOP_PIECES
    half_pieces = TOP_PIECES // 2
    top_recv = fresh(TOP_PIECES)
    top_next = fresh(TOP_PIECES)
    top_side = fresh(TOP_PIECES)

    def top_copies(piece, way):
        block = top_ref.at[pl.ds(piece * top_size, top_size)]
        onward = lax.rem(row + (2 if way == 1 else 6), ROWS)
        return (
            remote(block, block, top_next + piece, top_recv + piece, onward, col),
            remote(block, block, top_side + piece, top_recv + piece, row + 1 - 2 * core, col),
        )

    def top_step(number):
        for way in (1, -1):
            depth = chip if way == 1 else lax.rem(SIDE - chip, SIDE)
            count = number - depth - core
            piece = 2 * count + (0 if way == 1 else 1)

            @pl.when((count >= 0) & (count < half_pieces))
            def _(piece=piece, way=way, depth=depth):
                onward, side = top_copies(piece, way)

                @pl.when(row != 0)
                def _():
                    side.wait_recv()

                @pl.when((core == 0) & (depth < SIDE - 1))
                def _():
                    onward.start()

                @pl.when(core == 0)
                def _():
                    side.start()

    def top_drain(number):
        for way in (1, -1):
            depth = chip if way == 1 else lax.rem(SIDE - chip, SIDE)
            onward, side = top_copies(2 * number + (0 if way == 1 else 1), way)

            @pl.when((core == 0) & (depth < SIDE - 1))
            def _():
                onward.wait_send()

            @pl.when(core == 0)
            def _():
                side.wait_send()

    spread = []
    for half in range(2):
        spread.append((half, 2 * row + half, pl.ds(0, COL_WIDTH), pl.ds(0, COL_WIDTH)))
        spread.append((half, 0, pl.ds(half * TILE, TILE), pl.ds(COL_WIDTH, TILE)))
    spread_recv = [fresh() for _ in spread]
    spread_send = [fresh(COLS) for _ in spread]

    def spread_copy(index, step):
        half, _, lanes, to_lanes = spread[index]
        to_col = lax.rem(col + step, COLS)
        rows = pl.ds(to_col * SLICE, SLICE)
        return remote(
            top_ref.at[rows, lanes],
            pan_ref.at[half, rows, to_lanes],
            spread_send[index] + step,
            spread_recv[index],
            row,
            to_col,
        )

    def spread_start(index):
        half, holder, lanes, to_lanes = spread[index]
        rows = pl.ds(col * SLICE, SLICE)

        @pl.when(col == holder)
        def _():
            keep = pltpu.make_async_copy(
                top_ref.at[rows, lanes], pan_ref.at[half, rows, to_lanes], local_sem.at[2 + index]
            )
            keep.start()

            @pl.loop(1, COLS)
            def _(step):
                spread_copy(index, step).start()

            keep.wait()

    def spread_wait(index):
        @pl.when(col != spread[index][1])
        def _():
            spread_copy(index, 1).wait_recv()

    def spread_drain(index):
        @pl.when(col == spread[index][1])
        def _():
            @pl.loop(1, COLS)
            def _(step):
                spread_copy(index, step).wait_send()

    factor_steps = ring_steps(factor_rings)
    panel_steps = ring_steps(panel_rings)
    for run in factor_steps[:4]:
        run()

    @pl.when(row == 0)
    def _():
        load_top.wait()

    top_steps = half_pieces + SIDE
    for number in range(top_steps):
        top_step(number)
        if 4 + number < TOP_OVERLAP:
            factor_steps[4 + number]()
    for number in (1, 3, 0, 2):
        spread_start(number)
    for run in factor_steps[TOP_OVERLAP:]:
        run()
    for number in range(len(spread)):
        spread_wait(number)
    for run in panel_steps:
        run()
    keep_own.wait()
    for copy, _ in started:
        copy.wait_send()
    for number in range(half_pieces):
        top_drain(number)
    for number in range(len(spread)):
        spread_drain(number)


def gather_all(own_factor, front):
    anywhere = pl.BlockSpec(memory_space=pl.ANY)
    vmem = pl.BlockSpec(memory_space=pltpu.VMEM)
    return pl.pallas_call(
        gather_kernel,
        out_shape=(
            jax.ShapeDtypeStruct((COLS, TILE, CW), F32),
            jax.ShapeDtypeStruct((2, LEAD, COL_WIDTH + TILE), F32),
            jax.ShapeDtypeStruct((LEAD, COL_WIDTH), F32),
        ),
        in_specs=[vmem, anywhere],
        out_specs=(vmem, vmem, vmem),
        scratch_shapes=[
            pltpu.SemaphoreType.DMA((192,)),
            pltpu.SemaphoreType.DMA((192,)),
            pltpu.SemaphoreType.DMA((6,)),
        ],
        compiler_params=pltpu.CompilerParams(
            collective_id=0, has_side_effects=True, vmem_limit_bytes=40 * 2**20
        ),
        name="gather",
    )(own_factor, front)


BLOCK = 128
GROUP = 8
GROUPS = BLOCK // GROUP


def eliminate(block_ref, upper_ref, inverse_ref):
    shape = (GROUP, BLOCK)
    lanes = lax.broadcasted_iota(jnp.int32, shape, 1)
    sublanes = lax.broadcasted_iota(jnp.int32, shape, 0)
    left = [block_ref[GROUP * g : GROUP * (g + 1), :] for g in range(GROUPS)]
    right = [jnp.where(lanes == sublanes + GROUP * g, 1.0, 0.0) for g in range(GROUPS)]
    for g in range(GROUPS):
        base = GROUP * g
        row_l = [jnp.broadcast_to(left[g][s : s + 1, :], shape) for s in range(GROUP)]
        row_r = [jnp.broadcast_to(right[g][s : s + 1, :], shape) for s in range(GROUP)]
        entry = {}
        for s in range(GROUP):
            for t in range(s, GROUP):
                entry[s, t] = jnp.broadcast_to(row_l[s][:, base + t : base + t + 1], shape)
        recip = []
        ratio = {}
        for s in range(GROUP):
            recip.append(1.0 / entry[s, s])
            for t in range(s + 1, GROUP):
                ratio[t, s] = entry[s, t] * recip[s]
            for t in range(s + 1, GROUP):
                for u in range(t, GROUP):
                    entry[t, u] = entry[t, u] - ratio[t, s] * entry[s, u]
        for s in range(GROUP):
            for t in range(s):
                row_l[s] = row_l[s] - ratio[s, t] * row_l[t]
                row_r[s] = row_r[s] - ratio[s, t] * row_r[t]
        new_l, new_r, scale = row_l[0], row_r[0], recip[0]
        for s in range(1, GROUP):
            pick = sublanes == s
            new_l = jnp.where(pick, row_l[s], new_l)
            new_r = jnp.where(pick, row_r[s], new_r)
            scale = jnp.where(pick, recip[s], scale)
        for i in range(g + 1, GROUPS):
            plain = []
            for s in range(GROUP):
                value = jnp.broadcast_to(left[i][:, base + s : base + s + 1], shape)
                for t in range(s):
                    value = value - plain[t] * ratio[s, t]
                plain.append(value)
            for s in range(GROUP):
                scaled = plain[s] * recip[s]
                left[i] = left[i] - scaled * row_l[s]
                right[i] = right[i] - scaled * row_r[s]
        scale = jnp.sqrt(scale)
        upper = jnp.where(lanes >= sublanes + base, new_l * scale, 0.0)
        upper_ref[base : base + GROUP, :] = upper
        inverse_ref[base : base + GROUP, :] = new_r * scale


def panel_kernel(
    pan_ref, top_ref, panel_ref, cols_ref, block_ref, upper_ref, inv_ref, side_ref, low_ref,
    work_ref, full_ref,
):
    row = lax.axis_index("row")
    col = lax.axis_index("col")
    lead = [pan_ref.at[h, :, pl.ds(COL_WIDTH, TILE)] for h in range(2)]
    near = slice(0, BLOCK)
    away = slice(BLOCK, TILE)

    def join_inverse(tile):
        first, second, side = inv_ref[2 * tile], inv_ref[2 * tile + 1], side_ref[tile]
        full_ref[tile, near, near] = first
        full_ref[tile, near, away] = jnp.zeros((BLOCK, BLOCK), F32)
        full_ref[tile, away, near] = -product(second, product(side, first))
        full_ref[tile, away, away] = second

    def second_half(tile, below, corner):
        side = product_rows(below, inv_ref[2 * tile])
        side_ref[tile] = side
        block_ref[...] = corner - product_rows(side, side)

    def body(number, carry):
        @pl.when(number == 0)
        def _():
            block_ref[...] = lead[0][near, near]

        @pl.when(number == 1)
        def _():
            second_half(0, lead[0][away, near], lead[0][away, away])

        @pl.when(number == 2)
        def _():
            join_inverse(0)
            low = product_rows(lead[0][TILE:, :], full_ref[0])
            low_ref[...] = low
            work_ref[...] = lead[1][TILE:, :] - product_rows(low, low)
            block_ref[...] = work_ref[near, near]

        @pl.when(number == 3)
        def _():
            second_half(1, work_ref[away, near], work_ref[away, away])

        eliminate(block_ref, upper_ref.at[number], inv_ref.at[number])
        return carry

    lax.fori_loop(0, 4, body, 0)
    join_inverse(1)

    inverses = [halves(full_ref[t]) for t in range(2)]
    low = halves(low_ref[...])

    def chunk(source, lanes):
        first = three_pass(inverses[0], halves(source[:TILE, lanes]), ((1,), (0,)))
        rest = source[TILE:, lanes] - three_pass(low, halves(first), ((1,), (0,)))
        return first, three_pass(inverses[1], halves(rest), ((1,), (0,)))

    @pl.loop(0, PCT)
    def _(part):
        lanes = pl.ds(pl.multiple_of(part * TILE, TILE), TILE)
        first, second = chunk(top_ref, lanes)
        cols_ref[:TILE, lanes] = first
        cols_ref[TILE:, lanes] = second

    @pl.loop(0, RT)
    def _(part):
        lanes = pl.ds(pl.multiple_of(lax.rem(part, PCT) * TILE, TILE), TILE)
        rows = pl.ds(pl.multiple_of(part * TILE, TILE), TILE)
        first, second = chunk(pan_ref.at[part // PCT], lanes)
        panel_ref[rows, :TILE] = first.T
        panel_ref[rows, TILE:] = second.T

    blank = jnp.zeros((BLOCK, BLOCK), F32)

    @pl.when(col == 0)
    def _():
        for t in range(2):
            for r, c, value in (
                (0, 0, upper_ref[2 * t]),
                (0, 1, side_ref[t].T),
                (1, 0, blank),
                (1, 1, upper_ref[2 * t + 1]),
            ):
                r0, c0 = t * TILE + r * BLOCK, t * TILE + c * BLOCK
                cols_ref[r0 : r0 + BLOCK, c0 : c0 + BLOCK] = value
        cols_ref[TILE:, :TILE] = jnp.zeros((TILE, TILE), F32)

    @pl.when(row == 0)
    def _():
        for t in range(2):
            for r, c, value in (
                (0, 0, upper_ref[2 * t].T),
                (0, 1, blank),
                (1, 0, side_ref[t]),
                (1, 1, upper_ref[2 * t + 1].T),
            ):
                r0, c0 = t * TILE + r * BLOCK, t * TILE + c * BLOCK
                panel_ref[r0 : r0 + BLOCK, c0 : c0 + BLOCK] = value
        panel_ref[:TILE, TILE:] = jnp.zeros((TILE, TILE), F32)


def factor_panel(pan, top):
    vmem = pl.BlockSpec(memory_space=pltpu.VMEM)
    return pl.pallas_call(
        panel_kernel,
        out_shape=(
            jax.ShapeDtypeStruct((PANEL_ROWS, LEAD), F32),
            jax.ShapeDtypeStruct((LEAD, COL_WIDTH), F32),
        ),
        in_specs=[vmem, vmem],
        out_specs=(vmem, vmem),
        scratch_shapes=[
            pltpu.VMEM((BLOCK, BLOCK), F32),
            pltpu.VMEM((4, BLOCK, BLOCK), F32),
            pltpu.VMEM((4, BLOCK, BLOCK), F32),
            pltpu.VMEM((2, BLOCK, BLOCK), F32),
            pltpu.VMEM((TILE, TILE), F32),
            pltpu.VMEM((TILE, TILE), F32),
            pltpu.VMEM((2, TILE, TILE), F32),
        ],
        compiler_params=pltpu.CompilerParams(vmem_limit_bytes=40 * 2**20),
        cost_estimate=pl.CostEstimate(
            flops=60 * 10**9, bytes_accessed=14 * 2**20, transcendentals=0
        ),
        name="panel",
    )(pan, top)


PAIRS = COLS // 2


def tiles_kernel(order_ref, first_ref, second_ref, right_ref, out_ref, high_ref, low_ref):
    @pl.when(pl.program_id(0) == 0)
    def _():
        high_ref[...], low_ref[...] = halves(right_ref[0])

    right = (high_ref[...], low_ref[...])
    out_ref[0] = three_pass(halves(first_ref[0]), right, ((1,), (1,)))
    out_ref[1] = three_pass(halves(second_ref[0]), right, ((1,), (1,)))


def update_tiles(order, factors):
    return pl.pallas_call(
        tiles_kernel,
        out_shape=jax.ShapeDtypeStruct((COLS, TILE, TILE), F32),
        grid_spec=pltpu.PrefetchScalarGridSpec(
            num_scalar_prefetch=1,
            grid=(PAIRS,),
            in_specs=[
                pl.BlockSpec((1, TILE, CW), lambda i, order: (order[2 * i], 0, 0)),
                pl.BlockSpec((1, TILE, CW), lambda i, order: (order[2 * i + 1], 0, 0)),
                pl.BlockSpec((1, TILE, CW), lambda i, order: (order[COLS], 0, 0)),
            ],
            out_specs=pl.BlockSpec((2, TILE, TILE), lambda i, order: (i, 0, 0)),
            scratch_shapes=[pltpu.VMEM((TILE, CW), BF16), pltpu.VMEM((TILE, CW), BF16)],
        ),
        cost_estimate=pl.CostEstimate(
            flops=6 * COLS * TILE * TILE * CW, bytes_accessed=12 * 2**20, transcendentals=0
        ),
        name="tiles",
    )(order, factors, factors, factors)


def schur_kernel(
    rows_ref, cols_ref, front_ref, panel_ref, top_ref, tiles_ref, out_ref, high_ref, low_ref
):
    step = pl.program_id(0)

    @pl.when(step == 0)
    def _():
        high_ref[...], low_ref[...] = halves(top_ref[...])

    left = halves(panel_ref[...])
    for part in range(PCT):
        lanes = slice(part * TILE, (part + 1) * TILE)
        right = (high_ref[:, lanes], low_ref[:, lanes])
        out_ref[:, lanes] = front_ref[:, lanes] - three_pass(left, right, ((1,), (0,)))
    block = step // PCT
    for child in range(ROWS):

        @pl.when(rows_ref[child, block] == step)
        def _(child=child):
            start = pl.multiple_of(cols_ref[child] * TILE, TILE)
            out_ref[:, pl.ds(start, TILE)] -= tiles_ref[child, 0]


def schur_update(row_places, col_places, front, panel, top, tiles):
    return pl.pallas_call(
        schur_kernel,
        out_shape=jax.ShapeDtypeStruct((PANEL_ROWS, COL_WIDTH), F32),
        grid_spec=pltpu.PrefetchScalarGridSpec(
            num_scalar_prefetch=2,
            grid=(RT,),
            in_specs=[
                pl.BlockSpec((TILE, COL_WIDTH), lambda i, *_: (i, 0)),
                pl.BlockSpec((TILE, LEAD), lambda i, *_: (i, 0)),
                pl.BlockSpec((LEAD, COL_WIDTH), lambda i, *_: (0, 0)),
                pl.BlockSpec((ROWS, 1, TILE, TILE), lambda i, *_: (0, i // PCT, 0, 0)),
            ],
            out_specs=pl.BlockSpec((TILE, COL_WIDTH), lambda i, *_: (i, 0)),
            scratch_shapes=[
                pltpu.VMEM((LEAD, COL_WIDTH), BF16),
                pltpu.VMEM((LEAD, COL_WIDTH), BF16),
            ],
        ),
        cost_estimate=pl.CostEstimate(
            flops=6 * PANEL_ROWS * COL_WIDTH * LEAD,
            bytes_accessed=26 * 2**20,
            transcendentals=0,
        ),
        name="schur",
    )(row_places, col_places, front, panel, top, tiles)


def per_device(parent_front, child_panels, child_inverses, parent_index):
    here_row = lax.axis_index("row")
    here_col = lax.axis_index("col")
    own_factor = product_rows(child_panels[0], child_inverses[0])
    factors, panel, top = gather_all(own_factor, parent_front)

    block_of = parent_index // PCT
    my_blocks = lax.dynamic_index_in_dim(block_of, here_row, 0, keepdims=False)
    ids = jnp.arange(COLS, dtype=jnp.int32)
    wanted = jnp.concatenate([ids, here_col[None].astype(jnp.int32)])
    order = jnp.sum(jnp.where(my_blocks[None, :] == wanted[:, None], ids[None, :], 0), axis=1)
    outgoing = update_tiles(order, factors).reshape(ROWS, 2, TILE, TILE)
    tiles = lax.all_to_all(outgoing, "row", split_axis=0, concat_axis=0, tiled=True)

    row_blocks = 2 * here_row + jnp.arange(2, dtype=jnp.int32)
    row_places = (
        jnp.sum(
            jnp.where(
                block_of[:, None, :] == row_blocks[None, :, None], parent_index[:, None, :], 0
            ),
            axis=2,
        )
        - here_row * RT
    )
    col_places = (
        jnp.sum(jnp.where(block_of == here_col, parent_index, 0), axis=1) - here_col * PCT
    )

    panel_out, top_out = factor_panel(panel, top)
    schur = schur_update(
        row_places.astype(jnp.int32),
        col_places.astype(jnp.int32),
        parent_front,
        panel_out,
        top_out,
        tiles,
    )
    return (panel_out, schur)


def solution(mesh):
    placed = (P("row", "col"), P("row", "col", None), P("row", None, None), P())
    return jax.shard_map(
        per_device,
        mesh=mesh,
        in_specs=placed,
        out_specs=(P("row", None), P("row", "col")),
        check_vma=False,
    )
```

```python
import jax
import jax.numpy as jnp
from jax import lax
from jax.experimental import pallas as pl
from jax.experimental.pallas import tpu as pltpu
from jax.sharding import PartitionSpec as P

TILE = 256
CW = 512
PCT = 4
NSP = 2
ROWS = 8
COLS = 16
SIDE = 4
RT = 8
LEAD = NSP * TILE
PANEL_ROWS = RT * TILE
COL_WIDTH = PCT * TILE
SLICE = LEAD // COLS
TOP_PIECES = 8
MESH = pl.DeviceIdType.MESH
F32 = jnp.float32
BF16 = jnp.bfloat16


def product(matrix_a, matrix_b):
    return jnp.dot(
        matrix_a, matrix_b, precision=lax.Precision.HIGHEST, preferred_element_type=F32
    )


def product_rows(matrix_a, matrix_b):
    return lax.dot_general(
        matrix_a,
        matrix_b,
        (((1,), (1,)), ((), ())),
        precision=lax.Precision.HIGHEST,
        preferred_element_type=F32,
    )


def halves(value):
    high = value.astype(BF16)
    low = (value - high.astype(F32)).astype(BF16)
    return high, low


def three_pass(pair_a, pair_b, contract):
    def one(left, right):
        return lax.dot_general(left, right, (contract, ((), ())), preferred_element_type=F32)

    return one(pair_a[0], pair_b[0]) + (one(pair_a[0], pair_b[1]) + one(pair_a[1], pair_b[0]))


def wrap(value):
    return lax.rem(value + 2 * SIDE, SIDE)


class Wires:
    def __init__(self, send_sem, recv_sem):
        self.row = lax.axis_index("row")
        self.col = lax.axis_index("col")
        self.place_y = self.col // SIDE
        self.place_z = lax.rem(self.col, SIDE)
        self.chip = self.row // 2
        self.core = lax.rem(self.row, 2)
        self.send_sem = send_sem
        self.recv_sem = recv_sem
        self.used = 0
        self.started = []

    def fresh(self, count=1):
        self.used += count
        return self.used - count

    def at(self, step_y, step_z):
        return wrap(self.place_y + step_y) * SIDE + wrap(self.place_z + step_z)

    def remote(self, src, dst, send, recv, to_row, to_col):
        return pltpu.make_async_remote_copy(
            src_ref=src,
            dst_ref=dst,
            send_sem=self.send_sem.at[send],
            recv_sem=self.recv_sem.at[recv],
            device_id=(to_row, to_col),
            device_id_type=MESH,
        )

    def greet(self, devices):
        barrier = pltpu.get_barrier_semaphore()
        for who in devices:
            pl.semaphore_signal(barrier, inc=1, device_id=who, device_id_type=MESH)
        pl.semaphore_wait(barrier, len(devices))

    def col_others(self):
        return [(self.row, lax.rem(self.col + k, COLS)) for k in range(1, COLS)]

    def ring(self, half, piece, own):
        if half == 0:
            place = lambda i, j: self.at(j, i)
        else:
            place = lambda i, j: self.at(i, j)
        sem = {}

        def key(name):
            if name not in sem:
                sem[name] = self.fresh()
            return sem[name]

        pending = {}

        def go(name, i, j, part, to_i, to_j):
            source = own if (i, j) == (0, 0) else piece(place(i, j), half, part)
            target = piece(place(i, j), half, part)
            number = key(name)
            copy = self.remote(source, target, number, number, self.row, place(to_i, to_j))
            copy.start()
            pending[name] = copy
            self.started.append(copy)

        def arrived(name):
            pending[name].wait_recv()

        def quarter(d):
            return 1 if d == 1 else 2

        def first():
            for d in (1, -1):
                go(("a", d), 0, 0, 0, d, 0)

        def second():
            for e in (1, -1):
                go(("b", 0, e), 0, 0, 0, 0, e)

        def near(d):
            arrived(("a", d))
            go(("af", d), -d, 0, quarter(d), d, 0)
            for e in (1, -1):
                go(("b", -d, e), -d, 0, 0, 0, e)

        def far():
            arrived(("af", 1))
            arrived(("af", -1))
            for e in (1, -1):
                go(("b", 2, e), 2, 0, 0, 0, e)

        def cross(i):
            for e in (1, -1):
                arrived(("b", i, e))
                go(("bf", i, e), i, -e, quarter(e), 0, e)

        def last(i):
            for e in (1, -1):
                arrived(("bf", i, e))

        return first, second, near, far, cross, last

    def drain(self):
        for copy in self.started:
            copy.wait_send()


def ring_steps(rings):
    def each(index, *args):
        return [lambda r=r: r[index](*args) for r in rings]

    steps = each(0) + each(1) + each(2, 1) + each(2, -1) + each(4, 0) + each(3)
    for i in (1, -1, 2):
        steps += each(4, i)
    for i in (0, 1, -1, 2):
        steps += each(5, i)
    return steps


def gather_kernel(own_ref, front_ref, all_ref, top_ref, send_sem, recv_sem, local_sem):
    wires = Wires(send_sem, recv_sem)
    row, col, chip, core = wires.row, wires.col, wires.chip, wires.core
    fresh, remote = wires.fresh, wires.remote
    load_top = pltpu.make_async_copy(front_ref.at[pl.ds(0, LEAD)], top_ref, local_sem.at[0])

    @pl.when(row == 0)
    def _():
        load_top.start()

    keep_own = pltpu.make_async_copy(own_ref, all_ref.at[col], local_sem.at[1])
    keep_own.start()
    wires.greet(
        [(row, wires.at(*step)) for step in ((1, 0), (-1, 0), (0, 1), (0, -1))]
        + [
            (row + 1 - 2 * core, col),
            (lax.rem(row + 2, ROWS), col),
            (lax.rem(row + 6, ROWS), col),
        ]
    )

    def factor_piece(slot, half, part):
        if part == 0:
            return all_ref.at[slot, pl.ds(half * 128, 128)]
        return all_ref.at[slot, pl.ds(half * 128 + 64 * (part - 1), 64)]

    top_size = LEAD // TOP_PIECES
    half_pieces = TOP_PIECES // 2
    top_recv = fresh(TOP_PIECES)
    top_next = fresh(TOP_PIECES)
    top_side = fresh(TOP_PIECES)

    def top_copies(piece, way):
        block = top_ref.at[pl.ds(piece * top_size, top_size)]
        onward = lax.rem(row + (2 if way == 1 else 6), ROWS)
        return (
            remote(block, block, top_next + piece, top_recv + piece, onward, col),
            remote(block, block, top_side + piece, top_recv + piece, row + 1 - 2 * core, col),
        )

    def top_step(number):
        for way in (1, -1):
            depth = chip if way == 1 else lax.rem(SIDE - chip, SIDE)
            count = number - depth - core
            piece = 2 * count + (0 if way == 1 else 1)

            @pl.when((count >= 0) & (count < half_pieces))
            def _(piece=piece, way=way, depth=depth):
                onward, side = top_copies(piece, way)

                @pl.when(row != 0)
                def _():
                    side.wait_recv()

                @pl.when((core == 0) & (depth < SIDE - 1))
                def _():
                    onward.start()

                @pl.when(core == 0)
                def _():
                    side.start()

    def top_drain(number):
        for way in (1, -1):
            depth = chip if way == 1 else lax.rem(SIDE - chip, SIDE)
            onward, side = top_copies(2 * number + (0 if way == 1 else 1), way)

            @pl.when((core == 0) & (depth < SIDE - 1))
            def _():
                onward.wait_send()

            @pl.when(core == 0)
            def _():
                side.wait_send()

    rings = [wires.ring(h, factor_piece, own_ref.at[pl.ds(h * 128, 128)]) for h in range(2)]
    steps = ring_steps(rings)
    for run in steps[:4]:
        run()

    @pl.when(row == 0)
    def _():
        load_top.wait()

    for number in range(half_pieces + SIDE):
        top_step(number)
        for run in steps[4 + 2 * number : 6 + 2 * number]:
            run()
    for run in steps[4 + 2 * (half_pieces + SIDE) :]:
        run()
    keep_own.wait()
    wires.drain()
    for number in range(half_pieces):
        top_drain(number)


def spread_kernel(top_ref, pan_ref, send_sem, recv_sem, local_sem):
    wires = Wires(send_sem, recv_sem)
    row, col = wires.row, wires.col
    fresh, remote = wires.fresh, wires.remote
    wires.greet(wires.col_others())

    def panel_piece(slot, half, part):
        if part == 0:
            return pan_ref.at[half, pl.ds(slot * SLICE, SLICE)]
        size = SLICE // 2
        return pan_ref.at[half, pl.ds(slot * SLICE + size * (part - 1), size)]

    spread = []
    for half in range(2):
        spread.append((half, 2 * row + half, pl.ds(0, COL_WIDTH), pl.ds(0, COL_WIDTH)))
        spread.append((half, 0, pl.ds(half * TILE, TILE), pl.ds(COL_WIDTH, TILE)))
    spread_recv = [fresh() for _ in spread]
    spread_send = [fresh(COLS) for _ in spread]

    def spread_copy(index, step):
        half, _, lanes, to_lanes = spread[index]
        to_col = lax.rem(col + step, COLS)
        rows = pl.ds(to_col * SLICE, SLICE)
        return remote(
            top_ref.at[rows, lanes],
            pan_ref.at[half, rows, to_lanes],
            spread_send[index] + step,
            spread_recv[index],
            row,
            to_col,
        )

    def spread_start(index):
        half, holder, lanes, to_lanes = spread[index]
        rows = pl.ds(col * SLICE, SLICE)

        @pl.when(col == holder)
        def _():
            keep = pltpu.make_async_copy(
                top_ref.at[rows, lanes], pan_ref.at[half, rows, to_lanes], local_sem.at[index]
            )
            keep.start()

            @pl.loop(1, COLS)
            def _(step):
                spread_copy(index, step).start()

            keep.wait()

    def spread_wait(index):
        @pl.when(col != spread[index][1])
        def _():
            spread_copy(index, 1).wait_recv()

    def spread_drain(index):
        @pl.when(col == spread[index][1])
        def _():
            @pl.loop(1, COLS)
            def _(step):
                spread_copy(index, step).wait_send()

    for number in (1, 3, 0, 2):
        spread_start(number)
    for number in range(len(spread)):
        spread_wait(number)
    for run in ring_steps([wires.ring(h, panel_piece, panel_piece(col, h, 0)) for h in range(2)]):
        run()
    wires.drain()
    for number in range(len(spread)):
        spread_drain(number)


def gather_all(own_factor, front):
    anywhere = pl.BlockSpec(memory_space=pl.ANY)
    vmem = pl.BlockSpec(memory_space=pltpu.VMEM)
    return pl.pallas_call(
        gather_kernel,
        out_shape=(
            jax.ShapeDtypeStruct((COLS, TILE, CW), F32),
            jax.ShapeDtypeStruct((LEAD, COL_WIDTH), F32),
        ),
        in_specs=[vmem, anywhere],
        out_specs=(vmem, vmem),
        scratch_shapes=[
            pltpu.SemaphoreType.DMA((104,)),
            pltpu.SemaphoreType.DMA((104,)),
            pltpu.SemaphoreType.DMA((2,)),
        ],
        compiler_params=pltpu.CompilerParams(
            collective_id=0, has_side_effects=True, vmem_limit_bytes=52 * 2**20
        ),
        name="gather",
    )(own_factor, front)


def spread_panel(top):
    vmem = pl.BlockSpec(memory_space=pltpu.VMEM)
    return pl.pallas_call(
        spread_kernel,
        out_shape=jax.ShapeDtypeStruct((2, LEAD, COL_WIDTH + TILE), F32),
        in_specs=[vmem],
        out_specs=vmem,
        scratch_shapes=[
            pltpu.SemaphoreType.DMA((112,)),
            pltpu.SemaphoreType.DMA((112,)),
            pltpu.SemaphoreType.DMA((4,)),
        ],
        compiler_params=pltpu.CompilerParams(
            collective_id=1, has_side_effects=True, vmem_limit_bytes=16 * 2**20
        ),
        cost_estimate=pl.CostEstimate(
            flops=30 * 10**9, bytes_accessed=20 * 2**20, transcendentals=0
        ),
        name="spread",
    )(top)


BLOCK = 128
GROUP = 8
GROUPS = BLOCK // GROUP


def eliminate(block_ref, upper_ref, inverse_ref):
    shape = (GROUP, BLOCK)
    lanes = lax.broadcasted_iota(jnp.int32, shape, 1)
    sublanes = lax.broadcasted_iota(jnp.int32, shape, 0)
    left = [block_ref[GROUP * g : GROUP * (g + 1), :] for g in range(GROUPS)]
    right = [jnp.where(lanes == sublanes + GROUP * g, 1.0, 0.0) for g in range(GROUPS)]
    for g in range(GROUPS):
        base = GROUP * g
        row_l = [jnp.broadcast_to(left[g][s : s + 1, :], shape) for s in range(GROUP)]
        row_r = [jnp.broadcast_to(right[g][s : s + 1, :], shape) for s in range(GROUP)]
        entry = {}
        for s in range(GROUP):
            for t in range(s, GROUP):
                entry[s, t] = jnp.broadcast_to(row_l[s][:, base + t : base + t + 1], shape)
        recip = []
        ratio = {}
        for s in range(GROUP):
            recip.append(1.0 / entry[s, s])
            for t in range(s + 1, GROUP):
                ratio[t, s] = entry[s, t] * recip[s]
            for t in range(s + 1, GROUP):
                for u in range(t, GROUP):
                    entry[t, u] = entry[t, u] - ratio[t, s] * entry[s, u]
        for s in range(GROUP):
            for t in range(s):
                row_l[s] = row_l[s] - ratio[s, t] * row_l[t]
                row_r[s] = row_r[s] - ratio[s, t] * row_r[t]
        new_l, new_r, scale = row_l[0], row_r[0], recip[0]
        for s in range(1, GROUP):
            pick = sublanes == s
            new_l = jnp.where(pick, row_l[s], new_l)
            new_r = jnp.where(pick, row_r[s], new_r)
            scale = jnp.where(pick, recip[s], scale)
        for i in range(g + 1, GROUPS):
            plain = []
            for s in range(GROUP):
                value = jnp.broadcast_to(left[i][:, base + s : base + s + 1], shape)
                for t in range(s):
                    value = value - plain[t] * ratio[s, t]
                plain.append(value)
            for s in range(GROUP):
                scaled = plain[s] * recip[s]
                left[i] = left[i] - scaled * row_l[s]
                right[i] = right[i] - scaled * row_r[s]
        scale = jnp.sqrt(scale)
        upper = jnp.where(lanes >= sublanes + base, new_l * scale, 0.0)
        upper_ref[base : base + GROUP, :] = upper
        inverse_ref[base : base + GROUP, :] = new_r * scale


def panel_kernel(
    pan_ref, top_ref, panel_ref, cols_ref, block_ref, upper_ref, inv_ref, side_ref, low_ref,
    work_ref, full_ref,
):
    row = lax.axis_index("row")
    col = lax.axis_index("col")
    lead = [pan_ref.at[h, :, pl.ds(COL_WIDTH, TILE)] for h in range(2)]
    near = slice(0, BLOCK)
    away = slice(BLOCK, TILE)

    def join_inverse(tile):
        first, second, side = inv_ref[2 * tile], inv_ref[2 * tile + 1], side_ref[tile]
        full_ref[tile, near, near] = first
        full_ref[tile, near, away] = jnp.zeros((BLOCK, BLOCK), F32)
        full_ref[tile, away, near] = -product(second, product(side, first))
        full_ref[tile, away, away] = second

    def second_half(tile, below, corner):
        side = product_rows(below, inv_ref[2 * tile])
        side_ref[tile] = side
        block_ref[...] = corner - product_rows(side, side)

    def body(number, carry):
        @pl.when(number == 0)
        def _():
            block_ref[...] = lead[0][near, near]

        @pl.when(number == 1)
        def _():
            second_half(0, lead[0][away, near], lead[0][away, away])

        @pl.when(number == 2)
        def _():
            join_inverse(0)
            low = product_rows(lead[0][TILE:, :], full_ref[0])
            low_ref[...] = low
            work_ref[...] = lead[1][TILE:, :] - product_rows(low, low)
            block_ref[...] = work_ref[near, near]

        @pl.when(number == 3)
        def _():
            second_half(1, work_ref[away, near], work_ref[away, away])

        eliminate(block_ref, upper_ref.at[number], inv_ref.at[number])
        return carry

    lax.fori_loop(0, 4, body, 0)
    join_inverse(1)

    inverses = [halves(full_ref[t]) for t in range(2)]
    low = halves(low_ref[...])

    def chunk(source, lanes):
        first = three_pass(inverses[0], halves(source[:TILE, lanes]), ((1,), (0,)))
        rest = source[TILE:, lanes] - three_pass(low, halves(first), ((1,), (0,)))
        return first, three_pass(inverses[1], halves(rest), ((1,), (0,)))

    @pl.loop(0, PCT)
    def _(part):
        lanes = pl.ds(pl.multiple_of(part * TILE, TILE), TILE)
        first, second = chunk(top_ref, lanes)
        cols_ref[:TILE, lanes] = first
        cols_ref[TILE:, lanes] = second

    @pl.loop(0, RT)
    def _(part):
        lanes = pl.ds(pl.multiple_of(lax.rem(part, PCT) * TILE, TILE), TILE)
        rows = pl.ds(pl.multiple_of(part * TILE, TILE), TILE)
        first, second = chunk(pan_ref.at[part // PCT], lanes)
        panel_ref[rows, :TILE] = first.T
        panel_ref[rows, TILE:] = second.T

    blank = jnp.zeros((BLOCK, BLOCK), F32)

    @pl.when(col == 0)
    def _():
        for t in range(2):
            for r, c, value in (
                (0, 0, upper_ref[2 * t]),
                (0, 1, side_ref[t].T),
                (1, 0, blank),
                (1, 1, upper_ref[2 * t + 1]),
            ):
                r0, c0 = t * TILE + r * BLOCK, t * TILE + c * BLOCK
                cols_ref[r0 : r0 + BLOCK, c0 : c0 + BLOCK] = value
        cols_ref[TILE:, :TILE] = jnp.zeros((TILE, TILE), F32)

    @pl.when(row == 0)
    def _():
        for t in range(2):
            for r, c, value in (
                (0, 0, upper_ref[2 * t].T),
                (0, 1, blank),
                (1, 0, side_ref[t]),
                (1, 1, upper_ref[2 * t + 1].T),
            ):
                r0, c0 = t * TILE + r * BLOCK, t * TILE + c * BLOCK
                panel_ref[r0 : r0 + BLOCK, c0 : c0 + BLOCK] = value
        panel_ref[:TILE, TILE:] = jnp.zeros((TILE, TILE), F32)


def factor_panel(pan, top):
    vmem = pl.BlockSpec(memory_space=pltpu.VMEM)
    return pl.pallas_call(
        panel_kernel,
        out_shape=(
            jax.ShapeDtypeStruct((PANEL_ROWS, LEAD), F32),
            jax.ShapeDtypeStruct((LEAD, COL_WIDTH), F32),
        ),
        in_specs=[vmem, vmem],
        out_specs=(vmem, vmem),
        scratch_shapes=[
            pltpu.VMEM((BLOCK, BLOCK), F32),
            pltpu.VMEM((4, BLOCK, BLOCK), F32),
            pltpu.VMEM((4, BLOCK, BLOCK), F32),
            pltpu.VMEM((2, BLOCK, BLOCK), F32),
            pltpu.VMEM((TILE, TILE), F32),
            pltpu.VMEM((TILE, TILE), F32),
            pltpu.VMEM((2, TILE, TILE), F32),
        ],
        compiler_params=pltpu.CompilerParams(vmem_limit_bytes=40 * 2**20),
        cost_estimate=pl.CostEstimate(
            flops=60 * 10**9, bytes_accessed=14 * 2**20, transcendentals=0
        ),
        name="panel",
    )(pan, top)


PAIRS = COLS // 2


def tiles_kernel(order_ref, all_ref, out_ref, high_ref, low_ref):
    step = pl.program_id(0)

    @pl.when(step == 0)
    def _():
        high_ref[...], low_ref[...] = halves(all_ref[order_ref[COLS]])

    right = (high_ref[...], low_ref[...])
    for part in range(2):
        left = halves(all_ref[order_ref[2 * step + part]])
        out_ref[part] = three_pass(left, right, ((1,), (1,)))


def update_tiles(order, factors):
    return pl.pallas_call(
        tiles_kernel,
        out_shape=jax.ShapeDtypeStruct((COLS, TILE, TILE), F32),
        grid_spec=pltpu.PrefetchScalarGridSpec(
            num_scalar_prefetch=1,
            grid=(PAIRS,),
            in_specs=[pl.BlockSpec(memory_space=pltpu.VMEM)],
            out_specs=pl.BlockSpec((2, TILE, TILE), lambda i, order: (i, 0, 0)),
            scratch_shapes=[pltpu.VMEM((TILE, CW), BF16), pltpu.VMEM((TILE, CW), BF16)],
        ),
        cost_estimate=pl.CostEstimate(
            flops=6 * COLS * TILE * TILE * CW, bytes_accessed=12 * 2**20, transcendentals=0
        ),
        name="tiles",
    )(order, factors)


def schur_kernel(
    rows_ref, cols_ref, front_ref, panel_ref, top_ref, tiles_ref, out_ref, high_ref, low_ref
):
    step = pl.program_id(0)

    @pl.when(step == 0)
    def _():
        high_ref[...], low_ref[...] = halves(top_ref[...])

    left = halves(panel_ref[...])
    for part in range(PCT):
        lanes = slice(part * TILE, (part + 1) * TILE)
        right = (high_ref[:, lanes], low_ref[:, lanes])
        out_ref[:, lanes] = front_ref[:, lanes] - three_pass(left, right, ((1,), (0,)))
    block = step // PCT
    for child in range(ROWS):

        @pl.when(rows_ref[child, block] == step)
        def _(child=child):
            start = pl.multiple_of(cols_ref[child] * TILE, TILE)
            out_ref[:, pl.ds(start, TILE)] -= tiles_ref[child, 0]


def schur_update(row_places, col_places, front, panel, top, tiles):
    return pl.pallas_call(
        schur_kernel,
        out_shape=jax.ShapeDtypeStruct((PANEL_ROWS, COL_WIDTH), F32),
        grid_spec=pltpu.PrefetchScalarGridSpec(
            num_scalar_prefetch=2,
            grid=(RT,),
            in_specs=[
                pl.BlockSpec((TILE, COL_WIDTH), lambda i, *_: (i, 0)),
                pl.BlockSpec((TILE, LEAD), lambda i, *_: (i, 0)),
                pl.BlockSpec(memory_space=pltpu.VMEM),
                pl.BlockSpec((ROWS, 1, TILE, TILE), lambda i, *_: (0, i // PCT, 0, 0)),
            ],
            out_specs=pl.BlockSpec((TILE, COL_WIDTH), lambda i, *_: (i, 0)),
            scratch_shapes=[
                pltpu.VMEM((LEAD, COL_WIDTH), BF16),
                pltpu.VMEM((LEAD, COL_WIDTH), BF16),
            ],
        ),
        cost_estimate=pl.CostEstimate(
            flops=6 * PANEL_ROWS * COL_WIDTH * LEAD,
            bytes_accessed=26 * 2**20,
            transcendentals=0,
        ),
        name="schur",
    )(row_places, col_places, front, panel, top, tiles)


def per_device(parent_front, child_panels, child_inverses, parent_index):
    here_row = lax.axis_index("row")
    here_col = lax.axis_index("col")
    own_factor = product_rows(child_panels[0], child_inverses[0])
    factors, top = gather_all(own_factor, parent_front)

    block_of = parent_index // PCT
    my_blocks = lax.dynamic_index_in_dim(block_of, here_row, 0, keepdims=False)
    ids = jnp.arange(COLS, dtype=jnp.int32)
    wanted = jnp.concatenate([ids, here_col[None].astype(jnp.int32)])
    order = jnp.sum(jnp.where(my_blocks[None, :] == wanted[:, None], ids[None, :], 0), axis=1)
    outgoing = update_tiles(order, factors).reshape(ROWS, 2, TILE, TILE)
    outgoing, top = lax.optimization_barrier((outgoing, top))
    tiles = lax.all_to_all(outgoing, "row", split_axis=0, concat_axis=0, tiled=True)

    row_blocks = 2 * here_row + jnp.arange(2, dtype=jnp.int32)
    row_places = (
        jnp.sum(
            jnp.where(
                block_of[:, None, :] == row_blocks[None, :, None], parent_index[:, None, :], 0
            ),
            axis=2,
        )
        - here_row * RT
    )
    col_places = (
        jnp.sum(jnp.where(block_of == here_col, parent_index, 0), axis=1) - here_col * PCT
    )

    panel_out, top_out = factor_panel(spread_panel(top), top)
    schur = schur_update(
        row_places.astype(jnp.int32),
        col_places.astype(jnp.int32),
        parent_front,
        panel_out,
        top_out,
        tiles,
    )
    return (panel_out, schur)


def solution(mesh):
    placed = (P("row", "col"), P("row", "col", None), P("row", None, None), P())
    return jax.shard_map(
        per_device,
        mesh=mesh,
        in_specs=placed,
        out_specs=(P("row", None), P("row", "col")),
        check_vma=False,
    )
```

```python
import jax
import jax.numpy as jnp
from jax import lax
from jax.experimental import pallas as pl
from jax.experimental.pallas import tpu as pltpu
from jax.sharding import PartitionSpec as P

TILE = 256
CW = 512
PCT = 4
NSP = 2
ROWS = 8
COLS = 16
SIDE = 4
RT = 8
LEAD = NSP * TILE
PANEL_ROWS = RT * TILE
COL_WIDTH = PCT * TILE
SLICE = LEAD // COLS
TOP_PIECES = 8
MESH = pl.DeviceIdType.MESH
F32 = jnp.float32
BF16 = jnp.bfloat16


def product(matrix_a, matrix_b):
    return jnp.dot(
        matrix_a, matrix_b, precision=lax.Precision.HIGHEST, preferred_element_type=F32
    )


def product_rows(matrix_a, matrix_b):
    return lax.dot_general(
        matrix_a,
        matrix_b,
        (((1,), (1,)), ((), ())),
        precision=lax.Precision.HIGHEST,
        preferred_element_type=F32,
    )


def halves(value):
    high = value.astype(BF16)
    low = (value - high.astype(F32)).astype(BF16)
    return high, low


def three_pass(pair_a, pair_b, contract):
    def one(left, right):
        return lax.dot_general(left, right, (contract, ((), ())), preferred_element_type=F32)

    return one(pair_a[0], pair_b[0]) + (one(pair_a[0], pair_b[1]) + one(pair_a[1], pair_b[0]))


def wrap(value):
    return lax.rem(value + 2 * SIDE, SIDE)


class Wires:
    def __init__(self, send_sem, recv_sem):
        self.row = lax.axis_index("row")
        self.col = lax.axis_index("col")
        self.place_y = self.col // SIDE
        self.place_z = lax.rem(self.col, SIDE)
        self.chip = self.row // 2
        self.core = lax.rem(self.row, 2)
        self.send_sem = send_sem
        self.recv_sem = recv_sem
        self.used = 0
        self.started = []

    def fresh(self, count=1):
        self.used += count
        return self.used - count

    def at(self, step_y, step_z):
        return wrap(self.place_y + step_y) * SIDE + wrap(self.place_z + step_z)

    def remote(self, src, dst, send, recv, to_row, to_col):
        return pltpu.make_async_remote_copy(
            src_ref=src,
            dst_ref=dst,
            send_sem=self.send_sem.at[send],
            recv_sem=self.recv_sem.at[recv],
            device_id=(to_row, to_col),
            device_id_type=MESH,
        )

    def greet(self, devices):
        barrier = pltpu.get_barrier_semaphore()
        for who in devices:
            pl.semaphore_signal(barrier, inc=1, device_id=who, device_id_type=MESH)
        pl.semaphore_wait(barrier, len(devices))

    def col_others(self):
        return [(self.row, lax.rem(self.col + k, COLS)) for k in range(1, COLS)]

    def ring(self, half, piece, own):
        if half == 0:
            place = lambda i, j: self.at(j, i)
        else:
            place = lambda i, j: self.at(i, j)
        sem = {}

        def key(name):
            if name not in sem:
                sem[name] = self.fresh()
            return sem[name]

        pending = {}

        def go(name, i, j, part, to_i, to_j):
            number = key(name)

            def build():
                mine = (i, j) == (0, 0)
                source = own() if mine else piece(place(i, j), half, part)
                target = piece(place(i, j), half, part)
                return self.remote(source, target, number, number, self.row, place(to_i, to_j))

            build().start()
            pending[name] = build
            self.started.append(build)

        def arrived(name):
            pending[name]().wait_recv()

        def quarter(d):
            return 1 if d == 1 else 2

        def first():
            for d in (1, -1):
                go(("a", d), 0, 0, 0, d, 0)

        def second():
            for e in (1, -1):
                go(("b", 0, e), 0, 0, 0, 0, e)

        def near(d):
            arrived(("a", d))
            go(("af", d), -d, 0, quarter(d), d, 0)
            for e in (1, -1):
                go(("b", -d, e), -d, 0, 0, 0, e)

        def far():
            arrived(("af", 1))
            arrived(("af", -1))
            for e in (1, -1):
                go(("b", 2, e), 2, 0, 0, 0, e)

        def cross(i):
            for e in (1, -1):
                arrived(("b", i, e))
                go(("bf", i, e), i, -e, quarter(e), 0, e)

        def last(i):
            for e in (1, -1):
                arrived(("bf", i, e))

        return first, second, near, far, cross, last

    def drain(self):
        for build in self.started:
            build().wait_send()


def ring_steps(rings):
    def each(index, *args):
        return [lambda r=r: r[index](*args) for r in rings]

    steps = each(0) + each(1) + each(2, 1) + each(2, -1) + each(4, 0) + each(3)
    for i in (1, -1, 2):
        steps += each(4, i)
    for i in (0, 1, -1, 2):
        steps += each(5, i)
    return steps


def gather_kernel(
    own_ref, front_ref, all_ref, top_ref, lead_ref, send_sem, recv_sem, local_sem
):
    wires = Wires(send_sem, recv_sem)
    row, col, chip, core = wires.row, wires.col, wires.chip, wires.core
    fresh, remote = wires.fresh, wires.remote
    load_top = pltpu.make_async_copy(front_ref.at[pl.ds(0, LEAD)], top_ref, local_sem.at[0])

    @pl.when(row == 0)
    def _():
        load_top.start()

    keep_own = pltpu.make_async_copy(own_ref, all_ref.at[col], local_sem.at[1])
    keep_own.start()
    wires.greet(
        wires.col_others()
        + [
            (row + 1 - 2 * core, col),
            (lax.rem(row + 2, ROWS), col),
            (lax.rem(row + 6, ROWS), col),
        ]
    )

    def factor_piece(slot, half, part):
        if part == 0:
            return all_ref.at[slot, pl.ds(half * 128, 128)]
        return all_ref.at[slot, pl.ds(half * 128 + 64 * (part - 1), 64)]

    top_size = LEAD // TOP_PIECES
    half_pieces = TOP_PIECES // 2
    top_recv = fresh(TOP_PIECES)
    top_next = fresh(TOP_PIECES)
    top_side = fresh(TOP_PIECES)

    def top_copies(piece, way):
        block = top_ref.at[pl.ds(piece * top_size, top_size)]
        onward = lax.rem(row + (2 if way == 1 else 6), ROWS)
        return (
            remote(block, block, top_next + piece, top_recv + piece, onward, col),
            remote(block, block, top_side + piece, top_recv + piece, row + 1 - 2 * core, col),
        )

    def top_step(number):
        for way in (1, -1):
            depth = chip if way == 1 else lax.rem(SIDE - chip, SIDE)
            count = number - depth - core
            piece = 2 * count + (0 if way == 1 else 1)

            @pl.when((count >= 0) & (count < half_pieces))
            def _(piece=piece, way=way, depth=depth):
                onward, side = top_copies(piece, way)

                @pl.when(row != 0)
                def _():
                    side.wait_recv()

                @pl.when((core == 0) & (depth < SIDE - 1))
                def _():
                    onward.start()

                @pl.when(core == 0)
                def _():
                    side.start()

    def top_drain(number):
        for way in (1, -1):
            depth = chip if way == 1 else lax.rem(SIDE - chip, SIDE)
            onward, side = top_copies(2 * number + (0 if way == 1 else 1), way)

            @pl.when((core == 0) & (depth < SIDE - 1))
            def _():
                onward.wait_send()

            @pl.when(core == 0)
            def _():
                side.wait_send()

    lead_recv = fresh()
    lead_send = fresh(COLS)

    def lead_copy(step):
        to_col = lax.rem(col + step, COLS)
        rows = pl.ds(to_col * SLICE, SLICE)
        return remote(
            top_ref.at[rows, pl.ds(0, LEAD)],
            lead_ref.at[rows],
            lead_send + step,
            lead_recv,
            row,
            to_col,
        )

    def lead_piece(slot, half, part):
        size = SLICE // 2
        if part == 0:
            return lead_ref.at[pl.ds(slot * SLICE + half * size, size)]
        base = slot * SLICE + half * size + (size // 2) * (part - 1)
        return lead_ref.at[pl.ds(base, size // 2)]

    def lead_start():
        @pl.when(col == 0)
        def _():
            keep = pltpu.make_async_copy(
                top_ref.at[pl.ds(0, SLICE), pl.ds(0, LEAD)],
                lead_ref.at[pl.ds(0, SLICE)],
                local_sem.at[2],
            )
            keep.start()

            @pl.loop(1, COLS)
            def _(step):
                lead_copy(step).start()

            keep.wait()

    def lead_wait():
        @pl.when(col != 0)
        def _():
            lead_copy(1).wait_recv()

    rings = [
        wires.ring(h, factor_piece, lambda h=h: own_ref.at[pl.ds(h * 128, 128)]) for h in range(2)
    ]
    lead_rings = [
        wires.ring(h, lead_piece, lambda h=h: lead_piece(col, h, 0)) for h in range(2)
    ]
    steps = ring_steps(rings)
    lead_steps = ring_steps(lead_rings)
    for run in steps[:4]:
        run()

    @pl.when(row == 0)
    def _():
        load_top.wait()

    top_steps = half_pieces + SIDE
    for number in range(top_steps):
        top_step(number)
        for run in steps[4 + number : 5 + number]:
            run()
    lead_start()
    rest = steps[4 + top_steps :]
    rest[0]()
    rest[1]()
    lead_wait()
    for number in range(max(len(rest) - 2, len(lead_steps) // 2 + 1)):
        for run in lead_steps[2 * number : 2 * number + 2] + rest[number + 2 : number + 3]:
            run()
    keep_own.wait()
    wires.drain()
    for number in range(half_pieces):
        top_drain(number)

    @pl.when(col == 0)
    def _():
        @pl.loop(1, COLS)
        def _(step):
            lead_copy(step).wait_send()


BLOCK = 128
GROUP = 8
GROUPS = BLOCK // GROUP
NEAR = slice(0, BLOCK)
AWAY = slice(BLOCK, TILE)


def spread_kernel(
    top_ref, lead_ref, pan_ref, upper_ref, side_ref, full_ref, low_ref,
    block_ref, inv_ref, work_ref, send_sem, recv_sem, local_sem,
):
    wires = Wires(send_sem, recv_sem)
    row, col = wires.row, wires.col
    fresh, remote = wires.fresh, wires.remote
    wires.greet(wires.col_others())

    def panel_piece(slot, half, part):
        if part == 0:
            return pan_ref.at[half, pl.ds(slot * SLICE, SLICE)]
        size = SLICE // 2
        return pan_ref.at[half, pl.ds(slot * SLICE + size * (part - 1), size)]

    spread = []
    for half in range(2):
        spread.append((half, 2 * row + half, pl.ds(0, COL_WIDTH), pl.ds(0, COL_WIDTH)))
    spread_recv = [fresh() for _ in spread]
    spread_send = [fresh(COLS) for _ in spread]

    def spread_copy(index, step):
        half, _, lanes, to_lanes = spread[index]
        to_col = lax.rem(col + step, COLS)
        rows = pl.ds(to_col * SLICE, SLICE)
        return remote(
            top_ref.at[rows, lanes],
            pan_ref.at[half, rows, to_lanes],
            spread_send[index] + step,
            spread_recv[index],
            row,
            to_col,
        )

    def spread_start(index):
        half, holder, lanes, to_lanes = spread[index]
        rows = pl.ds(col * SLICE, SLICE)

        @pl.when(col == holder)
        def _():
            keep = pltpu.make_async_copy(
                top_ref.at[rows, lanes], pan_ref.at[half, rows, to_lanes], local_sem.at[index]
            )
            keep.start()

            @pl.loop(1, COLS)
            def _(step):
                spread_copy(index, step).start()

            keep.wait()

    def spread_wait(index):
        @pl.when(col != spread[index][1])
        def _():
            spread_copy(index, 1).wait_recv()

    def spread_drain(index):
        @pl.when(col == spread[index][1])
        def _():
            @pl.loop(1, COLS)
            def _(step):
                spread_copy(index, step).wait_send()

    for number in range(2):
        spread_start(number)
    steps = ring_steps(
        [wires.ring(h, panel_piece, lambda h=h: panel_piece(col, h, 0)) for h in range(2)]
    )

    def join_inverse(tile):
        first, second, side = inv_ref[2 * tile], inv_ref[2 * tile + 1], side_ref[tile]
        full_ref[tile, NEAR, NEAR] = first
        full_ref[tile, NEAR, AWAY] = jnp.zeros((BLOCK, BLOCK), F32)
        full_ref[tile, AWAY, NEAR] = -product(second, product(side, first))
        full_ref[tile, AWAY, AWAY] = second

    def second_half(tile, below, corner):
        side = product_rows(below, inv_ref[2 * tile])
        side_ref[tile] = side
        block_ref[...] = corner - product_rows(side, side)

    def body(number, carry):
        @pl.when(number == 0)
        def _():
            block_ref[...] = lead_ref[NEAR, NEAR]

        @pl.when(number == 1)
        def _():
            for index in range(2):
                spread_wait(index)
            for run in steps[:4]:
                run()
            second_half(0, lead_ref[AWAY, NEAR], lead_ref[AWAY, AWAY])

        @pl.when(number == 2)
        def _():
            for run in steps[4:8]:
                run()
            join_inverse(0)
            low = product_rows(lead_ref[TILE:, :TILE], full_ref[0])
            low_ref[...] = low
            work_ref[...] = lead_ref[TILE:, TILE:] - product_rows(low, low)
            block_ref[...] = work_ref[NEAR, NEAR]

        @pl.when(number == 3)
        def _():
            for run in steps[8:12]:
                run()
            second_half(1, work_ref[AWAY, NEAR], work_ref[AWAY, AWAY])

        eliminate(block_ref, upper_ref.at[number], inv_ref.at[number])
        return carry

    lax.fori_loop(0, 4, body, 0)
    for run in steps[12:16]:
        run()
    join_inverse(1)
    for run in steps[16:]:
        run()
    wires.drain()
    for number in range(2):
        spread_drain(number)


def gather_all(own_factor, front):
    anywhere = pl.BlockSpec(memory_space=pl.ANY)
    vmem = pl.BlockSpec(memory_space=pltpu.VMEM)
    return pl.pallas_call(
        gather_kernel,
        out_shape=(
            jax.ShapeDtypeStruct((COLS, TILE, CW), F32),
            jax.ShapeDtypeStruct((LEAD, COL_WIDTH), F32),
            jax.ShapeDtypeStruct((LEAD, LEAD), F32),
        ),
        in_specs=[vmem, anywhere],
        out_specs=(vmem, vmem, vmem),
        scratch_shapes=[
            pltpu.SemaphoreType.DMA((128,)),
            pltpu.SemaphoreType.DMA((128,)),
            pltpu.SemaphoreType.DMA((3,)),
        ],
        compiler_params=pltpu.CompilerParams(
            collective_id=0, has_side_effects=True, vmem_limit_bytes=52 * 2**20
        ),
        name="gather",
    )(own_factor, front)


def spread_panel(top, lead):
    vmem = pl.BlockSpec(memory_space=pltpu.VMEM)
    return pl.pallas_call(
        spread_kernel,
        out_shape=(
            jax.ShapeDtypeStruct((2, LEAD, COL_WIDTH), F32),
            jax.ShapeDtypeStruct((4, BLOCK, BLOCK), F32),
            jax.ShapeDtypeStruct((2, BLOCK, BLOCK), F32),
            jax.ShapeDtypeStruct((2, TILE, TILE), F32),
            jax.ShapeDtypeStruct((TILE, TILE), F32),
        ),
        in_specs=[vmem, vmem],
        out_specs=(vmem,) * 5,
        scratch_shapes=[
            pltpu.VMEM((BLOCK, BLOCK), F32),
            pltpu.VMEM((4, BLOCK, BLOCK), F32),
            pltpu.VMEM((TILE, TILE), F32),
            pltpu.SemaphoreType.DMA((80,)),
            pltpu.SemaphoreType.DMA((80,)),
            pltpu.SemaphoreType.DMA((2,)),
        ],
        compiler_params=pltpu.CompilerParams(
            collective_id=1, has_side_effects=True, vmem_limit_bytes=24 * 2**20
        ),
        cost_estimate=pl.CostEstimate(
            flops=30 * 10**9, bytes_accessed=20 * 2**20, transcendentals=0
        ),
        name="spread",
    )(top, lead)


def eliminate(block_ref, upper_ref, inverse_ref):
    shape = (GROUP, BLOCK)
    lanes = lax.broadcasted_iota(jnp.int32, shape, 1)
    sublanes = lax.broadcasted_iota(jnp.int32, shape, 0)
    left = [block_ref[GROUP * g : GROUP * (g + 1), :] for g in range(GROUPS)]
    right = [jnp.where(lanes == sublanes + GROUP * g, 1.0, 0.0) for g in range(GROUPS)]
    for g in range(GROUPS):
        base = GROUP * g
        row_l = [jnp.broadcast_to(left[g][s : s + 1, :], shape) for s in range(GROUP)]
        row_r = [jnp.broadcast_to(right[g][s : s + 1, :], shape) for s in range(GROUP)]
        entry = {}
        for s in range(GROUP):
            for t in range(s, GROUP):
                entry[s, t] = jnp.broadcast_to(row_l[s][:, base + t : base + t + 1], shape)
        recip = []
        ratio = {}
        for s in range(GROUP):
            recip.append(1.0 / entry[s, s])
            for t in range(s + 1, GROUP):
                ratio[t, s] = entry[s, t] * recip[s]
            for t in range(s + 1, GROUP):
                for u in range(t, GROUP):
                    entry[t, u] = entry[t, u] - ratio[t, s] * entry[s, u]
        for s in range(GROUP):
            for t in range(s):
                row_l[s] = row_l[s] - ratio[s, t] * row_l[t]
                row_r[s] = row_r[s] - ratio[s, t] * row_r[t]
        new_l, new_r, scale = row_l[0], row_r[0], recip[0]
        for s in range(1, GROUP):
            pick = sublanes == s
            new_l = jnp.where(pick, row_l[s], new_l)
            new_r = jnp.where(pick, row_r[s], new_r)
            scale = jnp.where(pick, recip[s], scale)
        for i in range(g + 1, GROUPS):
            plain = []
            for s in range(GROUP):
                value = jnp.broadcast_to(left[i][:, base + s : base + s + 1], shape)
                for t in range(s):
                    value = value - plain[t] * ratio[s, t]
                plain.append(value)
            for s in range(GROUP):
                scaled = plain[s] * recip[s]
                left[i] = left[i] - scaled * row_l[s]
                right[i] = right[i] - scaled * row_r[s]
        scale = jnp.sqrt(scale)
        upper = jnp.where(lanes >= sublanes + base, new_l * scale, 0.0)
        upper_ref[base : base + GROUP, :] = upper
        inverse_ref[base : base + GROUP, :] = new_r * scale


def panel_kernel(
    pan_ref, top_ref, upper_ref, side_ref, full_ref, low_ref, panel_ref, cols_ref
):
    row = lax.axis_index("row")
    col = lax.axis_index("col")
    inverses = [halves(full_ref[t]) for t in range(2)]
    low = halves(low_ref[...])

    def chunk(source, lanes):
        first = three_pass(inverses[0], halves(source[:TILE, lanes]), ((1,), (0,)))
        rest = source[TILE:, lanes] - three_pass(low, halves(first), ((1,), (0,)))
        return first, three_pass(inverses[1], halves(rest), ((1,), (0,)))

    @pl.loop(0, PCT)
    def _(part):
        lanes = pl.ds(pl.multiple_of(part * TILE, TILE), TILE)
        first, second = chunk(top_ref, lanes)
        cols_ref[:TILE, lanes] = first
        cols_ref[TILE:, lanes] = second

    @pl.loop(0, RT)
    def _(part):
        lanes = pl.ds(pl.multiple_of(lax.rem(part, PCT) * TILE, TILE), TILE)
        rows = pl.ds(pl.multiple_of(part * TILE, TILE), TILE)
        first, second = chunk(pan_ref.at[part // PCT], lanes)
        panel_ref[rows, :TILE] = first.T
        panel_ref[rows, TILE:] = second.T

    blank = jnp.zeros((BLOCK, BLOCK), F32)

    @pl.when(col == 0)
    def _():
        for t in range(2):
            for r, c, value in (
                (0, 0, upper_ref[2 * t]),
                (0, 1, side_ref[t].T),
                (1, 0, blank),
                (1, 1, upper_ref[2 * t + 1]),
            ):
                r0, c0 = t * TILE + r * BLOCK, t * TILE + c * BLOCK
                cols_ref[r0 : r0 + BLOCK, c0 : c0 + BLOCK] = value
        cols_ref[TILE:, :TILE] = jnp.zeros((TILE, TILE), F32)

    @pl.when(row == 0)
    def _():
        for t in range(2):
            for r, c, value in (
                (0, 0, upper_ref[2 * t].T),
                (0, 1, blank),
                (1, 0, side_ref[t]),
                (1, 1, upper_ref[2 * t + 1].T),
            ):
                r0, c0 = t * TILE + r * BLOCK, t * TILE + c * BLOCK
                panel_ref[r0 : r0 + BLOCK, c0 : c0 + BLOCK] = value
        panel_ref[:TILE, TILE:] = jnp.zeros((TILE, TILE), F32)


def factor_panel(pan, top, upper, side, full, low):
    vmem = pl.BlockSpec(memory_space=pltpu.VMEM)
    return pl.pallas_call(
        panel_kernel,
        out_shape=(
            jax.ShapeDtypeStruct((PANEL_ROWS, LEAD), F32),
            jax.ShapeDtypeStruct((LEAD, COL_WIDTH), F32),
        ),
        in_specs=[vmem] * 6,
        out_specs=(vmem, vmem),
        compiler_params=pltpu.CompilerParams(vmem_limit_bytes=32 * 2**20),
        cost_estimate=pl.CostEstimate(
            flops=10 * 10**9, bytes_accessed=14 * 2**20, transcendentals=0
        ),
        name="panel",
    )(pan, top, upper, side, full, low)


PAIRS = COLS // 2


def tiles_kernel(order_ref, all_ref, out_ref, high_ref, low_ref):
    step = pl.program_id(0)

    @pl.when(step == 0)
    def _():
        high_ref[...], low_ref[...] = halves(all_ref[order_ref[COLS]])

    right = (high_ref[...], low_ref[...])
    for part in range(2):
        left = halves(all_ref[order_ref[2 * step + part]])
        out_ref[part] = three_pass(left, right, ((1,), (1,)))


def update_tiles(order, factors):
    return pl.pallas_call(
        tiles_kernel,
        out_shape=jax.ShapeDtypeStruct((COLS, TILE, TILE), F32),
        grid_spec=pltpu.PrefetchScalarGridSpec(
            num_scalar_prefetch=1,
            grid=(PAIRS,),
            in_specs=[pl.BlockSpec(memory_space=pltpu.VMEM)],
            out_specs=pl.BlockSpec((2, TILE, TILE), lambda i, order: (i, 0, 0)),
            scratch_shapes=[pltpu.VMEM((TILE, CW), BF16), pltpu.VMEM((TILE, CW), BF16)],
        ),
        cost_estimate=pl.CostEstimate(
            flops=6 * COLS * TILE * TILE * CW, bytes_accessed=12 * 2**20, transcendentals=0
        ),
        name="tiles",
    )(order, factors)


def schur_kernel(
    rows_ref, cols_ref, front_ref, panel_ref, top_ref, tiles_ref, out_ref, high_ref, low_ref
):
    step = pl.program_id(0)

    @pl.when(step == 0)
    def _():
        high_ref[...], low_ref[...] = halves(top_ref[...])

    left = halves(panel_ref[...])
    for part in range(PCT):
        lanes = slice(part * TILE, (part + 1) * TILE)
        right = (high_ref[:, lanes], low_ref[:, lanes])
        out_ref[:, lanes] = front_ref[:, lanes] - three_pass(left, right, ((1,), (0,)))
    block = step // PCT
    for child in range(ROWS):

        @pl.when(rows_ref[child, block] == step)
        def _(child=child):
            start = pl.multiple_of(cols_ref[child] * TILE, TILE)
            out_ref[:, pl.ds(start, TILE)] -= tiles_ref[child, 0]


def schur_update(row_places, col_places, front, panel, top, tiles):
    return pl.pallas_call(
        schur_kernel,
        out_shape=jax.ShapeDtypeStruct((PANEL_ROWS, COL_WIDTH), F32),
        grid_spec=pltpu.PrefetchScalarGridSpec(
            num_scalar_prefetch=2,
            grid=(RT,),
            in_specs=[
                pl.BlockSpec((TILE, COL_WIDTH), lambda i, *_: (i, 0)),
                pl.BlockSpec((TILE, LEAD), lambda i, *_: (i, 0)),
                pl.BlockSpec(memory_space=pltpu.VMEM),
                pl.BlockSpec((ROWS, 1, TILE, TILE), lambda i, *_: (0, i // PCT, 0, 0)),
            ],
            out_specs=pl.BlockSpec((TILE, COL_WIDTH), lambda i, *_: (i, 0)),
            scratch_shapes=[
                pltpu.VMEM((LEAD, COL_WIDTH), BF16),
                pltpu.VMEM((LEAD, COL_WIDTH), BF16),
            ],
        ),
        cost_estimate=pl.CostEstimate(
            flops=6 * PANEL_ROWS * COL_WIDTH * LEAD,
            bytes_accessed=26 * 2**20,
            transcendentals=0,
        ),
        name="schur",
    )(row_places, col_places, front, panel, top, tiles)


def per_device(parent_front, child_panels, child_inverses, parent_index):
    here_row = lax.axis_index("row")
    here_col = lax.axis_index("col")
    own_factor = product_rows(child_panels[0], child_inverses[0])
    factors, top, lead = gather_all(own_factor, parent_front)

    block_of = parent_index // PCT
    my_blocks = lax.dynamic_index_in_dim(block_of, here_row, 0, keepdims=False)
    ids = jnp.arange(COLS, dtype=jnp.int32)
    wanted = jnp.concatenate([ids, here_col[None].astype(jnp.int32)])
    order = jnp.sum(jnp.where(my_blocks[None, :] == wanted[:, None], ids[None, :], 0), axis=1)
    outgoing = update_tiles(order, factors).reshape(ROWS, 2, TILE, TILE)
    outgoing, top, lead = lax.optimization_barrier((outgoing, top, lead))
    tiles = lax.all_to_all(outgoing, "row", split_axis=0, concat_axis=0, tiled=True)

    row_blocks = 2 * here_row + jnp.arange(2, dtype=jnp.int32)
    row_places = (
        jnp.sum(
            jnp.where(
                block_of[:, None, :] == row_blocks[None, :, None], parent_index[:, None, :], 0
            ),
            axis=2,
        )
        - here_row * RT
    )
    col_places = (
        jnp.sum(jnp.where(block_of == here_col, parent_index, 0), axis=1) - here_col * PCT
    )

    panel, upper, side, full, low = spread_panel(top, lead)
    panel_out, top_out = factor_panel(panel, top, upper, side, full, low)
    schur = schur_update(
        row_places.astype(jnp.int32),
        col_places.astype(jnp.int32),
        parent_front,
        panel_out,
        top_out,
        tiles,
    )
    return (panel_out, schur)


def solution(mesh):
    placed = (P("row", "col"), P("row", "col", None), P("row", None, None), P())
    return jax.shard_map(
        per_device,
        mesh=mesh,
        in_specs=placed,
        out_specs=(P("row", None), P("row", "col")),
        check_vma=False,
    )
```

```python
import jax
import jax.numpy as jnp
from jax import lax
from jax.experimental import pallas as pl
from jax.experimental.pallas import tpu as pltpu
from jax.sharding import PartitionSpec as P

TILE = 256
CW = 512
PCT = 4
NSP = 2
ROWS = 8
COLS = 16
SIDE = 4
RT = 8
LEAD = NSP * TILE
PANEL_ROWS = RT * TILE
COL_WIDTH = PCT * TILE
SLICE = LEAD // COLS
TOP_PIECES = 8
MESH = pl.DeviceIdType.MESH
F32 = jnp.float32
BF16 = jnp.bfloat16


def product(matrix_a, matrix_b):
    return jnp.dot(
        matrix_a, matrix_b, precision=lax.Precision.HIGHEST, preferred_element_type=F32
    )


def product_rows(matrix_a, matrix_b):
    return lax.dot_general(
        matrix_a,
        matrix_b,
        (((1,), (1,)), ((), ())),
        precision=lax.Precision.HIGHEST,
        preferred_element_type=F32,
    )


def halves(value):
    high = value.astype(BF16)
    low = (value - high.astype(F32)).astype(BF16)
    return high, low


def three_pass(pair_a, pair_b, contract):
    def one(left, right):
        return lax.dot_general(left, right, (contract, ((), ())), preferred_element_type=F32)

    return one(pair_a[0], pair_b[0]) + (one(pair_a[0], pair_b[1]) + one(pair_a[1], pair_b[0]))


def wrap(value):
    return lax.rem(value + 2 * SIDE, SIDE)


class Wires:
    def __init__(self, send_sem, recv_sem):
        self.row = lax.axis_index("row")
        self.col = lax.axis_index("col")
        self.place_y = self.col // SIDE
        self.place_z = lax.rem(self.col, SIDE)
        self.chip = self.row // 2
        self.core = lax.rem(self.row, 2)
        self.send_sem = send_sem
        self.recv_sem = recv_sem
        self.used = 0
        self.started = []

    def fresh(self, count=1):
        self.used += count
        return self.used - count

    def at(self, step_y, step_z):
        return wrap(self.place_y + step_y) * SIDE + wrap(self.place_z + step_z)

    def remote(self, src, dst, send, recv, to_row, to_col):
        return pltpu.make_async_remote_copy(
            src_ref=src,
            dst_ref=dst,
            send_sem=self.send_sem.at[send],
            recv_sem=self.recv_sem.at[recv],
            device_id=(to_row, to_col),
            device_id_type=MESH,
        )

    def greet(self, devices):
        barrier = pltpu.get_barrier_semaphore()
        for who in devices:
            pl.semaphore_signal(barrier, inc=1, device_id=who, device_id_type=MESH)
        pl.semaphore_wait(barrier, len(devices))

    def col_others(self):
        return [(self.row, lax.rem(self.col + k, COLS)) for k in range(1, COLS)]

    def ring(self, half, piece, own):
        if half == 0:
            place = lambda i, j: self.at(j, i)
        else:
            place = lambda i, j: self.at(i, j)
        sem = {}

        def key(name):
            if name not in sem:
                sem[name] = self.fresh()
            return sem[name]

        pending = {}

        def go(name, i, j, part, to_i, to_j):
            number = key(name)

            def build():
                mine = (i, j) == (0, 0)
                source = own() if mine else piece(place(i, j), half, part)
                target = piece(place(i, j), half, part)
                return self.remote(source, target, number, number, self.row, place(to_i, to_j))

            build().start()
            pending[name] = build
            self.started.append(build)

        def arrived(name):
            pending[name]().wait_recv()

        def quarter(d):
            return 1 if d == 1 else 2

        def first():
            for d in (1, -1):
                go(("a", d), 0, 0, 0, d, 0)

        def second():
            for e in (1, -1):
                go(("b", 0, e), 0, 0, 0, 0, e)

        def near(d):
            arrived(("a", d))
            go(("af", d), -d, 0, quarter(d), d, 0)
            for e in (1, -1):
                go(("b", -d, e), -d, 0, 0, 0, e)

        def far():
            arrived(("af", 1))
            arrived(("af", -1))
            for e in (1, -1):
                go(("b", 2, e), 2, 0, 0, 0, e)

        def cross(i):
            for e in (1, -1):
                arrived(("b", i, e))
                go(("bf", i, e), i, -e, quarter(e), 0, e)

        def last(i):
            for e in (1, -1):
                arrived(("bf", i, e))

        return first, second, near, far, cross, last

    def drain(self):
        for build in self.started:
            build().wait_send()


def ring_steps(rings):
    def each(index, *args):
        return [lambda r=r: r[index](*args) for r in rings]

    steps = each(0) + each(1) + each(2, 1) + each(2, -1) + each(4, 0) + each(3)
    for i in (1, -1, 2):
        steps += each(4, i)
    for i in (0, 1, -1, 2):
        steps += each(5, i)
    return steps


def gather_kernel(
    own_ref, front_ref, all_ref, top_ref, piece_ref, lead_ref, send_sem, recv_sem, local_sem
):
    wires = Wires(send_sem, recv_sem)
    row, col, chip, core = wires.row, wires.col, wires.chip, wires.core
    fresh, remote = wires.fresh, wires.remote
    load_top = pltpu.make_async_copy(front_ref.at[pl.ds(0, LEAD)], top_ref, local_sem.at[0])

    @pl.when(row == 0)
    def _():
        load_top.start()

    keep_own = pltpu.make_async_copy(own_ref, all_ref.at[col], local_sem.at[1])
    keep_own.start()
    wires.greet(
        wires.col_others()
        + [
            (row + 1 - 2 * core, col),
            (lax.rem(row + 2, ROWS), col),
            (lax.rem(row + 6, ROWS), col),
        ]
    )

    def factor_piece(slot, half, part):
        if part == 0:
            return all_ref.at[slot, pl.ds(half * 128, 128)]
        return all_ref.at[slot, pl.ds(half * 128 + 64 * (part - 1), 64)]

    top_size = LEAD // TOP_PIECES
    half_pieces = TOP_PIECES // 2
    top_recv = fresh(TOP_PIECES)
    top_next = fresh(TOP_PIECES)
    top_side = fresh(TOP_PIECES)

    def top_copies(piece, way):
        block = top_ref.at[pl.ds(piece * top_size, top_size)]
        onward = lax.rem(row + (2 if way == 1 else 6), ROWS)
        return (
            remote(block, block, top_next + piece, top_recv + piece, onward, col),
            remote(block, block, top_side + piece, top_recv + piece, row + 1 - 2 * core, col),
        )

    def top_step(number):
        for way in (1, -1):
            depth = chip if way == 1 else lax.rem(SIDE - chip, SIDE)
            count = number - depth - core
            piece = 2 * count + (0 if way == 1 else 1)

            @pl.when((count >= 0) & (count < half_pieces))
            def _(piece=piece, way=way, depth=depth):
                onward, side = top_copies(piece, way)

                @pl.when(row != 0)
                def _():
                    side.wait_recv()

                @pl.when((core == 0) & (depth < SIDE - 1))
                def _():
                    onward.start()

                @pl.when(core == 0)
                def _():
                    side.start()

    def top_drain(number):
        for way in (1, -1):
            depth = chip if way == 1 else lax.rem(SIDE - chip, SIDE)
            onward, side = top_copies(2 * number + (0 if way == 1 else 1), way)

            @pl.when((core == 0) & (depth < SIDE - 1))
            def _():
                onward.wait_send()

            @pl.when(core == 0)
            def _():
                side.wait_send()

    spread = [
        (0, pl.ds(0, LEAD), lead_ref),
        (2 * row, pl.ds(0, COL_WIDTH), piece_ref.at[0]),
        (2 * row + 1, pl.ds(0, COL_WIDTH), piece_ref.at[1]),
    ]
    spread_recv = fresh(len(spread))
    spread_send = fresh(len(spread) * COLS)

    def spread_copy(index, step):
        _, lanes, target = spread[index]
        to_col = lax.rem(col + step, COLS)
        return remote(
            top_ref.at[pl.ds(to_col * SLICE, SLICE), lanes],
            target,
            spread_send + index * COLS + step,
            spread_recv + index,
            row,
            to_col,
        )

    def spread_start(index):
        holder, lanes, target = spread[index]

        @pl.when(col == holder)
        def _():
            keep = pltpu.make_async_copy(
                top_ref.at[pl.ds(col * SLICE, SLICE), lanes], target, local_sem.at[2 + index]
            )
            keep.start()

            @pl.loop(1, COLS)
            def _(step):
                spread_copy(index, step).start()

            keep.wait()

    def spread_wait(index):
        @pl.when(col != spread[index][0])
        def _():
            spread_copy(index, 1).wait_recv()

    def spread_drain(index):
        @pl.when(col == spread[index][0])
        def _():
            @pl.loop(1, COLS)
            def _(step):
                spread_copy(index, step).wait_send()

    rings = [
        wires.ring(h, factor_piece, lambda h=h: own_ref.at[pl.ds(h * 128, 128)]) for h in range(2)
    ]
    steps = ring_steps(rings)
    for run in steps[:4]:
        run()

    @pl.when(row == 0)
    def _():
        load_top.wait()

    top_steps = half_pieces + SIDE
    for number in range(top_steps):
        top_step(number)
        for run in steps[4 + number : 5 + number]:
            run()
    for index in range(len(spread)):
        spread_start(index)
    for run in steps[4 + top_steps :]:
        run()
    for index in range(len(spread)):
        spread_wait(index)
    keep_own.wait()
    wires.drain()
    for number in range(half_pieces):
        top_drain(number)
    for index in range(len(spread)):
        spread_drain(index)


BLOCK = 128
GROUP = 8
GROUPS = BLOCK // GROUP
NEAR = slice(0, BLOCK)
AWAY = slice(BLOCK, TILE)


def factor_kernel(
    pieces_ref, upper_ref, side_ref, full_ref, low_ref, block_ref, inv_ref, work_ref, lead_ref
):
    lead_ref[...] = pieces_ref[...].reshape(LEAD, LEAD)

    def join_inverse(tile):
        first, second, side = inv_ref[2 * tile], inv_ref[2 * tile + 1], side_ref[tile]
        full_ref[tile, NEAR, NEAR] = first
        full_ref[tile, NEAR, AWAY] = jnp.zeros((BLOCK, BLOCK), F32)
        full_ref[tile, AWAY, NEAR] = -product(second, product(side, first))
        full_ref[tile, AWAY, AWAY] = second

    def second_half(tile, below, corner):
        side = product_rows(below, inv_ref[2 * tile])
        side_ref[tile] = side
        block_ref[...] = corner - product_rows(side, side)

    def body(number, carry):
        @pl.when(number == 0)
        def _():
            block_ref[...] = lead_ref[NEAR, NEAR]

        @pl.when(number == 1)
        def _():
            second_half(0, lead_ref[AWAY, NEAR], lead_ref[AWAY, AWAY])

        @pl.when(number == 2)
        def _():
            join_inverse(0)
            low = product_rows(lead_ref[TILE:, :TILE], full_ref[0])
            low_ref[...] = low
            work_ref[...] = lead_ref[TILE:, TILE:] - product_rows(low, low)
            block_ref[...] = work_ref[NEAR, NEAR]

        @pl.when(number == 3)
        def _():
            second_half(1, work_ref[AWAY, NEAR], work_ref[AWAY, AWAY])

        eliminate(block_ref, upper_ref.at[number], inv_ref.at[number])
        return carry

    lax.fori_loop(0, 4, body, 0)
    join_inverse(1)


def gather_all(own_factor, front):
    anywhere = pl.BlockSpec(memory_space=pl.ANY)
    vmem = pl.BlockSpec(memory_space=pltpu.VMEM)
    return pl.pallas_call(
        gather_kernel,
        out_shape=(
            jax.ShapeDtypeStruct((COLS, TILE, CW), F32),
            jax.ShapeDtypeStruct((LEAD, COL_WIDTH), F32),
            jax.ShapeDtypeStruct((2, SLICE, COL_WIDTH), F32),
            jax.ShapeDtypeStruct((SLICE, LEAD), F32),
        ),
        in_specs=[vmem, anywhere],
        out_specs=(vmem,) * 4,
        scratch_shapes=[
            pltpu.SemaphoreType.DMA((128,)),
            pltpu.SemaphoreType.DMA((128,)),
            pltpu.SemaphoreType.DMA((5,)),
        ],
        compiler_params=pltpu.CompilerParams(
            collective_id=0, has_side_effects=True, vmem_limit_bytes=52 * 2**20
        ),
        name="gather",
    )(own_factor, front)


def factor_lead(pieces):
    vmem = pl.BlockSpec(memory_space=pltpu.VMEM)
    return pl.pallas_call(
        factor_kernel,
        out_shape=(
            jax.ShapeDtypeStruct((4, BLOCK, BLOCK), F32),
            jax.ShapeDtypeStruct((2, BLOCK, BLOCK), F32),
            jax.ShapeDtypeStruct((2, TILE, TILE), F32),
            jax.ShapeDtypeStruct((TILE, TILE), F32),
        ),
        in_specs=[vmem],
        out_specs=(vmem,) * 4,
        scratch_shapes=[
            pltpu.VMEM((BLOCK, BLOCK), F32),
            pltpu.VMEM((4, BLOCK, BLOCK), F32),
            pltpu.VMEM((TILE, TILE), F32),
            pltpu.VMEM((LEAD, LEAD), F32),
        ],
        cost_estimate=pl.CostEstimate(
            flops=15 * 10**9, bytes_accessed=20 * 2**20, transcendentals=0
        ),
        name="factor",
    )(pieces)


def eliminate(block_ref, upper_ref, inverse_ref):
    shape = (GROUP, BLOCK)
    lanes = lax.broadcasted_iota(jnp.int32, shape, 1)
    sublanes = lax.broadcasted_iota(jnp.int32, shape, 0)
    left = [block_ref[GROUP * g : GROUP * (g + 1), :] for g in range(GROUPS)]
    right = [jnp.where(lanes == sublanes + GROUP * g, 1.0, 0.0) for g in range(GROUPS)]
    for g in range(GROUPS):
        base = GROUP * g
        row_l = [jnp.broadcast_to(left[g][s : s + 1, :], shape) for s in range(GROUP)]
        row_r = [jnp.broadcast_to(right[g][s : s + 1, :], shape) for s in range(GROUP)]
        entry = {}
        for s in range(GROUP):
            for t in range(s, GROUP):
                entry[s, t] = jnp.broadcast_to(row_l[s][:, base + t : base + t + 1], shape)
        recip = []
        ratio = {}
        for s in range(GROUP):
            recip.append(1.0 / entry[s, s])
            for t in range(s + 1, GROUP):
                ratio[t, s] = entry[s, t] * recip[s]
            for t in range(s + 1, GROUP):
                for u in range(t, GROUP):
                    entry[t, u] = entry[t, u] - ratio[t, s] * entry[s, u]
        for s in range(GROUP):
            for t in range(s):
                row_l[s] = row_l[s] - ratio[s, t] * row_l[t]
                row_r[s] = row_r[s] - ratio[s, t] * row_r[t]
        new_l, new_r, scale = row_l[0], row_r[0], recip[0]
        for s in range(1, GROUP):
            pick = sublanes == s
            new_l = jnp.where(pick, row_l[s], new_l)
            new_r = jnp.where(pick, row_r[s], new_r)
            scale = jnp.where(pick, recip[s], scale)
        for i in range(g + 1, GROUPS):
            plain = []
            for s in range(GROUP):
                value = jnp.broadcast_to(left[i][:, base + s : base + s + 1], shape)
                for t in range(s):
                    value = value - plain[t] * ratio[s, t]
                plain.append(value)
            for s in range(GROUP):
                scaled = plain[s] * recip[s]
                left[i] = left[i] - scaled * row_l[s]
                right[i] = right[i] - scaled * row_r[s]
        scale = jnp.sqrt(scale)
        upper = jnp.where(lanes >= sublanes + base, new_l * scale, 0.0)
        upper_ref[base : base + GROUP, :] = upper
        inverse_ref[base : base + GROUP, :] = new_r * scale


def panel_kernel(
    pan_ref, top_ref, upper_ref, side_ref, full_ref, low_ref, panel_ref, cols_ref
):
    row = lax.axis_index("row")
    col = lax.axis_index("col")
    inverses = [halves(full_ref[t]) for t in range(2)]
    low = halves(low_ref[...])

    def chunk(block):
        first = three_pass(inverses[0], halves(block[:TILE]), ((1,), (0,)))
        rest = block[TILE:] - three_pass(low, halves(first), ((1,), (0,)))
        return first, three_pass(inverses[1], halves(rest), ((1,), (0,)))

    @pl.loop(0, PCT)
    def _(part):
        lanes = pl.ds(pl.multiple_of(part * TILE, TILE), TILE)
        first, second = chunk(top_ref[:, lanes])
        cols_ref[:TILE, lanes] = first
        cols_ref[TILE:, lanes] = second

    @pl.loop(0, RT)
    def _(part):
        lanes = pl.ds(pl.multiple_of(lax.rem(part, PCT) * TILE, TILE), TILE)
        rows = pl.ds(pl.multiple_of(part * TILE, TILE), TILE)
        block = pan_ref[:, part // PCT, :, lanes].reshape(LEAD, TILE)
        first, second = chunk(block)
        panel_ref[rows, :TILE] = first.T
        panel_ref[rows, TILE:] = second.T

    blank = jnp.zeros((BLOCK, BLOCK), F32)

    @pl.when(col == 0)
    def _():
        for t in range(2):
            for r, c, value in (
                (0, 0, upper_ref[2 * t]),
                (0, 1, side_ref[t].T),
                (1, 0, blank),
                (1, 1, upper_ref[2 * t + 1]),
            ):
                r0, c0 = t * TILE + r * BLOCK, t * TILE + c * BLOCK
                cols_ref[r0 : r0 + BLOCK, c0 : c0 + BLOCK] = value
        cols_ref[TILE:, :TILE] = jnp.zeros((TILE, TILE), F32)

    @pl.when(row == 0)
    def _():
        for t in range(2):
            for r, c, value in (
                (0, 0, upper_ref[2 * t].T),
                (0, 1, blank),
                (1, 0, side_ref[t]),
                (1, 1, upper_ref[2 * t + 1].T),
            ):
                r0, c0 = t * TILE + r * BLOCK, t * TILE + c * BLOCK
                panel_ref[r0 : r0 + BLOCK, c0 : c0 + BLOCK] = value
        panel_ref[:TILE, TILE:] = jnp.zeros((TILE, TILE), F32)


def factor_panel(pan, top, upper, side, full, low):
    vmem = pl.BlockSpec(memory_space=pltpu.VMEM)
    return pl.pallas_call(
        panel_kernel,
        out_shape=(
            jax.ShapeDtypeStruct((PANEL_ROWS, LEAD), F32),
            jax.ShapeDtypeStruct((LEAD, COL_WIDTH), F32),
        ),
        in_specs=[vmem] * 6,
        out_specs=(vmem, vmem),
        compiler_params=pltpu.CompilerParams(vmem_limit_bytes=32 * 2**20),
        cost_estimate=pl.CostEstimate(
            flops=10 * 10**9, bytes_accessed=14 * 2**20, transcendentals=0
        ),
        name="panel",
    )(pan, top, upper, side, full, low)


PAIRS = COLS // 2


def tiles_kernel(order_ref, all_ref, out_ref, high_ref, low_ref):
    step = pl.program_id(0)

    @pl.when(step == 0)
    def _():
        high_ref[...], low_ref[...] = halves(all_ref[order_ref[COLS]])

    right = (high_ref[...], low_ref[...])
    for part in range(2):
        left = halves(all_ref[order_ref[2 * step + part]])
        out_ref[part] = three_pass(left, right, ((1,), (1,)))


def update_tiles(order, factors):
    return pl.pallas_call(
        tiles_kernel,
        out_shape=jax.ShapeDtypeStruct((COLS, TILE, TILE), F32),
        grid_spec=pltpu.PrefetchScalarGridSpec(
            num_scalar_prefetch=1,
            grid=(PAIRS,),
            in_specs=[pl.BlockSpec(memory_space=pltpu.VMEM)],
            out_specs=pl.BlockSpec((2, TILE, TILE), lambda i, order: (i, 0, 0)),
            scratch_shapes=[pltpu.VMEM((TILE, CW), BF16), pltpu.VMEM((TILE, CW), BF16)],
        ),
        cost_estimate=pl.CostEstimate(
            flops=6 * COLS * TILE * TILE * CW, bytes_accessed=12 * 2**20, transcendentals=0
        ),
        name="tiles",
    )(order, factors)


def schur_kernel(
    rows_ref, cols_ref, front_ref, panel_ref, top_ref, tiles_ref, out_ref, high_ref, low_ref
):
    step = pl.program_id(0)

    @pl.when(step == 0)
    def _():
        high_ref[...], low_ref[...] = halves(top_ref[...])

    left = halves(panel_ref[...])
    for part in range(PCT):
        lanes = slice(part * TILE, (part + 1) * TILE)
        right = (high_ref[:, lanes], low_ref[:, lanes])
        out_ref[:, lanes] = front_ref[:, lanes] - three_pass(left, right, ((1,), (0,)))
    block = step // PCT
    for child in range(ROWS):

        @pl.when(rows_ref[child, block] == step)
        def _(child=child):
            start = pl.multiple_of(cols_ref[child] * TILE, TILE)
            out_ref[:, pl.ds(start, TILE)] -= tiles_ref[child, 0]


def schur_update(row_places, col_places, front, panel, top, tiles):
    return pl.pallas_call(
        schur_kernel,
        out_shape=jax.ShapeDtypeStruct((PANEL_ROWS, COL_WIDTH), F32),
        grid_spec=pltpu.PrefetchScalarGridSpec(
            num_scalar_prefetch=2,
            grid=(RT,),
            in_specs=[
                pl.BlockSpec((TILE, COL_WIDTH), lambda i, *_: (i, 0)),
                pl.BlockSpec((TILE, LEAD), lambda i, *_: (i, 0)),
                pl.BlockSpec(memory_space=pltpu.VMEM),
                pl.BlockSpec((ROWS, 1, TILE, TILE), lambda i, *_: (0, i // PCT, 0, 0)),
            ],
            out_specs=pl.BlockSpec((TILE, COL_WIDTH), lambda i, *_: (i, 0)),
            scratch_shapes=[
                pltpu.VMEM((LEAD, COL_WIDTH), BF16),
                pltpu.VMEM((LEAD, COL_WIDTH), BF16),
            ],
        ),
        cost_estimate=pl.CostEstimate(
            flops=6 * PANEL_ROWS * COL_WIDTH * LEAD,
            bytes_accessed=26 * 2**20,
            transcendentals=0,
        ),
        name="schur",
    )(row_places, col_places, front, panel, top, tiles)


def per_device(parent_front, child_panels, child_inverses, parent_index):
    here_row = lax.axis_index("row")
    here_col = lax.axis_index("col")
    own_factor = product_rows(child_panels[0], child_inverses[0])
    factors, top, piece, lead = gather_all(own_factor, parent_front)
    lead = lax.all_gather(lead, "col", axis=0)
    panel = lax.all_gather(piece, "col", axis=0)

    block_of = parent_index // PCT
    my_blocks = lax.dynamic_index_in_dim(block_of, here_row, 0, keepdims=False)
    ids = jnp.arange(COLS, dtype=jnp.int32)
    wanted = jnp.concatenate([ids, here_col[None].astype(jnp.int32)])
    order = jnp.sum(jnp.where(my_blocks[None, :] == wanted[:, None], ids[None, :], 0), axis=1)
    outgoing = update_tiles(order, factors).reshape(ROWS, 2, TILE, TILE)
    tiles = lax.all_to_all(outgoing, "row", split_axis=0, concat_axis=0, tiled=True)

    row_blocks = 2 * here_row + jnp.arange(2, dtype=jnp.int32)
    row_places = (
        jnp.sum(
            jnp.where(
                block_of[:, None, :] == row_blocks[None, :, None], parent_index[:, None, :], 0
            ),
            axis=2,
        )
        - here_row * RT
    )
    col_places = (
        jnp.sum(jnp.where(block_of == here_col, parent_index, 0), axis=1) - here_col * PCT
    )

    upper, side, full, low = factor_lead(lead)
    panel_out, top_out = factor_panel(panel, top, upper, side, full, low)
    schur = schur_update(
        row_places.astype(jnp.int32),
        col_places.astype(jnp.int32),
        parent_front,
        panel_out,
        top_out,
        tiles,
    )
    return (panel_out, schur)


def solution(mesh):
    placed = (P("row", "col"), P("row", "col", None), P("row", None, None), P())
    return jax.shard_map(
        per_device,
        mesh=mesh,
        in_specs=placed,
        out_specs=(P("row", None), P("row", "col")),
        check_vma=False,
    )
```

```python
import jax
import jax.numpy as jnp
from jax import lax
from jax.experimental import pallas as pl
from jax.experimental.pallas import tpu as pltpu
from jax.sharding import PartitionSpec as P

TILE = 256
CW = 512
PCT = 4
NSP = 2
ROWS = 8
COLS = 16
SIDE = 4
RT = 8
LEAD = NSP * TILE
PANEL_ROWS = RT * TILE
COL_WIDTH = PCT * TILE
SLICE = LEAD // COLS
TOP_PIECES = 8
MESH = pl.DeviceIdType.MESH
F32 = jnp.float32
BF16 = jnp.bfloat16


def product(matrix_a, matrix_b):
    return jnp.dot(
        matrix_a, matrix_b, precision=lax.Precision.HIGHEST, preferred_element_type=F32
    )


def product_rows(matrix_a, matrix_b):
    return lax.dot_general(
        matrix_a,
        matrix_b,
        (((1,), (1,)), ((), ())),
        precision=lax.Precision.HIGHEST,
        preferred_element_type=F32,
    )


def halves(value):
    high = value.astype(BF16)
    low = (value - high.astype(F32)).astype(BF16)
    return high, low


def three_pass(pair_a, pair_b, contract):
    def one(left, right):
        return lax.dot_general(left, right, (contract, ((), ())), preferred_element_type=F32)

    return one(pair_a[0], pair_b[0]) + (one(pair_a[0], pair_b[1]) + one(pair_a[1], pair_b[0]))


def wrap(value):
    return lax.rem(value + 2 * SIDE, SIDE)


class Wires:
    def __init__(self, send_sem, recv_sem):
        self.row = lax.axis_index("row")
        self.col = lax.axis_index("col")
        self.place_y = self.col // SIDE
        self.place_z = lax.rem(self.col, SIDE)
        self.chip = self.row // 2
        self.core = lax.rem(self.row, 2)
        self.send_sem = send_sem
        self.recv_sem = recv_sem
        self.used = 0
        self.started = []

    def fresh(self, count=1):
        self.used += count
        return self.used - count

    def at(self, step_y, step_z):
        return wrap(self.place_y + step_y) * SIDE + wrap(self.place_z + step_z)

    def remote(self, src, dst, send, recv, to_row, to_col):
        return pltpu.make_async_remote_copy(
            src_ref=src,
            dst_ref=dst,
            send_sem=self.send_sem.at[send],
            recv_sem=self.recv_sem.at[recv],
            device_id=(to_row, to_col),
            device_id_type=MESH,
        )

    def greet(self, devices):
        barrier = pltpu.get_barrier_semaphore()
        for who in devices:
            pl.semaphore_signal(barrier, inc=1, device_id=who, device_id_type=MESH)
        pl.semaphore_wait(barrier, len(devices))

    def col_others(self):
        return [(self.row, lax.rem(self.col + k, COLS)) for k in range(1, COLS)]

    def ring(self, half, piece, own):
        if half == 0:
            place = lambda i, j: self.at(j, i)
        else:
            place = lambda i, j: self.at(i, j)
        sem = {}

        def key(name):
            if name not in sem:
                sem[name] = self.fresh()
            return sem[name]

        pending = {}

        def go(name, i, j, part, to_i, to_j):
            number = key(name)

            def build():
                mine = (i, j) == (0, 0)
                source = own() if mine else piece(place(i, j), half, part)
                target = piece(place(i, j), half, part)
                return self.remote(source, target, number, number, self.row, place(to_i, to_j))

            build().start()
            pending[name] = build
            self.started.append(build)

        def arrived(name):
            pending[name]().wait_recv()

        def quarter(d):
            return 1 if d == 1 else 2

        def first():
            for d in (1, -1):
                go(("a", d), 0, 0, 0, d, 0)

        def second():
            for e in (1, -1):
                go(("b", 0, e), 0, 0, 0, 0, e)

        def near(d):
            arrived(("a", d))
            go(("af", d), -d, 0, quarter(d), d, 0)
            for e in (1, -1):
                go(("b", -d, e), -d, 0, 0, 0, e)

        def far():
            arrived(("af", 1))
            arrived(("af", -1))
            for e in (1, -1):
                go(("b", 2, e), 2, 0, 0, 0, e)

        def cross(i):
            for e in (1, -1):
                arrived(("b", i, e))
                go(("bf", i, e), i, -e, quarter(e), 0, e)

        def last(i):
            for e in (1, -1):
                arrived(("bf", i, e))

        return first, second, near, far, cross, last

    def drain(self):
        for build in self.started:
            build().wait_send()


def ring_steps(rings):
    def each(index, *args):
        return [lambda r=r: r[index](*args) for r in rings]

    steps = each(0) + each(1) + each(2, 1) + each(2, -1) + each(4, 0) + each(3)
    for i in (1, -1, 2):
        steps += each(4, i)
    for i in (0, 1, -1, 2):
        steps += each(5, i)
    return steps


def gather_kernel(
    order_ref, own_ref, front_ref, tiles_ref, top_ref,
    all_ref, high_ref, low_ref, send_sem, recv_sem, local_sem,
):
    wires = Wires(send_sem, recv_sem)
    row, col, chip, core = wires.row, wires.col, wires.chip, wires.core
    fresh, remote = wires.fresh, wires.remote
    load_top = pltpu.make_async_copy(front_ref.at[pl.ds(0, LEAD)], top_ref, local_sem.at[0])

    @pl.when(row == 0)
    def _():
        load_top.start()

    keep_own = pltpu.make_async_copy(own_ref, all_ref.at[col], local_sem.at[1])
    keep_own.start()
    wires.greet(
        [(row, wires.at(*step)) for step in ((1, 0), (-1, 0), (0, 1), (0, -1))]
        + [
            (row + 1 - 2 * core, col),
            (lax.rem(row + 2, ROWS), col),
            (lax.rem(row + 6, ROWS), col),
        ]
    )

    def factor_piece(slot, half, part):
        if part == 0:
            return all_ref.at[slot, pl.ds(half * 128, 128)]
        return all_ref.at[slot, pl.ds(half * 128 + 64 * (part - 1), 64)]

    top_size = LEAD // TOP_PIECES
    half_pieces = TOP_PIECES // 2
    top_recv = fresh(TOP_PIECES)
    top_next = fresh(TOP_PIECES)
    top_side = fresh(TOP_PIECES)

    def top_copies(piece, way):
        block = top_ref.at[pl.ds(piece * top_size, top_size)]
        onward = lax.rem(row + (2 if way == 1 else 6), ROWS)
        return (
            remote(block, block, top_next + piece, top_recv + piece, onward, col),
            remote(block, block, top_side + piece, top_recv + piece, row + 1 - 2 * core, col),
        )

    def top_step(number):
        for way in (1, -1):
            depth = chip if way == 1 else lax.rem(SIDE - chip, SIDE)
            count = number - depth - core
            piece = 2 * count + (0 if way == 1 else 1)

            @pl.when((count >= 0) & (count < half_pieces))
            def _(piece=piece, way=way, depth=depth):
                onward, side = top_copies(piece, way)

                @pl.when(row != 0)
                def _():
                    side.wait_recv()

                @pl.when((core == 0) & (depth < SIDE - 1))
                def _():
                    onward.start()

                @pl.when(core == 0)
                def _():
                    side.start()

    def top_drain(number):
        for way in (1, -1):
            depth = chip if way == 1 else lax.rem(SIDE - chip, SIDE)
            onward, side = top_copies(2 * number + (0 if way == 1 else 1), way)

            @pl.when((core == 0) & (depth < SIDE - 1))
            def _():
                onward.wait_send()

            @pl.when(core == 0)
            def _():
                side.wait_send()

    rings = [
        wires.ring(h, factor_piece, lambda h=h: own_ref.at[pl.ds(h * 128, 128)]) for h in range(2)
    ]
    steps = ring_steps(rings)
    for run in steps[:4]:
        run()

    @pl.when(row == 0)
    def _():
        load_top.wait()

    for number in range(half_pieces + SIDE):
        top_step(number)
        for run in steps[4 + 2 * number : 6 + 2 * number]:
            run()
    for run in steps[4 + 2 * (half_pieces + SIDE) :]:
        run()
    keep_own.wait()
    high_ref[...], low_ref[...] = halves(all_ref[order_ref[COLS]])

    @pl.loop(0, COLS)
    def _(number):
        left = halves(all_ref[order_ref[number]])
        tiles_ref[number] = three_pass(left, (high_ref[...], low_ref[...]), ((1,), (1,)))

    wires.drain()
    for number in range(half_pieces):
        top_drain(number)


BLOCK = 128
GROUP = 8
GROUPS = BLOCK // GROUP
NEAR = slice(0, BLOCK)
AWAY = slice(BLOCK, TILE)


def spread_kernel(
    top_ref, pan_ref, upper_ref, side_ref, full_ref, low_ref,
    block_ref, inv_ref, work_ref, lead_ref, send_sem, recv_sem, local_sem,
):
    wires = Wires(send_sem, recv_sem)
    row, col = wires.row, wires.col
    fresh, remote = wires.fresh, wires.remote
    wires.greet(wires.col_others())

    def panel_piece(slot, half, part):
        if part == 0:
            return pan_ref.at[half, pl.ds(slot * SLICE, SLICE)]
        size = SLICE // 2
        return pan_ref.at[half, pl.ds(slot * SLICE + size * (part - 1), size)]

    spread = []
    for half in range(2):
        spread.append((half, 2 * row + half, pl.ds(0, COL_WIDTH), pl.ds(0, COL_WIDTH)))
    spread_recv = [fresh() for _ in spread]
    spread_send = [fresh(COLS) for _ in spread]

    def spread_copy(index, step):
        half, _, lanes, to_lanes = spread[index]
        to_col = lax.rem(col + step, COLS)
        rows = pl.ds(to_col * SLICE, SLICE)
        return remote(
            top_ref.at[rows, lanes],
            pan_ref.at[half, rows, to_lanes],
            spread_send[index] + step,
            spread_recv[index],
            row,
            to_col,
        )

    def spread_start(index):
        half, holder, lanes, to_lanes = spread[index]
        rows = pl.ds(col * SLICE, SLICE)

        @pl.when(col == holder)
        def _():
            keep = pltpu.make_async_copy(
                top_ref.at[rows, lanes], pan_ref.at[half, rows, to_lanes], local_sem.at[index]
            )
            keep.start()

            @pl.loop(1, COLS)
            def _(step):
                spread_copy(index, step).start()

            keep.wait()

    def spread_wait(index):
        @pl.when(col != spread[index][1])
        def _():
            spread_copy(index, 1).wait_recv()

    def spread_drain(index):
        @pl.when(col == spread[index][1])
        def _():
            @pl.loop(1, COLS)
            def _(step):
                spread_copy(index, step).wait_send()

    lead_recv = fresh()
    lead_send = fresh(COLS)

    def lead_copy(step):
        to_col = lax.rem(col + step, COLS)
        rows = pl.ds(to_col * SLICE, SLICE)
        return remote(
            top_ref.at[rows, pl.ds(0, LEAD)],
            lead_ref.at[rows],
            lead_send + step,
            lead_recv,
            row,
            to_col,
        )

    def lead_piece(slot, half, part):
        size = SLICE // 2
        if part == 0:
            return lead_ref.at[pl.ds(slot * SLICE + half * size, size)]
        base = slot * SLICE + half * size + (size // 2) * (part - 1)
        return lead_ref.at[pl.ds(base, size // 2)]

    def lead_start():
        @pl.when(col == 0)
        def _():
            keep = pltpu.make_async_copy(
                top_ref.at[pl.ds(0, SLICE), pl.ds(0, LEAD)],
                lead_ref.at[pl.ds(0, SLICE)],
                local_sem.at[2],
            )
            keep.start()

            @pl.loop(1, COLS)
            def _(step):
                lead_copy(step).start()

            keep.wait()

    def lead_wait():
        @pl.when(col != 0)
        def _():
            lead_copy(1).wait_recv()

    lead_start()
    for number in range(2):
        spread_start(number)
    lead_rings = [
        wires.ring(h, lead_piece, lambda h=h: lead_piece(col, h, 0)) for h in range(2)
    ]
    steps = ring_steps(
        [wires.ring(h, panel_piece, lambda h=h: panel_piece(col, h, 0)) for h in range(2)]
    )
    lead_wait()
    for run in ring_steps(lead_rings):
        run()

    def join_inverse(tile):
        first, second, side = inv_ref[2 * tile], inv_ref[2 * tile + 1], side_ref[tile]
        full_ref[tile, NEAR, NEAR] = first
        full_ref[tile, NEAR, AWAY] = jnp.zeros((BLOCK, BLOCK), F32)
        full_ref[tile, AWAY, NEAR] = -product(second, product(side, first))
        full_ref[tile, AWAY, AWAY] = second

    def second_half(tile, below, corner):
        side = product_rows(below, inv_ref[2 * tile])
        side_ref[tile] = side
        block_ref[...] = corner - product_rows(side, side)

    def body(number, carry):
        @pl.when(number == 0)
        def _():
            for index in range(2):
                spread_wait(index)
            for run in steps[:4]:
                run()
            block_ref[...] = lead_ref[NEAR, NEAR]

        @pl.when(number == 1)
        def _():
            for run in steps[4:8]:
                run()
            second_half(0, lead_ref[AWAY, NEAR], lead_ref[AWAY, AWAY])

        @pl.when(number == 2)
        def _():
            for run in steps[8:12]:
                run()
            join_inverse(0)
            low = product_rows(lead_ref[TILE:, :TILE], full_ref[0])
            low_ref[...] = low
            work_ref[...] = lead_ref[TILE:, TILE:] - product_rows(low, low)
            block_ref[...] = work_ref[NEAR, NEAR]

        @pl.when(number == 3)
        def _():
            for run in steps[12:16]:
                run()
            second_half(1, work_ref[AWAY, NEAR], work_ref[AWAY, AWAY])

        eliminate(block_ref, upper_ref.at[number], inv_ref.at[number])
        return carry

    lax.fori_loop(0, 4, body, 0)
    join_inverse(1)
    for run in steps[16:]:
        run()
    wires.drain()
    for number in range(2):
        spread_drain(number)

    @pl.when(col == 0)
    def _():
        @pl.loop(1, COLS)
        def _(step):
            lead_copy(step).wait_send()


def gather_tiles(order, own_factor, front):
    anywhere = pl.BlockSpec(memory_space=pl.ANY)
    vmem = pl.BlockSpec(memory_space=pltpu.VMEM)
    return pl.pallas_call(
        gather_kernel,
        out_shape=(
            jax.ShapeDtypeStruct((COLS, TILE, TILE), F32),
            jax.ShapeDtypeStruct((LEAD, COL_WIDTH), F32),
        ),
        in_specs=[pl.BlockSpec(memory_space=pltpu.SMEM), vmem, anywhere],
        out_specs=(vmem, vmem),
        scratch_shapes=[
            pltpu.VMEM((COLS, TILE, CW), F32),
            pltpu.VMEM((TILE, CW), BF16),
            pltpu.VMEM((TILE, CW), BF16),
            pltpu.SemaphoreType.DMA((72,)),
            pltpu.SemaphoreType.DMA((72,)),
            pltpu.SemaphoreType.DMA((2,)),
        ],
        compiler_params=pltpu.CompilerParams(
            collective_id=0, has_side_effects=True, vmem_limit_bytes=56 * 2**20
        ),
        name="gather",
    )(order, own_factor, front)


def spread_panel(top):
    vmem = pl.BlockSpec(memory_space=pltpu.VMEM)
    return pl.pallas_call(
        spread_kernel,
        out_shape=(
            jax.ShapeDtypeStruct((2, LEAD, COL_WIDTH), F32),
            jax.ShapeDtypeStruct((4, BLOCK, BLOCK), F32),
            jax.ShapeDtypeStruct((2, BLOCK, BLOCK), F32),
            jax.ShapeDtypeStruct((2, TILE, TILE), F32),
            jax.ShapeDtypeStruct((TILE, TILE), F32),
        ),
        in_specs=[vmem],
        out_specs=(vmem,) * 5,
        scratch_shapes=[
            pltpu.VMEM((BLOCK, BLOCK), F32),
            pltpu.VMEM((4, BLOCK, BLOCK), F32),
            pltpu.VMEM((TILE, TILE), F32),
            pltpu.VMEM((LEAD, LEAD), F32),
            pltpu.SemaphoreType.DMA((136,)),
            pltpu.SemaphoreType.DMA((136,)),
            pltpu.SemaphoreType.DMA((3,)),
        ],
        compiler_params=pltpu.CompilerParams(
            collective_id=1, has_side_effects=True, vmem_limit_bytes=56 * 2**20
        ),
        cost_estimate=pl.CostEstimate(
            flops=30 * 10**9, bytes_accessed=20 * 2**20, transcendentals=0
        ),
        name="spread",
    )(top)


def eliminate(block_ref, upper_ref, inverse_ref):
    shape = (GROUP, BLOCK)
    lanes = lax.broadcasted_iota(jnp.int32, shape, 1)
    sublanes = lax.broadcasted_iota(jnp.int32, shape, 0)
    left = [block_ref[GROUP * g : GROUP * (g + 1), :] for g in range(GROUPS)]
    right = [jnp.where(lanes == sublanes + GROUP * g, 1.0, 0.0) for g in range(GROUPS)]
    for g in range(GROUPS):
        base = GROUP * g
        row_l = [jnp.broadcast_to(left[g][s : s + 1, :], shape) for s in range(GROUP)]
        row_r = [jnp.broadcast_to(right[g][s : s + 1, :], shape) for s in range(GROUP)]
        entry = {}
        for s in range(GROUP):
            for t in range(s, GROUP):
                entry[s, t] = jnp.broadcast_to(row_l[s][:, base + t : base + t + 1], shape)
        recip = []
        ratio = {}
        for s in range(GROUP):
            recip.append(1.0 / entry[s, s])
            for t in range(s + 1, GROUP):
                ratio[t, s] = entry[s, t] * recip[s]
            for t in range(s + 1, GROUP):
                for u in range(t, GROUP):
                    entry[t, u] = entry[t, u] - ratio[t, s] * entry[s, u]
        for s in range(GROUP):
            for t in range(s):
                row_l[s] = row_l[s] - ratio[s, t] * row_l[t]
                row_r[s] = row_r[s] - ratio[s, t] * row_r[t]
        new_l, new_r, scale = row_l[0], row_r[0], recip[0]
        for s in range(1, GROUP):
            pick = sublanes == s
            new_l = jnp.where(pick, row_l[s], new_l)
            new_r = jnp.where(pick, row_r[s], new_r)
            scale = jnp.where(pick, recip[s], scale)
        for i in range(g + 1, GROUPS):
            plain = []
            for s in range(GROUP):
                value = jnp.broadcast_to(left[i][:, base + s : base + s + 1], shape)
                for t in range(s):
                    value = value - plain[t] * ratio[s, t]
                plain.append(value)
            for s in range(GROUP):
                scaled = plain[s] * recip[s]
                left[i] = left[i] - scaled * row_l[s]
                right[i] = right[i] - scaled * row_r[s]
        scale = jnp.sqrt(scale)
        upper = jnp.where(lanes >= sublanes + base, new_l * scale, 0.0)
        upper_ref[base : base + GROUP, :] = upper
        inverse_ref[base : base + GROUP, :] = new_r * scale


def final_kernel(
    rows_ref, cols_ref, front_ref, pan_ref, top_ref, upper_ref, side_ref, full_ref, low_ref,
    tiles_ref, panel_ref, out_ref, right_ref, high_ref, small_ref,
):
    row = lax.axis_index("row")
    col = lax.axis_index("col")
    step = pl.program_id(0)
    inverses = [halves(full_ref[t]) for t in range(2)]
    low = halves(low_ref[...])
    blank = jnp.zeros((BLOCK, BLOCK), F32)

    def chunk(block):
        first = three_pass(inverses[0], halves(block[:TILE]), ((1,), (0,)))
        rest = block[TILE:] - three_pass(low, halves(first), ((1,), (0,)))
        return first, three_pass(inverses[1], halves(rest), ((1,), (0,)))

    @pl.when(step == 0)
    def _():
        for part in range(PCT):
            lanes = slice(part * TILE, (part + 1) * TILE)
            right_ref[:TILE, lanes], right_ref[TILE:, lanes] = chunk(top_ref[:, lanes])

        @pl.when(col == 0)
        def _():
            for t in range(2):
                for r, c, value in (
                    (0, 0, upper_ref[2 * t]),
                    (0, 1, side_ref[t].T),
                    (1, 0, blank),
                    (1, 1, upper_ref[2 * t + 1]),
                ):
                    r0, c0 = t * TILE + r * BLOCK, t * TILE + c * BLOCK
                    right_ref[r0 : r0 + BLOCK, c0 : c0 + BLOCK] = value
            right_ref[TILE:, :TILE] = jnp.zeros((TILE, TILE), F32)

        high_ref[...], small_ref[...] = halves(right_ref[...])

    first, second = chunk(pan_ref[0])
    panel_ref[:, :TILE] = first.T
    panel_ref[:, TILE:] = second.T

    for t in range(2):

        @pl.when((row == 0) & (step == t))
        def _(t=t):
            for r, c, value in (
                (0, 0, upper_ref[2 * t].T),
                (0, 1, blank),
                (1, 0, side_ref[t]),
                (1, 1, upper_ref[2 * t + 1].T),
            ):
                r0, c0 = r * BLOCK, t * TILE + c * BLOCK
                panel_ref[r0 : r0 + BLOCK, c0 : c0 + BLOCK] = value
            if t == 0:
                panel_ref[:, TILE:] = jnp.zeros((TILE, TILE), F32)

    left = halves(panel_ref[...])
    for part in range(PCT):
        span = slice(part * TILE, (part + 1) * TILE)
        right = (high_ref[:, span], small_ref[:, span])
        out_ref[:, span] = front_ref[:, span] - three_pass(left, right, ((1,), (0,)))
    block = step // PCT
    for child in range(ROWS):

        @pl.when(rows_ref[child, block] == step)
        def _(child=child):
            start = pl.multiple_of(cols_ref[child] * TILE, TILE)
            out_ref[:, pl.ds(start, TILE)] -= tiles_ref[child, 0]


def finish(row_places, col_places, front, pan, top, upper, side, full, low, tiles):
    return pl.pallas_call(
        final_kernel,
        out_shape=(
            jax.ShapeDtypeStruct((PANEL_ROWS, LEAD), F32),
            jax.ShapeDtypeStruct((PANEL_ROWS, COL_WIDTH), F32),
        ),
        grid_spec=pltpu.PrefetchScalarGridSpec(
            num_scalar_prefetch=2,
            grid=(RT,),
            in_specs=[
                pl.BlockSpec((TILE, COL_WIDTH), lambda i, *_: (i, 0)),
                pl.BlockSpec((1, LEAD, TILE), lambda i, *_: (i // PCT, 0, lax.rem(i, PCT))),
                pl.BlockSpec((LEAD, COL_WIDTH), lambda i, *_: (0, 0)),
                pl.BlockSpec((4, BLOCK, BLOCK), lambda i, *_: (0, 0, 0)),
                pl.BlockSpec((2, BLOCK, BLOCK), lambda i, *_: (0, 0, 0)),
                pl.BlockSpec((2, TILE, TILE), lambda i, *_: (0, 0, 0)),
                pl.BlockSpec((TILE, TILE), lambda i, *_: (0, 0)),
                pl.BlockSpec((ROWS, 1, TILE, TILE), lambda i, *_: (0, i // PCT, 0, 0)),
            ],
            out_specs=(
                pl.BlockSpec((TILE, LEAD), lambda i, *_: (i, 0)),
                pl.BlockSpec((TILE, COL_WIDTH), lambda i, *_: (i, 0)),
            ),
            scratch_shapes=[
                pltpu.VMEM((LEAD, COL_WIDTH), F32),
                pltpu.VMEM((LEAD, COL_WIDTH), BF16),
                pltpu.VMEM((LEAD, COL_WIDTH), BF16),
            ],
        ),
        compiler_params=pltpu.CompilerParams(vmem_limit_bytes=40 * 2**20),
        cost_estimate=pl.CostEstimate(
            flops=9 * PANEL_ROWS * COL_WIDTH * LEAD,
            bytes_accessed=30 * 2**20,
            transcendentals=0,
        ),
        name="finish",
    )(row_places, col_places, front, pan, top, upper, side, full, low, tiles)


def per_device(parent_front, child_panels, child_inverses, parent_index):
    here_row = lax.axis_index("row")
    here_col = lax.axis_index("col")
    own_factor = product_rows(child_panels[0], child_inverses[0])
    block_of = parent_index // PCT
    my_blocks = lax.dynamic_index_in_dim(block_of, here_row, 0, keepdims=False)
    ids = jnp.arange(COLS, dtype=jnp.int32)
    wanted = jnp.concatenate([ids, here_col[None].astype(jnp.int32)])
    order = jnp.sum(jnp.where(my_blocks[None, :] == wanted[:, None], ids[None, :], 0), axis=1)
    outgoing, top = gather_tiles(order, own_factor, parent_front)
    outgoing = outgoing.reshape(ROWS, 2, TILE, TILE)
    tiles = lax.all_to_all(outgoing, "row", split_axis=0, concat_axis=0, tiled=True)

    row_blocks = 2 * here_row + jnp.arange(2, dtype=jnp.int32)
    row_places = (
        jnp.sum(
            jnp.where(
                block_of[:, None, :] == row_blocks[None, :, None], parent_index[:, None, :], 0
            ),
            axis=2,
        )
        - here_row * RT
    )
    col_places = (
        jnp.sum(jnp.where(block_of == here_col, parent_index, 0), axis=1) - here_col * PCT
    )

    top, row_places, col_places = lax.optimization_barrier(
        (top, row_places.astype(jnp.int32), col_places.astype(jnp.int32))
    )
    pan, upper, side, full, low = spread_panel(top)
    panel_out, schur = finish(
        row_places,
        col_places,
        parent_front,
        pan,
        top,
        upper,
        side,
        full,
        low,
        tiles,
    )
    return (panel_out, schur)


def solution(mesh):
    placed = (P("row", "col"), P("row", "col", None), P("row", None, None), P())
    return jax.shard_map(
        per_device,
        mesh=mesh,
        in_specs=placed,
        out_specs=(P("row", None), P("row", "col")),
        check_vma=False,
    )
```

```python
import jax
import jax.numpy as jnp
from jax import lax
from jax.experimental import pallas as pl
from jax.experimental.pallas import tpu as pltpu
from jax.sharding import PartitionSpec as P

TILE = 256
CW = 512
PCT = 4
NSP = 2
ROWS = 8
COLS = 16
SIDE = 4
RT = 8
LEAD = NSP * TILE
PANEL_ROWS = RT * TILE
COL_WIDTH = PCT * TILE
SLICE = LEAD // COLS
TOP_PIECES = 8
MESH = pl.DeviceIdType.MESH
F32 = jnp.float32
BF16 = jnp.bfloat16


def product(matrix_a, matrix_b):
    return jnp.dot(
        matrix_a, matrix_b, precision=lax.Precision.HIGHEST, preferred_element_type=F32
    )


def product_rows(matrix_a, matrix_b):
    return lax.dot_general(
        matrix_a,
        matrix_b,
        (((1,), (1,)), ((), ())),
        precision=lax.Precision.HIGHEST,
        preferred_element_type=F32,
    )


def halves(value):
    high = value.astype(BF16)
    low = (value - high.astype(F32)).astype(BF16)
    return high, low


def three_pass(pair_a, pair_b, contract):
    def one(left, right):
        return lax.dot_general(left, right, (contract, ((), ())), preferred_element_type=F32)

    return one(pair_a[0], pair_b[0]) + (one(pair_a[0], pair_b[1]) + one(pair_a[1], pair_b[0]))


def wrap(value):
    return lax.rem(value + 2 * SIDE, SIDE)


class Wires:
    def __init__(self, send_sem, recv_sem):
        self.row = lax.axis_index("row")
        self.col = lax.axis_index("col")
        self.place_y = self.col // SIDE
        self.place_z = lax.rem(self.col, SIDE)
        self.chip = self.row // 2
        self.core = lax.rem(self.row, 2)
        self.send_sem = send_sem
        self.recv_sem = recv_sem
        self.used = 0
        self.started = []

    def fresh(self, count=1):
        self.used += count
        return self.used - count

    def at(self, step_y, step_z):
        return wrap(self.place_y + step_y) * SIDE + wrap(self.place_z + step_z)

    def remote(self, src, dst, send, recv, to_row, to_col):
        return pltpu.make_async_remote_copy(
            src_ref=src,
            dst_ref=dst,
            send_sem=self.send_sem.at[send],
            recv_sem=self.recv_sem.at[recv],
            device_id=(to_row, to_col),
            device_id_type=MESH,
        )

    def greet(self, devices):
        barrier = pltpu.get_barrier_semaphore()
        for who in devices:
            pl.semaphore_signal(barrier, inc=1, device_id=who, device_id_type=MESH)
        pl.semaphore_wait(barrier, len(devices))

    def col_others(self):
        return [(self.row, lax.rem(self.col + k, COLS)) for k in range(1, COLS)]

    def ring(self, half, piece, own):
        if half == 0:
            place = lambda i, j: self.at(j, i)
        else:
            place = lambda i, j: self.at(i, j)
        sem = {}

        def key(name):
            if name not in sem:
                sem[name] = self.fresh()
            return sem[name]

        pending = {}

        def go(name, i, j, part, to_i, to_j):
            number = key(name)

            def build():
                mine = (i, j) == (0, 0)
                source = own() if mine else piece(place(i, j), half, part)
                target = piece(place(i, j), half, part)
                return self.remote(source, target, number, number, self.row, place(to_i, to_j))

            build().start()
            pending[name] = build
            self.started.append(build)

        def arrived(name):
            pending[name]().wait_recv()

        def quarter(d):
            return 1 if d == 1 else 2

        def first():
            for d in (1, -1):
                go(("a", d), 0, 0, 0, d, 0)

        def second():
            for e in (1, -1):
                go(("b", 0, e), 0, 0, 0, 0, e)

        def near(d):
            arrived(("a", d))
            go(("af", d), -d, 0, quarter(d), d, 0)
            for e in (1, -1):
                go(("b", -d, e), -d, 0, 0, 0, e)

        def far():
            arrived(("af", 1))
            arrived(("af", -1))
            for e in (1, -1):
                go(("b", 2, e), 2, 0, 0, 0, e)

        def cross(i):
            for e in (1, -1):
                arrived(("b", i, e))
                go(("bf", i, e), i, -e, quarter(e), 0, e)

        def last(i):
            for e in (1, -1):
                arrived(("bf", i, e))

        return first, second, near, far, cross, last

    def drain(self):
        for build in self.started:
            build().wait_send()


def ring_steps(rings):
    def each(index, *args):
        return [lambda r=r: r[index](*args) for r in rings]

    steps = each(0) + each(1) + each(2, 1) + each(2, -1) + each(4, 0) + each(3)
    for i in (1, -1, 2):
        steps += each(4, i)
    for i in (0, 1, -1, 2):
        steps += each(5, i)
    return steps


def gather_kernel(
    order_ref, own_ref, front_ref, tiles_ref, top_ref, piece_ref, lead_ref,
    all_ref, high_ref, low_ref, send_sem, recv_sem, local_sem,
):
    wires = Wires(send_sem, recv_sem)
    row, col, chip, core = wires.row, wires.col, wires.chip, wires.core
    fresh, remote = wires.fresh, wires.remote
    load_top = pltpu.make_async_copy(front_ref.at[pl.ds(0, LEAD)], top_ref, local_sem.at[0])

    @pl.when(row == 0)
    def _():
        load_top.start()

    keep_own = pltpu.make_async_copy(own_ref, all_ref.at[col], local_sem.at[1])
    keep_own.start()
    wires.greet(
        wires.col_others()
        + [
            (row + 1 - 2 * core, col),
            (lax.rem(row + 2, ROWS), col),
            (lax.rem(row + 6, ROWS), col),
        ]
    )

    def factor_piece(slot, half, part):
        if part == 0:
            return all_ref.at[slot, pl.ds(half * 128, 128)]
        return all_ref.at[slot, pl.ds(half * 128 + 64 * (part - 1), 64)]

    top_size = LEAD // TOP_PIECES
    half_pieces = TOP_PIECES // 2
    top_recv = fresh(TOP_PIECES)
    top_next = fresh(TOP_PIECES)
    top_side = fresh(TOP_PIECES)

    def top_copies(piece, way):
        block = top_ref.at[pl.ds(piece * top_size, top_size)]
        onward = lax.rem(row + (2 if way == 1 else 6), ROWS)
        return (
            remote(block, block, top_next + piece, top_recv + piece, onward, col),
            remote(block, block, top_side + piece, top_recv + piece, row + 1 - 2 * core, col),
        )

    def top_step(number):
        for way in (1, -1):
            depth = chip if way == 1 else lax.rem(SIDE - chip, SIDE)
            count = number - depth - core
            piece = 2 * count + (0 if way == 1 else 1)

            @pl.when((count >= 0) & (count < half_pieces))
            def _(piece=piece, way=way, depth=depth):
                onward, side = top_copies(piece, way)

                @pl.when(row != 0)
                def _():
                    side.wait_recv()

                @pl.when((core == 0) & (depth < SIDE - 1))
                def _():
                    onward.start()

                @pl.when(core == 0)
                def _():
                    side.start()

    def top_drain(number):
        for way in (1, -1):
            depth = chip if way == 1 else lax.rem(SIDE - chip, SIDE)
            onward, side = top_copies(2 * number + (0 if way == 1 else 1), way)

            @pl.when((core == 0) & (depth < SIDE - 1))
            def _():
                onward.wait_send()

            @pl.when(core == 0)
            def _():
                side.wait_send()

    spread = [
        (0, pl.ds(0, LEAD), lead_ref),
        (2 * row, pl.ds(0, COL_WIDTH), piece_ref.at[0]),
        (2 * row + 1, pl.ds(0, COL_WIDTH), piece_ref.at[1]),
    ]
    spread_recv = fresh(len(spread))
    spread_send = fresh(len(spread) * COLS)

    def spread_copy(index, step):
        _, lanes, target = spread[index]
        to_col = lax.rem(col + step, COLS)
        return remote(
            top_ref.at[pl.ds(to_col * SLICE, SLICE), lanes],
            target,
            spread_send + index * COLS + step,
            spread_recv + index,
            row,
            to_col,
        )

    def spread_start(index):
        holder, lanes, target = spread[index]

        @pl.when(col == holder)
        def _():
            keep = pltpu.make_async_copy(
                top_ref.at[pl.ds(col * SLICE, SLICE), lanes], target, local_sem.at[2 + index]
            )
            keep.start()

            @pl.loop(1, COLS)
            def _(step):
                spread_copy(index, step).start()

            keep.wait()

    def spread_wait(index):
        @pl.when(col != spread[index][0])
        def _():
            spread_copy(index, 1).wait_recv()

    def spread_drain(index):
        @pl.when(col == spread[index][0])
        def _():
            @pl.loop(1, COLS)
            def _(step):
                spread_copy(index, step).wait_send()

    rings = [
        wires.ring(h, factor_piece, lambda h=h: own_ref.at[pl.ds(h * 128, 128)]) for h in range(2)
    ]
    steps = ring_steps(rings)
    for run in steps[:4]:
        run()

    @pl.when(row == 0)
    def _():
        load_top.wait()

    for number in range(half_pieces + SIDE):
        top_step(number)
        for run in steps[4 + 2 * number : 6 + 2 * number]:
            run()
    for run in steps[4 + 2 * (half_pieces + SIDE) :]:
        run()
    for index in range(len(spread)):
        spread_start(index)
    keep_own.wait()
    high_ref[...], low_ref[...] = halves(all_ref[order_ref[COLS]])

    @pl.loop(0, COLS)
    def _(number):
        left = halves(all_ref[order_ref[number]])
        tiles_ref[number] = three_pass(left, (high_ref[...], low_ref[...]), ((1,), (1,)))

    wires.drain()
    for number in range(half_pieces):
        top_drain(number)
    for index in range(len(spread)):
        spread_wait(index)
        spread_drain(index)


BLOCK = 128
GROUP = 8
GROUPS = BLOCK // GROUP
NEAR = slice(0, BLOCK)
AWAY = slice(BLOCK, TILE)


def spread_kernel(
    piece_ref, corner_ref, pan_ref, upper_ref, side_ref, full_ref, low_ref,
    block_ref, inv_ref, work_ref, lead_ref, send_sem, recv_sem, local_sem,
):
    wires = Wires(send_sem, recv_sem)
    row, col = wires.row, wires.col
    mine = pl.ds(col * SLICE, SLICE)
    keeps = [
        pltpu.make_async_copy(corner_ref, lead_ref.at[mine], local_sem.at[0]),
        pltpu.make_async_copy(piece_ref.at[0], pan_ref.at[0, mine], local_sem.at[1]),
        pltpu.make_async_copy(piece_ref.at[1], pan_ref.at[1, mine], local_sem.at[2]),
    ]
    for keep in keeps:
        keep.start()
    wires.greet([(row, wires.at(*step)) for step in ((1, 0), (-1, 0), (0, 1), (0, -1))])

    def panel_piece(slot, half, part):
        if part == 0:
            return pan_ref.at[half, pl.ds(slot * SLICE, SLICE)]
        size = SLICE // 2
        return pan_ref.at[half, pl.ds(slot * SLICE + size * (part - 1), size)]

    def lead_piece(slot, half, part):
        size = SLICE // 2
        if part == 0:
            return lead_ref.at[pl.ds(slot * SLICE + half * size, size)]
        base = slot * SLICE + half * size + (size // 2) * (part - 1)
        return lead_ref.at[pl.ds(base, size // 2)]

    size = SLICE // 2
    lead_steps = ring_steps(
        [
            wires.ring(h, lead_piece, lambda h=h: corner_ref.at[pl.ds(h * size, size)])
            for h in range(2)
        ]
    )
    steps = ring_steps(
        [wires.ring(h, panel_piece, lambda h=h: piece_ref.at[h]) for h in range(2)]
    )
    for run in lead_steps[:-8] + steps[:2] + lead_steps[-8:] + steps[2:4]:
        run()
    for keep in keeps:
        keep.wait()

    def join_inverse(tile):
        first, second, side = inv_ref[2 * tile], inv_ref[2 * tile + 1], side_ref[tile]
        full_ref[tile, NEAR, NEAR] = first
        full_ref[tile, NEAR, AWAY] = jnp.zeros((BLOCK, BLOCK), F32)
        full_ref[tile, AWAY, NEAR] = -product(second, product(side, first))
        full_ref[tile, AWAY, AWAY] = second

    def second_half(tile, below, corner):
        side = product_rows(below, inv_ref[2 * tile])
        side_ref[tile] = side
        block_ref[...] = corner - product_rows(side, side)

    def body(number, carry):
        @pl.when(number == 0)
        def _():
            block_ref[...] = lead_ref[NEAR, NEAR]

        @pl.when(number == 1)
        def _():
            for run in steps[4:8]:
                run()
            second_half(0, lead_ref[AWAY, NEAR], lead_ref[AWAY, AWAY])

        @pl.when(number == 2)
        def _():
            for run in steps[8:12]:
                run()
            join_inverse(0)
            low = product_rows(lead_ref[TILE:, :TILE], full_ref[0])
            low_ref[...] = low
            work_ref[...] = lead_ref[TILE:, TILE:] - product_rows(low, low)
            block_ref[...] = work_ref[NEAR, NEAR]

        @pl.when(number == 3)
        def _():
            for run in steps[12:16]:
                run()
            second_half(1, work_ref[AWAY, NEAR], work_ref[AWAY, AWAY])

        eliminate(block_ref, upper_ref.at[number], inv_ref.at[number])
        return carry

    lax.fori_loop(0, 4, body, 0)
    join_inverse(1)
    for run in steps[16:]:
        run()
    wires.drain()


def gather_tiles(order, own_factor, front):
    anywhere = pl.BlockSpec(memory_space=pl.ANY)
    vmem = pl.BlockSpec(memory_space=pltpu.VMEM)
    return pl.pallas_call(
        gather_kernel,
        out_shape=(
            jax.ShapeDtypeStruct((COLS, TILE, TILE), F32),
            jax.ShapeDtypeStruct((LEAD, COL_WIDTH), F32),
            jax.ShapeDtypeStruct((2, SLICE, COL_WIDTH), F32),
            jax.ShapeDtypeStruct((SLICE, LEAD), F32),
        ),
        in_specs=[pl.BlockSpec(memory_space=pltpu.SMEM), vmem, anywhere],
        out_specs=(vmem,) * 4,
        scratch_shapes=[
            pltpu.VMEM((COLS, TILE, CW), F32),
            pltpu.VMEM((TILE, CW), BF16),
            pltpu.VMEM((TILE, CW), BF16),
            pltpu.SemaphoreType.DMA((120,)),
            pltpu.SemaphoreType.DMA((120,)),
            pltpu.SemaphoreType.DMA((5,)),
        ],
        compiler_params=pltpu.CompilerParams(
            collective_id=0, has_side_effects=True, vmem_limit_bytes=56 * 2**20
        ),
        name="gather",
    )(order, own_factor, front)


def spread_panel(piece, corner):
    vmem = pl.BlockSpec(memory_space=pltpu.VMEM)
    return pl.pallas_call(
        spread_kernel,
        out_shape=(
            jax.ShapeDtypeStruct((2, LEAD, COL_WIDTH), F32),
            jax.ShapeDtypeStruct((4, BLOCK, BLOCK), F32),
            jax.ShapeDtypeStruct((2, BLOCK, BLOCK), F32),
            jax.ShapeDtypeStruct((2, TILE, TILE), F32),
            jax.ShapeDtypeStruct((TILE, TILE), F32),
        ),
        in_specs=[vmem, vmem],
        out_specs=(vmem,) * 5,
        scratch_shapes=[
            pltpu.VMEM((BLOCK, BLOCK), F32),
            pltpu.VMEM((4, BLOCK, BLOCK), F32),
            pltpu.VMEM((TILE, TILE), F32),
            pltpu.VMEM((LEAD, LEAD), F32),
            pltpu.SemaphoreType.DMA((80,)),
            pltpu.SemaphoreType.DMA((80,)),
            pltpu.SemaphoreType.DMA((3,)),
        ],
        compiler_params=pltpu.CompilerParams(
            collective_id=1, has_side_effects=True, vmem_limit_bytes=56 * 2**20
        ),
        cost_estimate=pl.CostEstimate(
            flops=30 * 10**9, bytes_accessed=20 * 2**20, transcendentals=0
        ),
        name="spread",
    )(piece, corner)


def eliminate(block_ref, upper_ref, inverse_ref):
    shape = (GROUP, BLOCK)
    lanes = lax.broadcasted_iota(jnp.int32, shape, 1)
    sublanes = lax.broadcasted_iota(jnp.int32, shape, 0)
    left = [block_ref[GROUP * g : GROUP * (g + 1), :] for g in range(GROUPS)]
    right = [jnp.where(lanes == sublanes + GROUP * g, 1.0, 0.0) for g in range(GROUPS)]
    for g in range(GROUPS):
        base = GROUP * g
        row_l = [jnp.broadcast_to(left[g][s : s + 1, :], shape) for s in range(GROUP)]
        row_r = [jnp.broadcast_to(right[g][s : s + 1, :], shape) for s in range(GROUP)]
        entry = {}
        for s in range(GROUP):
            for t in range(s, GROUP):
                entry[s, t] = jnp.broadcast_to(row_l[s][:, base + t : base + t + 1], shape)
        recip = []
        ratio = {}
        for s in range(GROUP):
            recip.append(1.0 / entry[s, s])
            for t in range(s + 1, GROUP):
                ratio[t, s] = entry[s, t] * recip[s]
            for t in range(s + 1, GROUP):
                for u in range(t, GROUP):
                    entry[t, u] = entry[t, u] - ratio[t, s] * entry[s, u]
        for s in range(GROUP):
            for t in range(s):
                row_l[s] = row_l[s] - ratio[s, t] * row_l[t]
                row_r[s] = row_r[s] - ratio[s, t] * row_r[t]
        new_l, new_r, scale = row_l[0], row_r[0], recip[0]
        for s in range(1, GROUP):
            pick = sublanes == s
            new_l = jnp.where(pick, row_l[s], new_l)
            new_r = jnp.where(pick, row_r[s], new_r)
            scale = jnp.where(pick, recip[s], scale)
        for i in range(g + 1, GROUPS):
            plain = []
            for s in range(GROUP):
                value = jnp.broadcast_to(left[i][:, base + s : base + s + 1], shape)
                for t in range(s):
                    value = value - plain[t] * ratio[s, t]
                plain.append(value)
            for s in range(GROUP):
                scaled = plain[s] * recip[s]
                left[i] = left[i] - scaled * row_l[s]
                right[i] = right[i] - scaled * row_r[s]
        scale = jnp.sqrt(scale)
        upper = jnp.where(lanes >= sublanes + base, new_l * scale, 0.0)
        upper_ref[base : base + GROUP, :] = upper
        inverse_ref[base : base + GROUP, :] = new_r * scale


def final_kernel(
    rows_ref, cols_ref, front_ref, pan_ref, top_ref, upper_ref, side_ref, full_ref, low_ref,
    tiles_ref, panel_ref, out_ref, right_ref, high_ref, small_ref,
):
    row = lax.axis_index("row")
    col = lax.axis_index("col")
    step = pl.program_id(0)
    inverses = [halves(full_ref[t]) for t in range(2)]
    low = halves(low_ref[...])
    blank = jnp.zeros((BLOCK, BLOCK), F32)

    def chunk(block):
        first = three_pass(inverses[0], halves(block[:TILE]), ((1,), (0,)))
        rest = block[TILE:] - three_pass(low, halves(first), ((1,), (0,)))
        return first, three_pass(inverses[1], halves(rest), ((1,), (0,)))

    @pl.when(step == 0)
    def _():
        for part in range(PCT):
            lanes = slice(part * TILE, (part + 1) * TILE)
            right_ref[:TILE, lanes], right_ref[TILE:, lanes] = chunk(top_ref[:, lanes])

        @pl.when(col == 0)
        def _():
            for t in range(2):
                for r, c, value in (
                    (0, 0, upper_ref[2 * t]),
                    (0, 1, side_ref[t].T),
                    (1, 0, blank),
                    (1, 1, upper_ref[2 * t + 1]),
                ):
                    r0, c0 = t * TILE + r * BLOCK, t * TILE + c * BLOCK
                    right_ref[r0 : r0 + BLOCK, c0 : c0 + BLOCK] = value
            right_ref[TILE:, :TILE] = jnp.zeros((TILE, TILE), F32)

        high_ref[...], small_ref[...] = halves(right_ref[...])

    first, second = chunk(pan_ref[0])
    panel_ref[:, :TILE] = first.T
    panel_ref[:, TILE:] = second.T

    for t in range(2):

        @pl.when((row == 0) & (step == t))
        def _(t=t):
            for r, c, value in (
                (0, 0, upper_ref[2 * t].T),
                (0, 1, blank),
                (1, 0, side_ref[t]),
                (1, 1, upper_ref[2 * t + 1].T),
            ):
                r0, c0 = r * BLOCK, t * TILE + c * BLOCK
                panel_ref[r0 : r0 + BLOCK, c0 : c0 + BLOCK] = value
            if t == 0:
                panel_ref[:, TILE:] = jnp.zeros((TILE, TILE), F32)

    left = halves(panel_ref[...])
    for part in range(PCT):
        span = slice(part * TILE, (part + 1) * TILE)
        right = (high_ref[:, span], small_ref[:, span])
        out_ref[:, span] = front_ref[:, span] - three_pass(left, right, ((1,), (0,)))
    block = step // PCT
    for child in range(ROWS):

        @pl.when(rows_ref[child, block] == step)
        def _(child=child):
            start = pl.multiple_of(cols_ref[child] * TILE, TILE)
            out_ref[:, pl.ds(start, TILE)] -= tiles_ref[child, 0]


def finish(row_places, col_places, front, pan, top, upper, side, full, low, tiles):
    return pl.pallas_call(
        final_kernel,
        out_shape=(
            jax.ShapeDtypeStruct((PANEL_ROWS, LEAD), F32),
            jax.ShapeDtypeStruct((PANEL_ROWS, COL_WIDTH), F32),
        ),
        grid_spec=pltpu.PrefetchScalarGridSpec(
            num_scalar_prefetch=2,
            grid=(RT,),
            in_specs=[
                pl.BlockSpec((TILE, COL_WIDTH), lambda i, *_: (i, 0)),
                pl.BlockSpec((1, LEAD, TILE), lambda i, *_: (i // PCT, 0, lax.rem(i, PCT))),
                pl.BlockSpec((LEAD, COL_WIDTH), lambda i, *_: (0, 0)),
                pl.BlockSpec((4, BLOCK, BLOCK), lambda i, *_: (0, 0, 0)),
                pl.BlockSpec((2, BLOCK, BLOCK), lambda i, *_: (0, 0, 0)),
                pl.BlockSpec((2, TILE, TILE), lambda i, *_: (0, 0, 0)),
                pl.BlockSpec((TILE, TILE), lambda i, *_: (0, 0)),
                pl.BlockSpec((ROWS, 1, TILE, TILE), lambda i, *_: (0, i // PCT, 0, 0)),
            ],
            out_specs=(
                pl.BlockSpec((TILE, LEAD), lambda i, *_: (i, 0)),
                pl.BlockSpec((TILE, COL_WIDTH), lambda i, *_: (i, 0)),
            ),
            scratch_shapes=[
                pltpu.VMEM((LEAD, COL_WIDTH), F32),
                pltpu.VMEM((LEAD, COL_WIDTH), BF16),
                pltpu.VMEM((LEAD, COL_WIDTH), BF16),
            ],
        ),
        compiler_params=pltpu.CompilerParams(vmem_limit_bytes=58 * 2**20),
        cost_estimate=pl.CostEstimate(
            flops=9 * PANEL_ROWS * COL_WIDTH * LEAD,
            bytes_accessed=30 * 2**20,
            transcendentals=0,
        ),
        name="finish",
    )(row_places, col_places, front, pan, top, upper, side, full, low, tiles)


def per_device(parent_front, child_panels, child_inverses, parent_index):
    here_row = lax.axis_index("row")
    here_col = lax.axis_index("col")
    own_factor = product_rows(child_panels[0], child_inverses[0])
    block_of = parent_index // PCT
    my_blocks = lax.dynamic_index_in_dim(block_of, here_row, 0, keepdims=False)
    ids = jnp.arange(COLS, dtype=jnp.int32)
    wanted = jnp.concatenate([ids, here_col[None].astype(jnp.int32)])
    order = jnp.sum(jnp.where(my_blocks[None, :] == wanted[:, None], ids[None, :], 0), axis=1)
    outgoing, top, piece, corner = gather_tiles(order, own_factor, parent_front)
    outgoing = outgoing.reshape(ROWS, 2, TILE, TILE)
    tiles = lax.all_to_all(outgoing, "row", split_axis=0, concat_axis=0, tiled=True)

    row_blocks = 2 * here_row + jnp.arange(2, dtype=jnp.int32)
    row_places = (
        jnp.sum(
            jnp.where(
                block_of[:, None, :] == row_blocks[None, :, None], parent_index[:, None, :], 0
            ),
            axis=2,
        )
        - here_row * RT
    )
    col_places = (
        jnp.sum(jnp.where(block_of == here_col, parent_index, 0), axis=1) - here_col * PCT
    )

    piece, corner, row_places, col_places = lax.optimization_barrier(
        (piece, corner, row_places.astype(jnp.int32), col_places.astype(jnp.int32))
    )
    pan, upper, side, full, low = spread_panel(piece, corner)
    panel_out, schur = finish(
        row_places,
        col_places,
        parent_front,
        pan,
        top,
        upper,
        side,
        full,
        low,
        tiles,
    )
    return (panel_out, schur)


def solution(mesh):
    placed = (P("row", "col"), P("row", "col", None), P("row", None, None), P())
    return jax.shard_map(
        per_device,
        mesh=mesh,
        in_specs=placed,
        out_specs=(P("row", None), P("row", "col")),
        check_vma=False,
    )
```

```python
import jax
import jax.numpy as jnp
from jax import lax
from jax.experimental import pallas as pl
from jax.experimental.pallas import tpu as pltpu
from jax.sharding import PartitionSpec as P

TILE = 256
CW = 512
PCT = 4
NSP = 2
ROWS = 8
COLS = 16
SIDE = 4
RT = 8
LEAD = NSP * TILE
PANEL_ROWS = RT * TILE
COL_WIDTH = PCT * TILE
SLICE = LEAD // COLS
TOP_PIECES = 8
MESH = pl.DeviceIdType.MESH
F32 = jnp.float32
BF16 = jnp.bfloat16


def product(matrix_a, matrix_b):
    return jnp.dot(
        matrix_a, matrix_b, precision=lax.Precision.HIGHEST, preferred_element_type=F32
    )


def product_rows(matrix_a, matrix_b):
    return lax.dot_general(
        matrix_a,
        matrix_b,
        (((1,), (1,)), ((), ())),
        precision=lax.Precision.HIGHEST,
        preferred_element_type=F32,
    )


def halves(value):
    high = value.astype(BF16)
    low = (value - high.astype(F32)).astype(BF16)
    return high, low


def three_pass(pair_a, pair_b, contract):
    def one(left, right):
        return lax.dot_general(left, right, (contract, ((), ())), preferred_element_type=F32)

    return one(pair_a[0], pair_b[0]) + (one(pair_a[0], pair_b[1]) + one(pair_a[1], pair_b[0]))


def wrap(value):
    return lax.rem(value + 2 * SIDE, SIDE)


class Wires:
    def __init__(self, send_sem, recv_sem):
        self.row = lax.axis_index("row")
        self.col = lax.axis_index("col")
        self.place_y = self.col // SIDE
        self.place_z = lax.rem(self.col, SIDE)
        self.chip = self.row // 2
        self.core = lax.rem(self.row, 2)
        self.send_sem = send_sem
        self.recv_sem = recv_sem
        self.used = 0
        self.started = []

    def fresh(self, count=1):
        self.used += count
        return self.used - count

    def at(self, step_y, step_z):
        return wrap(self.place_y + step_y) * SIDE + wrap(self.place_z + step_z)

    def remote(self, src, dst, send, recv, to_row, to_col):
        return pltpu.make_async_remote_copy(
            src_ref=src,
            dst_ref=dst,
            send_sem=self.send_sem.at[send],
            recv_sem=self.recv_sem.at[recv],
            device_id=(to_row, to_col),
            device_id_type=MESH,
        )

    def greet(self, devices):
        barrier = pltpu.get_barrier_semaphore()
        for who in devices:
            pl.semaphore_signal(barrier, inc=1, device_id=who, device_id_type=MESH)
        pl.semaphore_wait(barrier, len(devices))

    def col_others(self):
        return [(self.row, lax.rem(self.col + k, COLS)) for k in range(1, COLS)]

    def ring(self, half, piece, own):
        if half == 0:
            place = lambda i, j: self.at(j, i)
        else:
            place = lambda i, j: self.at(i, j)
        sem = {}

        def key(name):
            if name not in sem:
                sem[name] = self.fresh()
            return sem[name]

        pending = {}

        def go(name, i, j, part, to_i, to_j):
            number = key(name)

            def build():
                mine = (i, j) == (0, 0)
                source = own() if mine else piece(place(i, j), half, part)
                target = piece(place(i, j), half, part)
                return self.remote(source, target, number, number, self.row, place(to_i, to_j))

            build().start()
            pending[name] = build
            self.started.append(build)

        def arrived(name):
            pending[name]().wait_recv()

        def quarter(d):
            return 1 if d == 1 else 2

        def first():
            for d in (1, -1):
                go(("a", d), 0, 0, 0, d, 0)

        def second():
            for e in (1, -1):
                go(("b", 0, e), 0, 0, 0, 0, e)

        def near(d):
            arrived(("a", d))
            go(("af", d), -d, 0, quarter(d), d, 0)
            for e in (1, -1):
                go(("b", -d, e), -d, 0, 0, 0, e)

        def far():
            arrived(("af", 1))
            arrived(("af", -1))
            for e in (1, -1):
                go(("b", 2, e), 2, 0, 0, 0, e)

        def cross(i):
            for e in (1, -1):
                arrived(("b", i, e))
                go(("bf", i, e), i, -e, quarter(e), 0, e)

        def last(i):
            for e in (1, -1):
                arrived(("bf", i, e))

        return first, second, near, far, cross, last

    def drain(self):
        for build in self.started:
            build().wait_send()


def ring_steps(rings):
    def each(index, *args):
        return [lambda r=r: r[index](*args) for r in rings]

    steps = each(0) + each(1) + each(2, 1) + each(2, -1) + each(4, 0) + each(3)
    for i in (1, -1, 2):
        steps += each(4, i)
    for i in (0, 1, -1, 2):
        steps += each(5, i)
    return steps


def gather_kernel(
    order_ref, own_ref, front_ref, tiles_ref, top_ref, lead_ref,
    all_ref, high_ref, low_ref, corner_ref, send_sem, recv_sem, local_sem,
):
    wires = Wires(send_sem, recv_sem)
    row, col, chip, core = wires.row, wires.col, wires.chip, wires.core
    fresh, remote = wires.fresh, wires.remote
    load_top = pltpu.make_async_copy(front_ref.at[pl.ds(0, LEAD)], top_ref, local_sem.at[0])

    @pl.when(row == 0)
    def _():
        load_top.start()

    keep_own = pltpu.make_async_copy(own_ref, all_ref.at[col], local_sem.at[1])
    keep_own.start()
    wires.greet(
        wires.col_others()
        + [
            (lax.rem(row + k, ROWS), col) for k in range(1, ROWS)
        ]
    )

    def factor_piece(slot, half, part):
        if part == 0:
            return all_ref.at[slot, pl.ds(half * 128, 128)]
        return all_ref.at[slot, pl.ds(half * 128 + 64 * (part - 1), 64)]

    top_size = LEAD // TOP_PIECES
    half_pieces = TOP_PIECES // 2
    top_recv = fresh(TOP_PIECES)
    top_next = fresh(TOP_PIECES)
    top_side = fresh(TOP_PIECES)

    def top_copies(piece, way):
        block = top_ref.at[pl.ds(piece * top_size, top_size)]
        onward = lax.rem(row + (2 if way == 1 else 6), ROWS)
        return (
            remote(block, block, top_next + piece, top_recv + piece, onward, col),
            remote(block, block, top_side + piece, top_recv + piece, row + 1 - 2 * core, col),
        )

    def top_step(number):
        for way in (1, -1):
            depth = chip if way == 1 else lax.rem(SIDE - chip, SIDE)
            count = number - depth - core
            piece = 2 * count + (0 if way == 1 else 1)

            @pl.when((count >= 0) & (count < half_pieces))
            def _(piece=piece, way=way, depth=depth):
                onward, side = top_copies(piece, way)

                @pl.when(row != 0)
                def _():
                    side.wait_recv()

                @pl.when((core == 0) & (depth < SIDE - 1))
                def _():
                    onward.start()

                @pl.when(core == 0)
                def _():
                    side.start()

    def top_drain(number):
        for way in (1, -1):
            depth = chip if way == 1 else lax.rem(SIDE - chip, SIDE)
            onward, side = top_copies(2 * number + (0 if way == 1 else 1), way)

            @pl.when((core == 0) & (depth < SIDE - 1))
            def _():
                onward.wait_send()

            @pl.when(core == 0)
            def _():
                side.wait_send()

    corner_recv = fresh()
    along = fresh(COLS)
    down = fresh(ROWS)
    load_corner = pltpu.make_async_copy(
        front_ref.at[pl.ds(0, SLICE), pl.ds(0, LEAD)], corner_ref, local_sem.at[2]
    )

    def along_copy(step):
        return remote(
            front_ref.at[pl.ds(step * SLICE, SLICE), pl.ds(0, LEAD)],
            corner_ref,
            along + step,
            corner_recv,
            row,
            step,
        )

    def down_copy(step):
        return remote(corner_ref, corner_ref, down + step, corner_recv, step, col)

    def each_along(act):
        @pl.when((row == 0) & (col == 0))
        def _():
            @pl.loop(1, COLS)
            def _(step):
                act(along_copy(step))

    def each_down(act):
        @pl.when(row == 0)
        def _():
            @pl.loop(1, ROWS)
            def _(step):
                act(down_copy(step))

    def corner_start():
        each_along(lambda copy: copy.start())

        @pl.when((row == 0) & (col == 0))
        def _():
            load_corner.start()

    def corner_pass():
        @pl.when((row == 0) & (col == 0))
        def _():
            load_corner.wait()

        @pl.when((row == 0) & (col != 0))
        def _():
            down_copy(1).wait_recv()

        each_down(lambda copy: copy.start())

    def corner_wait():
        @pl.when(row != 0)
        def _():
            down_copy(1).wait_recv()

    def lead_piece(slot, half, part):
        size = SLICE // 2
        if part == 0:
            return lead_ref.at[pl.ds(slot * SLICE + half * size, size)]
        base = slot * SLICE + half * size + (size // 2) * (part - 1)
        return lead_ref.at[pl.ds(base, size // 2)]

    rings = [
        wires.ring(h, factor_piece, lambda h=h: own_ref.at[pl.ds(h * 128, 128)]) for h in range(2)
    ]
    size = SLICE // 2
    lead_rings = [
        wires.ring(h, lead_piece, lambda h=h: corner_ref.at[pl.ds(h * size, size)])
        for h in range(2)
    ]
    steps = ring_steps(rings)
    corner_start()
    for run in steps[:4]:
        run()

    @pl.when(row == 0)
    def _():
        load_top.wait()

    for number in range(half_pieces + SIDE):
        top_step(number)
        if number == 2:
            corner_pass()
        for run in steps[4 + 2 * number : 6 + 2 * number]:
            run()
    for run in steps[4 + 2 * (half_pieces + SIDE) :]:
        run()
    corner_wait()
    keep_corner = pltpu.make_async_copy(
        corner_ref, lead_ref.at[pl.ds(col * SLICE, SLICE)], local_sem.at[3]
    )
    keep_corner.start()
    keep_own.wait()
    lead_steps = ring_steps(lead_rings)
    for run in lead_steps[:4]:
        run()
    high_ref[...], low_ref[...] = halves(all_ref[order_ref[COLS]])

    def tile(number):
        left = halves(all_ref[order_ref[number]])
        tiles_ref[number] = three_pass(left, (high_ref[...], low_ref[...]), ((1,), (1,)))

    for part in range(COLS // 2):
        pl.loop(2 * part, 2 * part + 2)(tile)
        for run in lead_steps[4 + 4 * part : 8 + 4 * part]:
            run()
    keep_corner.wait()
    wires.drain()
    for number in range(half_pieces):
        top_drain(number)
    each_along(lambda copy: copy.wait_send())
    each_down(lambda copy: copy.wait_send())


BLOCK = 128
GROUP = 8
GROUPS = BLOCK // GROUP
NEAR = slice(0, BLOCK)
AWAY = slice(BLOCK, TILE)


def spread_kernel(
    top_ref, lead_ref, pan_ref, upper_ref, side_ref, full_ref, low_ref,
    block_ref, inv_ref, work_ref, send_sem, recv_sem, local_sem,
):
    wires = Wires(send_sem, recv_sem)
    row, col = wires.row, wires.col
    fresh, remote = wires.fresh, wires.remote
    wires.greet(wires.col_others())

    def panel_piece(slot, half, part):
        if part == 0:
            return pan_ref.at[half, pl.ds(slot * SLICE, SLICE)]
        size = SLICE // 2
        return pan_ref.at[half, pl.ds(slot * SLICE + size * (part - 1), size)]

    spread = []
    for half in range(2):
        spread.append((half, 2 * row + half, pl.ds(0, COL_WIDTH), pl.ds(0, COL_WIDTH)))
    spread_recv = [fresh() for _ in spread]
    spread_send = [fresh(COLS) for _ in spread]

    def spread_copy(index, step):
        half, _, lanes, to_lanes = spread[index]
        to_col = lax.rem(col + step, COLS)
        rows = pl.ds(to_col * SLICE, SLICE)
        return remote(
            top_ref.at[rows, lanes],
            pan_ref.at[half, rows, to_lanes],
            spread_send[index] + step,
            spread_recv[index],
            row,
            to_col,
        )

    def spread_start(index):
        half, holder, lanes, to_lanes = spread[index]
        rows = pl.ds(col * SLICE, SLICE)

        @pl.when(col == holder)
        def _():
            keep = pltpu.make_async_copy(
                top_ref.at[rows, lanes], pan_ref.at[half, rows, to_lanes], local_sem.at[index]
            )
            keep.start()

            @pl.loop(1, COLS)
            def _(step):
                spread_copy(index, step).start()

            keep.wait()

    def spread_wait(index):
        @pl.when(col != spread[index][1])
        def _():
            spread_copy(index, 1).wait_recv()

    def spread_drain(index):
        @pl.when(col == spread[index][1])
        def _():
            @pl.loop(1, COLS)
            def _(step):
                spread_copy(index, step).wait_send()

    for index in range(2):
        spread_start(index)
    steps = ring_steps(
        [wires.ring(h, panel_piece, lambda h=h: panel_piece(col, h, 0)) for h in range(2)]
    )

    def join_inverse(tile):
        first, second, side = inv_ref[2 * tile], inv_ref[2 * tile + 1], side_ref[tile]
        full_ref[tile, NEAR, NEAR] = first
        full_ref[tile, NEAR, AWAY] = jnp.zeros((BLOCK, BLOCK), F32)
        full_ref[tile, AWAY, NEAR] = -product(second, product(side, first))
        full_ref[tile, AWAY, AWAY] = second

    def second_half(tile, below, corner):
        side = product_rows(below, inv_ref[2 * tile])
        side_ref[tile] = side
        block_ref[...] = corner - product_rows(side, side)

    def body(number, carry):
        @pl.when(number == 0)
        def _():
            block_ref[...] = lead_ref[NEAR, NEAR]

        @pl.when(number == 1)
        def _():
            second_half(0, lead_ref[AWAY, NEAR], lead_ref[AWAY, AWAY])

        @pl.when(number == 2)
        def _():
            for index in range(2):
                spread_wait(index)
            for run in steps[:4]:
                run()
            join_inverse(0)
            low = product_rows(lead_ref[TILE:, :TILE], full_ref[0])
            low_ref[...] = low
            work_ref[...] = lead_ref[TILE:, TILE:] - product_rows(low, low)
            block_ref[...] = work_ref[NEAR, NEAR]

        @pl.when(number == 3)
        def _():
            for run in steps[4:8]:
                run()
            second_half(1, work_ref[AWAY, NEAR], work_ref[AWAY, AWAY])

        eliminate(block_ref, upper_ref.at[number], inv_ref.at[number])
        return carry

    lax.fori_loop(0, 4, body, 0)
    for run in steps[8:12]:
        run()
    join_inverse(1)
    for run in steps[12:]:
        run()
    wires.drain()
    for index in range(2):
        spread_drain(index)


def gather_tiles(order, own_factor, front):
    anywhere = pl.BlockSpec(memory_space=pl.ANY)
    vmem = pl.BlockSpec(memory_space=pltpu.VMEM)
    return pl.pallas_call(
        gather_kernel,
        out_shape=(
            jax.ShapeDtypeStruct((COLS, TILE, TILE), F32),
            jax.ShapeDtypeStruct((LEAD, COL_WIDTH), F32),
            jax.ShapeDtypeStruct((LEAD, LEAD), F32),
        ),
        in_specs=[pl.BlockSpec(memory_space=pltpu.SMEM), vmem, anywhere],
        out_specs=(vmem,) * 3,
        scratch_shapes=[
            pltpu.VMEM((COLS, TILE, CW), F32),
            pltpu.VMEM((TILE, CW), BF16),
            pltpu.VMEM((TILE, CW), BF16),
            pltpu.VMEM((SLICE, LEAD), F32),
            pltpu.SemaphoreType.DMA((136,)),
            pltpu.SemaphoreType.DMA((136,)),
            pltpu.SemaphoreType.DMA((4,)),
        ],
        compiler_params=pltpu.CompilerParams(
            collective_id=0, has_side_effects=True, vmem_limit_bytes=56 * 2**20
        ),
        name="gather",
    )(order, own_factor, front)


def spread_panel(top, lead):
    vmem = pl.BlockSpec(memory_space=pltpu.VMEM)
    return pl.pallas_call(
        spread_kernel,
        out_shape=(
            jax.ShapeDtypeStruct((2, LEAD, COL_WIDTH), F32),
            jax.ShapeDtypeStruct((4, BLOCK, BLOCK), F32),
            jax.ShapeDtypeStruct((2, BLOCK, BLOCK), F32),
            jax.ShapeDtypeStruct((2, TILE, TILE), F32),
            jax.ShapeDtypeStruct((TILE, TILE), F32),
        ),
        in_specs=[vmem, vmem],
        out_specs=(vmem,) * 5,
        scratch_shapes=[
            pltpu.VMEM((BLOCK, BLOCK), F32),
            pltpu.VMEM((4, BLOCK, BLOCK), F32),
            pltpu.VMEM((TILE, TILE), F32),
            pltpu.SemaphoreType.DMA((80,)),
            pltpu.SemaphoreType.DMA((80,)),
            pltpu.SemaphoreType.DMA((3,)),
        ],
        compiler_params=pltpu.CompilerParams(
            collective_id=1, has_side_effects=True, vmem_limit_bytes=56 * 2**20
        ),
        cost_estimate=pl.CostEstimate(
            flops=30 * 10**9, bytes_accessed=20 * 2**20, transcendentals=0
        ),
        name="spread",
    )(top, lead)


def eliminate(block_ref, upper_ref, inverse_ref):
    shape = (GROUP, BLOCK)
    lanes = lax.broadcasted_iota(jnp.int32, shape, 1)
    sublanes = lax.broadcasted_iota(jnp.int32, shape, 0)
    left = [block_ref[GROUP * g : GROUP * (g + 1), :] for g in range(GROUPS)]
    right = [jnp.where(lanes == sublanes + GROUP * g, 1.0, 0.0) for g in range(GROUPS)]
    for g in range(GROUPS):
        base = GROUP * g
        row_l = [jnp.broadcast_to(left[g][s : s + 1, :], shape) for s in range(GROUP)]
        row_r = [jnp.broadcast_to(right[g][s : s + 1, :], shape) for s in range(GROUP)]
        entry = {}
        for s in range(GROUP):
            for t in range(s, GROUP):
                entry[s, t] = jnp.broadcast_to(row_l[s][:, base + t : base + t + 1], shape)
        recip = []
        ratio = {}
        for s in range(GROUP):
            recip.append(1.0 / entry[s, s])
            for t in range(s + 1, GROUP):
                ratio[t, s] = entry[s, t] * recip[s]
            for t in range(s + 1, GROUP):
                for u in range(t, GROUP):
                    entry[t, u] = entry[t, u] - ratio[t, s] * entry[s, u]
        for s in range(GROUP):
            for t in range(s):
                row_l[s] = row_l[s] - ratio[s, t] * row_l[t]
                row_r[s] = row_r[s] - ratio[s, t] * row_r[t]
        new_l, new_r, scale = row_l[0], row_r[0], recip[0]
        for s in range(1, GROUP):
            pick = sublanes == s
            new_l = jnp.where(pick, row_l[s], new_l)
            new_r = jnp.where(pick, row_r[s], new_r)
            scale = jnp.where(pick, recip[s], scale)
        for i in range(g + 1, GROUPS):
            plain = []
            for s in range(GROUP):
                value = jnp.broadcast_to(left[i][:, base + s : base + s + 1], shape)
                for t in range(s):
                    value = value - plain[t] * ratio[s, t]
                plain.append(value)
            for s in range(GROUP):
                scaled = plain[s] * recip[s]
                left[i] = left[i] - scaled * row_l[s]
                right[i] = right[i] - scaled * row_r[s]
        scale = jnp.sqrt(scale)
        upper = jnp.where(lanes >= sublanes + base, new_l * scale, 0.0)
        upper_ref[base : base + GROUP, :] = upper
        inverse_ref[base : base + GROUP, :] = new_r * scale


def final_kernel(
    rows_ref, cols_ref, front_ref, pan_ref, top_ref, upper_ref, side_ref, full_ref, low_ref,
    tiles_ref, panel_ref, out_ref, right_ref, high_ref, small_ref,
):
    row = lax.axis_index("row")
    col = lax.axis_index("col")
    step = pl.program_id(0)
    inverses = [halves(full_ref[t]) for t in range(2)]
    low = halves(low_ref[...])
    blank = jnp.zeros((BLOCK, BLOCK), F32)

    def chunk(block):
        first = three_pass(inverses[0], halves(block[:TILE]), ((1,), (0,)))
        rest = block[TILE:] - three_pass(low, halves(first), ((1,), (0,)))
        return first, three_pass(inverses[1], halves(rest), ((1,), (0,)))

    @pl.when(step == 0)
    def _():
        for part in range(PCT):
            lanes = slice(part * TILE, (part + 1) * TILE)
            right_ref[:TILE, lanes], right_ref[TILE:, lanes] = chunk(top_ref[:, lanes])

        @pl.when(col == 0)
        def _():
            for t in range(2):
                for r, c, value in (
                    (0, 0, upper_ref[2 * t]),
                    (0, 1, side_ref[t].T),
                    (1, 0, blank),
                    (1, 1, upper_ref[2 * t + 1]),
                ):
                    r0, c0 = t * TILE + r * BLOCK, t * TILE + c * BLOCK
                    right_ref[r0 : r0 + BLOCK, c0 : c0 + BLOCK] = value
            right_ref[TILE:, :TILE] = jnp.zeros((TILE, TILE), F32)

        high_ref[...], small_ref[...] = halves(right_ref[...])

    first, second = chunk(pan_ref[0])
    panel_ref[:, :TILE] = first.T
    panel_ref[:, TILE:] = second.T

    for t in range(2):

        @pl.when((row == 0) & (step == t))
        def _(t=t):
            for r, c, value in (
                (0, 0, upper_ref[2 * t].T),
                (0, 1, blank),
                (1, 0, side_ref[t]),
                (1, 1, upper_ref[2 * t + 1].T),
            ):
                r0, c0 = r * BLOCK, t * TILE + c * BLOCK
                panel_ref[r0 : r0 + BLOCK, c0 : c0 + BLOCK] = value
            if t == 0:
                panel_ref[:, TILE:] = jnp.zeros((TILE, TILE), F32)

    left = halves(panel_ref[...])
    for part in range(PCT):
        span = slice(part * TILE, (part + 1) * TILE)
        right = (high_ref[:, span], small_ref[:, span])
        out_ref[:, span] = front_ref[:, span] - three_pass(left, right, ((1,), (0,)))
    block = step // PCT
    for child in range(ROWS):

        @pl.when(rows_ref[child, block] == step)
        def _(child=child):
            start = pl.multiple_of(cols_ref[child] * TILE, TILE)
            out_ref[:, pl.ds(start, TILE)] -= tiles_ref[child, 0]


def finish(row_places, col_places, front, pan, top, upper, side, full, low, tiles):
    return pl.pallas_call(
        final_kernel,
        out_shape=(
            jax.ShapeDtypeStruct((PANEL_ROWS, LEAD), F32),
            jax.ShapeDtypeStruct((PANEL_ROWS, COL_WIDTH), F32),
        ),
        grid_spec=pltpu.PrefetchScalarGridSpec(
            num_scalar_prefetch=2,
            grid=(RT,),
            in_specs=[
                pl.BlockSpec((TILE, COL_WIDTH), lambda i, *_: (i, 0)),
                pl.BlockSpec((1, LEAD, TILE), lambda i, *_: (i // PCT, 0, lax.rem(i, PCT))),
                pl.BlockSpec((LEAD, COL_WIDTH), lambda i, *_: (0, 0)),
                pl.BlockSpec((4, BLOCK, BLOCK), lambda i, *_: (0, 0, 0)),
                pl.BlockSpec((2, BLOCK, BLOCK), lambda i, *_: (0, 0, 0)),
                pl.BlockSpec((2, TILE, TILE), lambda i, *_: (0, 0, 0)),
                pl.BlockSpec((TILE, TILE), lambda i, *_: (0, 0)),
                pl.BlockSpec((ROWS, 1, TILE, TILE), lambda i, *_: (0, i // PCT, 0, 0)),
            ],
            out_specs=(
                pl.BlockSpec((TILE, LEAD), lambda i, *_: (i, 0)),
                pl.BlockSpec((TILE, COL_WIDTH), lambda i, *_: (i, 0)),
            ),
            scratch_shapes=[
                pltpu.VMEM((LEAD, COL_WIDTH), F32),
                pltpu.VMEM((LEAD, COL_WIDTH), BF16),
                pltpu.VMEM((LEAD, COL_WIDTH), BF16),
            ],
        ),
        compiler_params=pltpu.CompilerParams(vmem_limit_bytes=58 * 2**20),
        cost_estimate=pl.CostEstimate(
            flops=9 * PANEL_ROWS * COL_WIDTH * LEAD,
            bytes_accessed=30 * 2**20,
            transcendentals=0,
        ),
        name="finish",
    )(row_places, col_places, front, pan, top, upper, side, full, low, tiles)


def per_device(parent_front, child_panels, child_inverses, parent_index):
    here_row = lax.axis_index("row")
    here_col = lax.axis_index("col")
    own_factor = product_rows(child_panels[0], child_inverses[0])
    block_of = parent_index // PCT
    my_blocks = lax.dynamic_index_in_dim(block_of, here_row, 0, keepdims=False)
    ids = jnp.arange(COLS, dtype=jnp.int32)
    wanted = jnp.concatenate([ids, here_col[None].astype(jnp.int32)])
    order = jnp.sum(jnp.where(my_blocks[None, :] == wanted[:, None], ids[None, :], 0), axis=1)
    outgoing, top, lead = gather_tiles(order, own_factor, parent_front)
    outgoing = outgoing.reshape(ROWS, 2, TILE, TILE)
    tiles = lax.all_to_all(outgoing, "row", split_axis=0, concat_axis=0, tiled=True)

    row_blocks = 2 * here_row + jnp.arange(2, dtype=jnp.int32)
    row_places = (
        jnp.sum(
            jnp.where(
                block_of[:, None, :] == row_blocks[None, :, None], parent_index[:, None, :], 0
            ),
            axis=2,
        )
        - here_row * RT
    )
    col_places = (
        jnp.sum(jnp.where(block_of == here_col, parent_index, 0), axis=1) - here_col * PCT
    )

    top, lead, row_places, col_places = lax.optimization_barrier(
        (top, lead, row_places.astype(jnp.int32), col_places.astype(jnp.int32))
    )
    pan, upper, side, full, low = spread_panel(top, lead)
    panel_out, schur = finish(
        row_places,
        col_places,
        parent_front,
        pan,
        top,
        upper,
        side,
        full,
        low,
        tiles,
    )
    return (panel_out, schur)


def solution(mesh):
    placed = (P("row", "col"), P("row", "col", None), P("row", None, None), P())
    return jax.shard_map(
        per_device,
        mesh=mesh,
        in_specs=placed,
        out_specs=(P("row", None), P("row", "col")),
        check_vma=False,
    )
```

```python
import jax
import jax.numpy as jnp
from jax import lax
from jax.experimental import pallas as pl
from jax.experimental.pallas import tpu as pltpu
from jax.sharding import PartitionSpec as P

TILE = 256
CW = 512
PCT = 4
NSP = 2
ROWS = 8
COLS = 16
SIDE = 4
RT = 8
LEAD = NSP * TILE
PANEL_ROWS = RT * TILE
COL_WIDTH = PCT * TILE
SLICE = LEAD // COLS
TOP_PIECES = 8
MESH = pl.DeviceIdType.MESH
F32 = jnp.float32
BF16 = jnp.bfloat16


def product(matrix_a, matrix_b):
    return jnp.dot(
        matrix_a, matrix_b, precision=lax.Precision.HIGHEST, preferred_element_type=F32
    )


def product_rows(matrix_a, matrix_b):
    return lax.dot_general(
        matrix_a,
        matrix_b,
        (((1,), (1,)), ((), ())),
        precision=lax.Precision.HIGHEST,
        preferred_element_type=F32,
    )


def halves(value):
    high = value.astype(BF16)
    low = (value - high.astype(F32)).astype(BF16)
    return high, low


def three_pass(pair_a, pair_b, contract):
    def one(left, right):
        return lax.dot_general(left, right, (contract, ((), ())), preferred_element_type=F32)

    return one(pair_a[0], pair_b[0]) + (one(pair_a[0], pair_b[1]) + one(pair_a[1], pair_b[0]))


def wrap(value):
    return lax.rem(value + 2 * SIDE, SIDE)


class Wires:
    def __init__(self, send_sem, recv_sem):
        self.row = lax.axis_index("row")
        self.col = lax.axis_index("col")
        self.place_y = self.col // SIDE
        self.place_z = lax.rem(self.col, SIDE)
        self.chip = self.row // 2
        self.core = lax.rem(self.row, 2)
        self.send_sem = send_sem
        self.recv_sem = recv_sem
        self.used = 0
        self.started = []

    def fresh(self, count=1):
        self.used += count
        return self.used - count

    def at(self, step_y, step_z):
        return wrap(self.place_y + step_y) * SIDE + wrap(self.place_z + step_z)

    def remote(self, src, dst, send, recv, to_row, to_col):
        return pltpu.make_async_remote_copy(
            src_ref=src,
            dst_ref=dst,
            send_sem=self.send_sem.at[send],
            recv_sem=self.recv_sem.at[recv],
            device_id=(to_row, to_col),
            device_id_type=MESH,
        )

    def greet(self, devices):
        barrier = pltpu.get_barrier_semaphore()
        for who in devices:
            pl.semaphore_signal(barrier, inc=1, device_id=who, device_id_type=MESH)
        pl.semaphore_wait(barrier, len(devices))

    def col_others(self):
        return [(self.row, lax.rem(self.col + k, COLS)) for k in range(1, COLS)]

    def ring(self, half, piece, own):
        if half == 0:
            place = lambda i, j: self.at(j, i)
        else:
            place = lambda i, j: self.at(i, j)
        sem = {}

        def key(name):
            if name not in sem:
                sem[name] = self.fresh()
            return sem[name]

        pending = {}

        def go(name, i, j, part, to_i, to_j):
            number = key(name)

            def build():
                mine = (i, j) == (0, 0)
                source = own() if mine else piece(place(i, j), half, part)
                target = piece(place(i, j), half, part)
                return self.remote(source, target, number, number, self.row, place(to_i, to_j))

            build().start()
            pending[name] = build
            self.started.append(build)

        def arrived(name):
            pending[name]().wait_recv()

        def quarter(d):
            return 1 if d == 1 else 2

        def first():
            for d in (1, -1):
                go(("a", d), 0, 0, 0, d, 0)

        def second():
            for e in (1, -1):
                go(("b", 0, e), 0, 0, 0, 0, e)

        def near(d):
            arrived(("a", d))
            go(("af", d), -d, 0, quarter(d), d, 0)
            for e in (1, -1):
                go(("b", -d, e), -d, 0, 0, 0, e)

        def far():
            arrived(("af", 1))
            arrived(("af", -1))
            for e in (1, -1):
                go(("b", 2, e), 2, 0, 0, 0, e)

        def cross(i):
            for e in (1, -1):
                arrived(("b", i, e))
                go(("bf", i, e), i, -e, quarter(e), 0, e)

        def last(i):
            for e in (1, -1):
                arrived(("bf", i, e))

        return first, second, near, far, cross, last

    def drain(self):
        for build in self.started:
            build().wait_send()


def ring_steps(rings):
    def each(index, *args):
        return [lambda r=r: r[index](*args) for r in rings]

    steps = each(0) + each(1) + each(2, 1) + each(2, -1) + each(4, 0) + each(3)
    for i in (1, -1, 2):
        steps += each(4, i)
    for i in (0, 1, -1, 2):
        steps += each(5, i)
    return steps


def gather_kernel(
    order_ref, own_ref, front_ref, tiles_ref, top_ref, lead_ref,
    all_ref, high_ref, low_ref, corner_ref, send_sem, recv_sem, local_sem,
):
    wires = Wires(send_sem, recv_sem)
    row, col, chip, core = wires.row, wires.col, wires.chip, wires.core
    fresh, remote = wires.fresh, wires.remote
    load_top = pltpu.make_async_copy(front_ref.at[pl.ds(0, LEAD)], top_ref, local_sem.at[0])

    @pl.when(row == 0)
    def _():
        load_top.start()

    keep_own = pltpu.make_async_copy(own_ref, all_ref.at[col], local_sem.at[1])
    keep_own.start()
    wires.greet(
        wires.col_others()
        + [
            (lax.rem(row + k, ROWS), col) for k in range(1, ROWS)
        ]
    )

    def factor_piece(slot, half, part):
        if part == 0:
            return all_ref.at[slot, pl.ds(half * 128, 128)]
        return all_ref.at[slot, pl.ds(half * 128 + 64 * (part - 1), 64)]

    top_size = LEAD // TOP_PIECES
    half_pieces = TOP_PIECES // 2
    top_recv = fresh(TOP_PIECES)
    top_next = fresh(TOP_PIECES)
    top_side = fresh(TOP_PIECES)

    def top_copies(piece, way):
        block = top_ref.at[pl.ds(piece * top_size, top_size)]
        onward = lax.rem(row + (2 if way == 1 else 6), ROWS)
        return (
            remote(block, block, top_next + piece, top_recv + piece, onward, col),
            remote(block, block, top_side + piece, top_recv + piece, row + 1 - 2 * core, col),
        )

    def top_step(number):
        for way in (1, -1):
            depth = chip if way == 1 else lax.rem(SIDE - chip, SIDE)
            count = number - depth - core
            piece = 2 * count + (0 if way == 1 else 1)

            @pl.when((count >= 0) & (count < half_pieces))
            def _(piece=piece, way=way, depth=depth):
                onward, side = top_copies(piece, way)

                @pl.when(row != 0)
                def _():
                    side.wait_recv()

                @pl.when((core == 0) & (depth < SIDE - 1))
                def _():
                    onward.start()

                @pl.when(core == 0)
                def _():
                    side.start()

    def top_drain(number):
        for way in (1, -1):
            depth = chip if way == 1 else lax.rem(SIDE - chip, SIDE)
            onward, side = top_copies(2 * number + (0 if way == 1 else 1), way)

            @pl.when((core == 0) & (depth < SIDE - 1))
            def _():
                onward.wait_send()

            @pl.when(core == 0)
            def _():
                side.wait_send()

    corner_recv = fresh()
    along = fresh(COLS)
    down = fresh(ROWS)
    load_corner = pltpu.make_async_copy(
        front_ref.at[pl.ds(0, SLICE), pl.ds(0, LEAD)], corner_ref, local_sem.at[2]
    )

    def along_copy(step):
        return remote(
            front_ref.at[pl.ds(step * SLICE, SLICE), pl.ds(0, LEAD)],
            corner_ref,
            along + step,
            corner_recv,
            row,
            step,
        )

    def down_copy(step):
        start = pl.multiple_of(lax.rem(step, 2) * (SLICE // 2), SLICE // 2)
        part = corner_ref.at[pl.ds(start, SLICE // 2)]
        return remote(part, part, down + step, corner_recv, step, col)

    def each_along(act):
        @pl.when((row == 0) & (col == 0))
        def _():
            @pl.loop(1, COLS)
            def _(step):
                act(along_copy(step))

    def each_down(act):
        @pl.when(row == 0)
        def _():
            @pl.loop(1, ROWS)
            def _(step):
                act(down_copy(step))

    def corner_start():
        each_along(lambda copy: copy.start())

        @pl.when((row == 0) & (col == 0))
        def _():
            load_corner.start()

    def corner_pass():
        @pl.when((row == 0) & (col == 0))
        def _():
            load_corner.wait()

        @pl.when((row == 0) & (col != 0))
        def _():
            along_copy(1).wait_recv()

        each_down(lambda copy: copy.start())

    def corner_wait():
        @pl.when(row != 0)
        def _():
            down_copy(1).wait_recv()

    half_slice = SLICE // 2

    def lead_piece(slot, _, part):
        if part == 0:
            return lead_ref.at[slot, core]
        return lead_ref.at[slot, core, pl.ds((half_slice // 2) * (part - 1), half_slice // 2)]

    def own_corner():
        return corner_ref.at[pl.ds(pl.multiple_of(core * half_slice, half_slice), half_slice)]

    swap_sem = fresh()

    def swap_copy():
        mine = lead_ref.at[:, core]
        return remote(mine, mine, swap_sem, swap_sem, row + 1 - 2 * core, col)

    rings = [
        wires.ring(h, factor_piece, lambda h=h: own_ref.at[pl.ds(h * 128, 128)]) for h in range(2)
    ]
    lead_ring = wires.ring(0, lead_piece, own_corner)
    steps = ring_steps(rings)
    corner_start()
    for run in steps[:4]:
        run()

    @pl.when(row == 0)
    def _():
        load_top.wait()

    for number in range(half_pieces + SIDE):
        top_step(number)
        if number == 2:
            corner_pass()
        for run in steps[4 + 2 * number : 6 + 2 * number]:
            run()
    for run in steps[4 + 2 * (half_pieces + SIDE) :]:
        run()
    corner_wait()
    keep_corner = pltpu.make_async_copy(own_corner(), lead_ref.at[col, core], local_sem.at[3])
    keep_corner.start()
    keep_own.wait()
    lead_steps = ring_steps([lead_ring])
    for run in lead_steps[:2]:
        run()
    high_ref[...], low_ref[...] = halves(all_ref[order_ref[COLS]])

    def tile(number):
        left = halves(all_ref[order_ref[number]])
        tiles_ref[number] = three_pass(left, (high_ref[...], low_ref[...]), ((1,), (1,)))

    for part in range(COLS // 2):
        pl.loop(2 * part, 2 * part + 2)(tile)
        for run in lead_steps[2 + 2 * part : 4 + 2 * part]:
            run()
        if part == COLS // 2 - 2:
            keep_corner.wait()
            swap_copy().start()
    swap_copy().wait_recv()
    swap_copy().wait_send()
    wires.drain()
    for number in range(half_pieces):
        top_drain(number)
    each_along(lambda copy: copy.wait_send())
    each_down(lambda copy: copy.wait_send())


BLOCK = 128
GROUP = 8
GROUPS = BLOCK // GROUP
NEAR = slice(0, BLOCK)
AWAY = slice(BLOCK, TILE)


def triangular(inverses, low, block):
    first = three_pass(inverses[0], halves(block[:TILE]), ((1,), (0,)))
    rest = block[TILE:] - three_pass(low, halves(first), ((1,), (0,)))
    return first, three_pass(inverses[1], halves(rest), ((1,), (0,)))


def spread_kernel(
    top_ref, lead_ref, pan_ref, upper_ref, side_ref, full_ref, low_ref, cols_ref,
    block_ref, inv_ref, work_ref, send_sem, recv_sem, local_sem,
):
    wires = Wires(send_sem, recv_sem)
    row, col = wires.row, wires.col
    fresh, remote = wires.fresh, wires.remote
    wires.greet(wires.col_others())

    def panel_piece(slot, half, part):
        if part == 0:
            return pan_ref.at[half, pl.ds(slot * SLICE, SLICE)]
        size = SLICE // 2
        return pan_ref.at[half, pl.ds(slot * SLICE + size * (part - 1), size)]

    spread = []
    for half in range(2):
        spread.append((half, 2 * row + half, pl.ds(0, COL_WIDTH), pl.ds(0, COL_WIDTH)))
    spread_recv = [fresh() for _ in spread]
    spread_send = [fresh(COLS) for _ in spread]

    def spread_copy(index, step):
        half, _, lanes, to_lanes = spread[index]
        to_col = lax.rem(col + step, COLS)
        rows = pl.ds(to_col * SLICE, SLICE)
        return remote(
            top_ref.at[rows, lanes],
            pan_ref.at[half, rows, to_lanes],
            spread_send[index] + step,
            spread_recv[index],
            row,
            to_col,
        )

    def spread_start(index):
        half, holder, lanes, to_lanes = spread[index]
        rows = pl.ds(col * SLICE, SLICE)

        @pl.when(col == holder)
        def _():
            keep = pltpu.make_async_copy(
                top_ref.at[rows, lanes], pan_ref.at[half, rows, to_lanes], local_sem.at[index]
            )
            keep.start()

            @pl.loop(1, COLS)
            def _(step):
                spread_copy(index, step).start()

            keep.wait()

    def spread_wait(index):
        @pl.when(col != spread[index][1])
        def _():
            spread_copy(index, 1).wait_recv()

    def spread_drain(index):
        @pl.when(col == spread[index][1])
        def _():
            @pl.loop(1, COLS)
            def _(step):
                spread_copy(index, step).wait_send()

    for index in range(2):
        spread_start(index)
    steps = ring_steps(
        [wires.ring(h, panel_piece, lambda h=h: panel_piece(col, h, 0)) for h in range(2)]
    )

    def join_inverse(tile):
        first, second, side = inv_ref[2 * tile], inv_ref[2 * tile + 1], side_ref[tile]
        full_ref[tile, NEAR, NEAR] = first
        full_ref[tile, NEAR, AWAY] = jnp.zeros((BLOCK, BLOCK), F32)
        full_ref[tile, AWAY, NEAR] = -product(second, product(side, first))
        full_ref[tile, AWAY, AWAY] = second

    def second_half(tile, below, corner):
        side = product_rows(below, inv_ref[2 * tile])
        side_ref[tile] = side
        block_ref[...] = corner - product_rows(side, side)

    def body(number, carry):
        @pl.when(number == 0)
        def _():
            block_ref[...] = lead_ref[NEAR, NEAR]

        @pl.when(number == 1)
        def _():
            second_half(0, lead_ref[AWAY, NEAR], lead_ref[AWAY, AWAY])

        @pl.when(number == 2)
        def _():
            for index in range(2):
                spread_wait(index)
            for run in steps[:4]:
                run()
            join_inverse(0)
            low = product_rows(lead_ref[TILE:, :TILE], full_ref[0])
            low_ref[...] = low
            work_ref[...] = lead_ref[TILE:, TILE:] - product_rows(low, low)
            block_ref[...] = work_ref[NEAR, NEAR]

        @pl.when(number == 3)
        def _():
            for run in steps[4:8]:
                run()
            second_half(1, work_ref[AWAY, NEAR], work_ref[AWAY, AWAY])

        eliminate(block_ref, upper_ref.at[number], inv_ref.at[number])
        return carry

    lax.fori_loop(0, 4, body, 0)
    for run in steps[8:12]:
        run()
    join_inverse(1)
    inverses = [halves(full_ref[t]) for t in range(2)]
    low = halves(low_ref[...])
    blank = jnp.zeros((BLOCK, BLOCK), F32)
    for part in range(PCT):
        for run in steps[12 + 2 * part : 14 + 2 * part]:
            run()
        lanes = slice(part * TILE, (part + 1) * TILE)
        first, second = triangular(inverses, low, top_ref[:, lanes])
        cols_ref[:TILE, lanes] = first
        cols_ref[TILE:, lanes] = second

    @pl.when(col == 0)
    def _():
        for t in range(2):
            for r, c, value in (
                (0, 0, upper_ref[2 * t]),
                (0, 1, side_ref[t].T),
                (1, 0, blank),
                (1, 1, upper_ref[2 * t + 1]),
            ):
                r0, c0 = t * TILE + r * BLOCK, t * TILE + c * BLOCK
                cols_ref[r0 : r0 + BLOCK, c0 : c0 + BLOCK] = value
        cols_ref[TILE:, :TILE] = jnp.zeros((TILE, TILE), F32)

    for run in steps[20:]:
        run()
    wires.drain()
    for index in range(2):
        spread_drain(index)


def gather_tiles(order, own_factor, front):
    anywhere = pl.BlockSpec(memory_space=pl.ANY)
    vmem = pl.BlockSpec(memory_space=pltpu.VMEM)
    return pl.pallas_call(
        gather_kernel,
        out_shape=(
            jax.ShapeDtypeStruct((COLS, TILE, TILE), F32),
            jax.ShapeDtypeStruct((LEAD, COL_WIDTH), F32),
            jax.ShapeDtypeStruct((COLS, 2, SLICE // 2, LEAD), F32),
        ),
        in_specs=[pl.BlockSpec(memory_space=pltpu.SMEM), vmem, anywhere],
        out_specs=(vmem,) * 3,
        scratch_shapes=[
            pltpu.VMEM((COLS, TILE, CW), F32),
            pltpu.VMEM((TILE, CW), BF16),
            pltpu.VMEM((TILE, CW), BF16),
            pltpu.VMEM((SLICE, LEAD), F32),
            pltpu.SemaphoreType.DMA((136,)),
            pltpu.SemaphoreType.DMA((136,)),
            pltpu.SemaphoreType.DMA((4,)),
        ],
        compiler_params=pltpu.CompilerParams(
            collective_id=0, has_side_effects=True, vmem_limit_bytes=56 * 2**20
        ),
        name="gather",
    )(order, own_factor, front)


def spread_panel(top, lead):
    vmem = pl.BlockSpec(memory_space=pltpu.VMEM)
    return pl.pallas_call(
        spread_kernel,
        out_shape=(
            jax.ShapeDtypeStruct((2, LEAD, COL_WIDTH), F32),
            jax.ShapeDtypeStruct((4, BLOCK, BLOCK), F32),
            jax.ShapeDtypeStruct((2, BLOCK, BLOCK), F32),
            jax.ShapeDtypeStruct((2, TILE, TILE), F32),
            jax.ShapeDtypeStruct((TILE, TILE), F32),
            jax.ShapeDtypeStruct((LEAD, COL_WIDTH), F32),
        ),
        in_specs=[vmem, vmem],
        out_specs=(vmem,) * 6,
        scratch_shapes=[
            pltpu.VMEM((BLOCK, BLOCK), F32),
            pltpu.VMEM((4, BLOCK, BLOCK), F32),
            pltpu.VMEM((TILE, TILE), F32),
            pltpu.SemaphoreType.DMA((80,)),
            pltpu.SemaphoreType.DMA((80,)),
            pltpu.SemaphoreType.DMA((3,)),
        ],
        compiler_params=pltpu.CompilerParams(
            collective_id=1, has_side_effects=True, vmem_limit_bytes=56 * 2**20
        ),
        cost_estimate=pl.CostEstimate(
            flops=30 * 10**9, bytes_accessed=20 * 2**20, transcendentals=0
        ),
        name="spread",
    )(top, lead)


def eliminate(block_ref, upper_ref, inverse_ref):
    shape = (GROUP, BLOCK)
    lanes = lax.broadcasted_iota(jnp.int32, shape, 1)
    sublanes = lax.broadcasted_iota(jnp.int32, shape, 0)
    left = [block_ref[GROUP * g : GROUP * (g + 1), :] for g in range(GROUPS)]
    right = [jnp.where(lanes == sublanes + GROUP * g, 1.0, 0.0) for g in range(GROUPS)]
    for g in range(GROUPS):
        base = GROUP * g
        row_l = [jnp.broadcast_to(left[g][s : s + 1, :], shape) for s in range(GROUP)]
        row_r = [jnp.broadcast_to(right[g][s : s + 1, :], shape) for s in range(GROUP)]
        entry = {}
        for s in range(GROUP):
            for t in range(s, GROUP):
                entry[s, t] = jnp.broadcast_to(row_l[s][:, base + t : base + t + 1], shape)
        recip = []
        ratio = {}
        for s in range(GROUP):
            recip.append(1.0 / entry[s, s])
            for t in range(s + 1, GROUP):
                ratio[t, s] = entry[s, t] * recip[s]
            for t in range(s + 1, GROUP):
                for u in range(t, GROUP):
                    entry[t, u] = entry[t, u] - ratio[t, s] * entry[s, u]
        for s in range(GROUP):
            for t in range(s):
                row_l[s] = row_l[s] - ratio[s, t] * row_l[t]
                row_r[s] = row_r[s] - ratio[s, t] * row_r[t]
        new_l, new_r, scale = row_l[0], row_r[0], recip[0]
        for s in range(1, GROUP):
            pick = sublanes == s
            new_l = jnp.where(pick, row_l[s], new_l)
            new_r = jnp.where(pick, row_r[s], new_r)
            scale = jnp.where(pick, recip[s], scale)
        for i in range(g + 1, GROUPS):
            plain = []
            for s in range(GROUP):
                value = jnp.broadcast_to(left[i][:, base + s : base + s + 1], shape)
                for t in range(s):
                    value = value - plain[t] * ratio[s, t]
                plain.append(value)
            for s in range(GROUP):
                scaled = plain[s] * recip[s]
                left[i] = left[i] - scaled * row_l[s]
                right[i] = right[i] - scaled * row_r[s]
        scale = jnp.sqrt(scale)
        upper = jnp.where(lanes >= sublanes + base, new_l * scale, 0.0)
        upper_ref[base : base + GROUP, :] = upper
        inverse_ref[base : base + GROUP, :] = new_r * scale


def final_kernel(
    rows_ref, cols_ref, front_ref, pan_ref, right_ref, upper_ref, side_ref, full_ref, low_ref,
    tiles_ref, panel_ref, out_ref, high_ref, small_ref,
):
    row = lax.axis_index("row")
    step = pl.program_id(0)
    inverses = [halves(full_ref[t]) for t in range(2)]
    low = halves(low_ref[...])
    blank = jnp.zeros((BLOCK, BLOCK), F32)

    @pl.when(step == 0)
    def _():
        high_ref[...], small_ref[...] = halves(right_ref[...])

    first, second = triangular(inverses, low, pan_ref[0])
    panel_ref[:, :TILE] = first.T
    panel_ref[:, TILE:] = second.T

    for t in range(2):

        @pl.when((row == 0) & (step == t))
        def _(t=t):
            for r, c, value in (
                (0, 0, upper_ref[2 * t].T),
                (0, 1, blank),
                (1, 0, side_ref[t]),
                (1, 1, upper_ref[2 * t + 1].T),
            ):
                r0, c0 = r * BLOCK, t * TILE + c * BLOCK
                panel_ref[r0 : r0 + BLOCK, c0 : c0 + BLOCK] = value
            if t == 0:
                panel_ref[:, TILE:] = jnp.zeros((TILE, TILE), F32)

    left = halves(panel_ref[...])
    for part in range(PCT):
        span = slice(part * TILE, (part + 1) * TILE)
        right = (high_ref[:, span], small_ref[:, span])
        out_ref[:, span] = front_ref[:, span] - three_pass(left, right, ((1,), (0,)))
    block = step // PCT
    for child in range(ROWS):

        @pl.when(rows_ref[child, block] == step)
        def _(child=child):
            start = pl.multiple_of(cols_ref[child] * TILE, TILE)
            out_ref[:, pl.ds(start, TILE)] -= tiles_ref[child, 0]


def finish(row_places, col_places, front, pan, top, upper, side, full, low, tiles):
    return pl.pallas_call(
        final_kernel,
        out_shape=(
            jax.ShapeDtypeStruct((PANEL_ROWS, LEAD), F32),
            jax.ShapeDtypeStruct((PANEL_ROWS, COL_WIDTH), F32),
        ),
        grid_spec=pltpu.PrefetchScalarGridSpec(
            num_scalar_prefetch=2,
            grid=(RT,),
            in_specs=[
                pl.BlockSpec((TILE, COL_WIDTH), lambda i, *_: (i, 0)),
                pl.BlockSpec((1, LEAD, TILE), lambda i, *_: (i // PCT, 0, lax.rem(i, PCT))),
                pl.BlockSpec((LEAD, COL_WIDTH), lambda i, *_: (0, 0)),
                pl.BlockSpec((4, BLOCK, BLOCK), lambda i, *_: (0, 0, 0)),
                pl.BlockSpec((2, BLOCK, BLOCK), lambda i, *_: (0, 0, 0)),
                pl.BlockSpec((2, TILE, TILE), lambda i, *_: (0, 0, 0)),
                pl.BlockSpec((TILE, TILE), lambda i, *_: (0, 0)),
                pl.BlockSpec((ROWS, 1, TILE, TILE), lambda i, *_: (0, i // PCT, 0, 0)),
            ],
            out_specs=(
                pl.BlockSpec((TILE, LEAD), lambda i, *_: (i, 0)),
                pl.BlockSpec((TILE, COL_WIDTH), lambda i, *_: (i, 0)),
            ),
            scratch_shapes=[
                pltpu.VMEM((LEAD, COL_WIDTH), BF16),
                pltpu.VMEM((LEAD, COL_WIDTH), BF16),
            ],
        ),
        compiler_params=pltpu.CompilerParams(vmem_limit_bytes=58 * 2**20),
        cost_estimate=pl.CostEstimate(
            flops=9 * PANEL_ROWS * COL_WIDTH * LEAD,
            bytes_accessed=30 * 2**20,
            transcendentals=0,
        ),
        name="finish",
    )(row_places, col_places, front, pan, top, upper, side, full, low, tiles)


def per_device(parent_front, child_panels, child_inverses, parent_index):
    here_row = lax.axis_index("row")
    here_col = lax.axis_index("col")
    own_factor = product_rows(child_panels[0], child_inverses[0])
    block_of = parent_index // PCT
    my_blocks = lax.dynamic_index_in_dim(block_of, here_row, 0, keepdims=False)
    ids = jnp.arange(COLS, dtype=jnp.int32)
    wanted = jnp.concatenate([ids, here_col[None].astype(jnp.int32)])
    order = jnp.sum(jnp.where(my_blocks[None, :] == wanted[:, None], ids[None, :], 0), axis=1)
    outgoing, top, lead = gather_tiles(order, own_factor, parent_front)
    lead = lead.reshape(LEAD, LEAD)
    outgoing = outgoing.reshape(ROWS, 2, TILE, TILE)
    tiles = lax.all_to_all(outgoing, "row", split_axis=0, concat_axis=0, tiled=True)

    row_blocks = 2 * here_row + jnp.arange(2, dtype=jnp.int32)
    row_places = (
        jnp.sum(
            jnp.where(
                block_of[:, None, :] == row_blocks[None, :, None], parent_index[:, None, :], 0
            ),
            axis=2,
        )
        - here_row * RT
    )
    col_places = (
        jnp.sum(jnp.where(block_of == here_col, parent_index, 0), axis=1) - here_col * PCT
    )

    top, lead, row_places, col_places = lax.optimization_barrier(
        (top, lead, row_places.astype(jnp.int32), col_places.astype(jnp.int32))
    )
    pan, upper, side, full, low, cols = spread_panel(top, lead)
    panel_out, schur = finish(
        row_places,
        col_places,
        parent_front,
        pan,
        cols,
        upper,
        side,
        full,
        low,
        tiles,
    )
    return (panel_out, schur)


def solution(mesh):
    placed = (P("row", "col"), P("row", "col", None), P("row", None, None), P())
    return jax.shard_map(
        per_device,
        mesh=mesh,
        in_specs=placed,
        out_specs=(P("row", None), P("row", "col")),
        check_vma=False,
    )
```

```python
import jax
import jax.numpy as jnp
from jax import lax
from jax.experimental import pallas as pl
from jax.experimental.pallas import tpu as pltpu
from jax.sharding import PartitionSpec as P

TILE = 256
CW = 512
PCT = 4
NSP = 2
ROWS = 8
COLS = 16
SIDE = 4
RT = 8
LEAD = NSP * TILE
PANEL_ROWS = RT * TILE
COL_WIDTH = PCT * TILE
SLICE = LEAD // COLS
TOP_PIECES = 8
MESH = pl.DeviceIdType.MESH
F32 = jnp.float32
BF16 = jnp.bfloat16


def product(matrix_a, matrix_b):
    return jnp.dot(
        matrix_a, matrix_b, precision=lax.Precision.HIGHEST, preferred_element_type=F32
    )


def product_rows(matrix_a, matrix_b):
    return lax.dot_general(
        matrix_a,
        matrix_b,
        (((1,), (1,)), ((), ())),
        precision=lax.Precision.HIGHEST,
        preferred_element_type=F32,
    )


def halves(value):
    high = value.astype(BF16)
    low = (value - high.astype(F32)).astype(BF16)
    return high, low


def three_pass(pair_a, pair_b, contract):
    def one(left, right):
        return lax.dot_general(left, right, (contract, ((), ())), preferred_element_type=F32)

    return one(pair_a[0], pair_b[0]) + (one(pair_a[0], pair_b[1]) + one(pair_a[1], pair_b[0]))


def wrap(value):
    return lax.rem(value + 2 * SIDE, SIDE)


class Wires:
    def __init__(self, send_sem, recv_sem):
        self.row = lax.axis_index("row")
        self.col = lax.axis_index("col")
        self.place_y = self.col // SIDE
        self.place_z = lax.rem(self.col, SIDE)
        self.chip = self.row // 2
        self.core = lax.rem(self.row, 2)
        self.send_sem = send_sem
        self.recv_sem = recv_sem
        self.used = 0
        self.started = []

    def fresh(self, count=1):
        self.used += count
        return self.used - count

    def at(self, step_y, step_z):
        return wrap(self.place_y + step_y) * SIDE + wrap(self.place_z + step_z)

    def remote(self, src, dst, send, recv, to_row, to_col):
        return pltpu.make_async_remote_copy(
            src_ref=src,
            dst_ref=dst,
            send_sem=self.send_sem.at[send],
            recv_sem=self.recv_sem.at[recv],
            device_id=(to_row, to_col),
            device_id_type=MESH,
        )

    def greet(self, devices):
        barrier = pltpu.get_barrier_semaphore()
        for who in devices:
            pl.semaphore_signal(barrier, inc=1, device_id=who, device_id_type=MESH)
        pl.semaphore_wait(barrier, len(devices))

    def col_others(self):
        return [(self.row, lax.rem(self.col + k, COLS)) for k in range(1, COLS)]

    def ring(self, half, piece, own):
        if half == 0:
            place = lambda i, j: self.at(j, i)
        else:
            place = lambda i, j: self.at(i, j)
        sem = {}

        def key(name):
            if name not in sem:
                sem[name] = self.fresh()
            return sem[name]

        pending = {}

        def go(name, i, j, part, to_i, to_j):
            number = key(name)

            def build():
                mine = (i, j) == (0, 0)
                source = own() if mine else piece(place(i, j), half, part)
                target = piece(place(i, j), half, part)
                return self.remote(source, target, number, number, self.row, place(to_i, to_j))

            build().start()
            pending[name] = build
            self.started.append(build)

        def arrived(name):
            pending[name]().wait_recv()

        def quarter(d):
            return 1 if d == 1 else 2

        def first():
            for d in (1, -1):
                go(("a", d), 0, 0, 0, d, 0)

        def second():
            for e in (1, -1):
                go(("b", 0, e), 0, 0, 0, 0, e)

        def near(d):
            arrived(("a", d))
            go(("af", d), -d, 0, quarter(d), d, 0)
            for e in (1, -1):
                go(("b", -d, e), -d, 0, 0, 0, e)

        def far():
            arrived(("af", 1))
            arrived(("af", -1))
            for e in (1, -1):
                go(("b", 2, e), 2, 0, 0, 0, e)

        def cross(i):
            for e in (1, -1):
                arrived(("b", i, e))
                go(("bf", i, e), i, -e, quarter(e), 0, e)

        def last(i):
            for e in (1, -1):
                arrived(("bf", i, e))

        return first, second, near, far, cross, last

    def drain(self):
        for build in self.started:
            build().wait_send()


def ring_steps(rings):
    def each(index, *args):
        return [lambda r=r: r[index](*args) for r in rings]

    steps = each(0) + each(1) + each(2, 1) + each(2, -1) + each(4, 0) + each(3)
    for i in (1, -1, 2):
        steps += each(4, i)
    for i in (0, 1, -1, 2):
        steps += each(5, i)
    return steps


def gather_kernel(
    order_ref, own_ref, front_ref, tiles_ref, top_ref, lead_ref,
    all_ref, high_ref, low_ref, corner_ref, send_sem, recv_sem, local_sem,
):
    wires = Wires(send_sem, recv_sem)
    row, col, chip, core = wires.row, wires.col, wires.chip, wires.core
    fresh, remote = wires.fresh, wires.remote
    load_top = pltpu.make_async_copy(front_ref.at[pl.ds(0, LEAD)], top_ref, local_sem.at[0])

    @pl.when(row == 0)
    def _():
        load_top.start()

    keep_own = pltpu.make_async_copy(own_ref, all_ref.at[col], local_sem.at[1])
    keep_own.start()
    wires.greet(
        wires.col_others()
        + [
            (lax.rem(row + k, ROWS), col) for k in range(1, ROWS)
        ]
    )

    def factor_piece(slot, half, part):
        if part == 0:
            return all_ref.at[slot, pl.ds(half * 128, 128)]
        return all_ref.at[slot, pl.ds(half * 128 + 64 * (part - 1), 64)]

    top_size = LEAD // TOP_PIECES
    half_pieces = TOP_PIECES // 2
    top_recv = fresh(TOP_PIECES)
    top_next = fresh(TOP_PIECES)
    top_side = fresh(TOP_PIECES)

    def top_copies(piece, way):
        block = top_ref.at[pl.ds(piece * top_size, top_size)]
        onward = lax.rem(row + (2 if way == 1 else 6), ROWS)
        return (
            remote(block, block, top_next + piece, top_recv + piece, onward, col),
            remote(block, block, top_side + piece, top_recv + piece, row + 1 - 2 * core, col),
        )

    def top_step(number):
        for way in (1, -1):
            depth = chip if way == 1 else lax.rem(SIDE - chip, SIDE)
            count = number - depth - core
            piece = 2 * count + (0 if way == 1 else 1)

            @pl.when((count >= 0) & (count < half_pieces))
            def _(piece=piece, way=way, depth=depth):
                onward, side = top_copies(piece, way)

                @pl.when(row != 0)
                def _():
                    side.wait_recv()

                @pl.when((core == 0) & (depth < SIDE - 1))
                def _():
                    onward.start()

                @pl.when(core == 0)
                def _():
                    side.start()

    def top_drain(number):
        for way in (1, -1):
            depth = chip if way == 1 else lax.rem(SIDE - chip, SIDE)
            onward, side = top_copies(2 * number + (0 if way == 1 else 1), way)

            @pl.when((core == 0) & (depth < SIDE - 1))
            def _():
                onward.wait_send()

            @pl.when(core == 0)
            def _():
                side.wait_send()

    corner_recv = fresh()
    along = fresh(COLS)
    down = fresh(ROWS)
    load_corner = pltpu.make_async_copy(
        front_ref.at[pl.ds(0, SLICE), pl.ds(0, LEAD)], corner_ref, local_sem.at[2]
    )

    def along_copy(step):
        return remote(
            front_ref.at[pl.ds(step * SLICE, SLICE), pl.ds(0, LEAD)],
            corner_ref,
            along + step,
            corner_recv,
            row,
            step,
        )

    def down_copy(step):
        start = pl.multiple_of(lax.rem(step, 2) * (SLICE // 2), SLICE // 2)
        part = corner_ref.at[pl.ds(start, SLICE // 2)]
        return remote(part, part, down + step, corner_recv, step, col)

    def each_along(act):
        @pl.when((row == 0) & (col == 0))
        def _():
            @pl.loop(1, COLS)
            def _(step):
                act(along_copy(step))

    def each_down(act):
        @pl.when(row == 0)
        def _():
            @pl.loop(1, ROWS)
            def _(step):
                act(down_copy(step))

    def corner_start():
        each_along(lambda copy: copy.start())

        @pl.when((row == 0) & (col == 0))
        def _():
            load_corner.start()

    def corner_pass():
        @pl.when((row == 0) & (col == 0))
        def _():
            load_corner.wait()

        @pl.when((row == 0) & (col != 0))
        def _():
            along_copy(1).wait_recv()

        each_down(lambda copy: copy.start())

    def corner_wait():
        @pl.when(row != 0)
        def _():
            down_copy(1).wait_recv()

    half_slice = SLICE // 2

    def lead_piece(slot, _, part):
        if part == 0:
            return lead_ref.at[slot, core]
        return lead_ref.at[slot, core, pl.ds((half_slice // 2) * (part - 1), half_slice // 2)]

    def own_corner():
        return corner_ref.at[pl.ds(pl.multiple_of(core * half_slice, half_slice), half_slice)]

    swap_sem = fresh()

    def swap_copy():
        mine = lead_ref.at[:, core]
        return remote(mine, mine, swap_sem, swap_sem, row + 1 - 2 * core, col)

    rings = [
        wires.ring(h, factor_piece, lambda h=h: own_ref.at[pl.ds(h * 128, 128)]) for h in range(2)
    ]
    lead_ring = wires.ring(0, lead_piece, own_corner)
    steps = ring_steps(rings)
    for run in steps[:4]:
        run()
    corner_start()

    @pl.when(row == 0)
    def _():
        load_top.wait()

    for run in steps[4:8]:
        run()
    for number in range(half_pieces + SIDE):
        top_step(number)
        if number == 6:
            corner_pass()
        for run in steps[8 + 2 * number : 10 + 2 * number]:
            run()
    for run in steps[8 + 2 * (half_pieces + SIDE) :]:
        run()
    corner_wait()
    keep_corner = pltpu.make_async_copy(own_corner(), lead_ref.at[col, core], local_sem.at[3])
    keep_corner.start()
    keep_own.wait()
    lead_steps = ring_steps([lead_ring])
    for run in lead_steps[:2]:
        run()
    high_ref[...], low_ref[...] = halves(all_ref[order_ref[COLS]])

    def tile(number):
        left = halves(all_ref[order_ref[number]])
        tiles_ref[number] = three_pass(left, (high_ref[...], low_ref[...]), ((1,), (1,)))

    for part in range(COLS // 2):
        pl.loop(2 * part, 2 * part + 2)(tile)
        for run in lead_steps[2 + 2 * part : 4 + 2 * part]:
            run()
        if part == COLS // 2 - 2:
            keep_corner.wait()
            swap_copy().start()
    swap_copy().wait_recv()
    swap_copy().wait_send()
    wires.drain()
    for number in range(half_pieces):
        top_drain(number)
    each_along(lambda copy: copy.wait_send())
    each_down(lambda copy: copy.wait_send())


BLOCK = 128
GROUP = 8
GROUPS = BLOCK // GROUP
NEAR = slice(0, BLOCK)
AWAY = slice(BLOCK, TILE)


def triangular(inverses, low, block):
    first = three_pass(inverses[0], halves(block[:TILE]), ((1,), (0,)))
    rest = block[TILE:] - three_pass(low, halves(first), ((1,), (0,)))
    return first, three_pass(inverses[1], halves(rest), ((1,), (0,)))


def spread_kernel(
    top_ref, lead_ref, pan_ref, upper_ref, side_ref, full_ref, low_ref, cols_ref,
    block_ref, inv_ref, work_ref, send_sem, recv_sem, local_sem,
):
    wires = Wires(send_sem, recv_sem)
    row, col = wires.row, wires.col
    fresh, remote = wires.fresh, wires.remote
    wires.greet(wires.col_others())

    def panel_piece(slot, half, part):
        if part == 0:
            return pan_ref.at[half, pl.ds(slot * SLICE, SLICE)]
        size = SLICE // 2
        return pan_ref.at[half, pl.ds(slot * SLICE + size * (part - 1), size)]

    spread = []
    for half in range(2):
        spread.append((half, 2 * row + half, pl.ds(0, COL_WIDTH), pl.ds(0, COL_WIDTH)))
    spread_recv = [fresh() for _ in spread]
    spread_send = [fresh(COLS) for _ in spread]

    def spread_copy(index, step):
        half, _, lanes, to_lanes = spread[index]
        to_col = lax.rem(col + step, COLS)
        rows = pl.ds(to_col * SLICE, SLICE)
        return remote(
            top_ref.at[rows, lanes],
            pan_ref.at[half, rows, to_lanes],
            spread_send[index] + step,
            spread_recv[index],
            row,
            to_col,
        )

    def spread_start(index):
        half, holder, lanes, to_lanes = spread[index]
        rows = pl.ds(col * SLICE, SLICE)

        @pl.when(col == holder)
        def _():
            keep = pltpu.make_async_copy(
                top_ref.at[rows, lanes], pan_ref.at[half, rows, to_lanes], local_sem.at[index]
            )
            keep.start()

            @pl.loop(1, COLS)
            def _(step):
                spread_copy(index, step).start()

            keep.wait()

    def spread_wait(index):
        @pl.when(col != spread[index][1])
        def _():
            spread_copy(index, 1).wait_recv()

    def spread_drain(index):
        @pl.when(col == spread[index][1])
        def _():
            @pl.loop(1, COLS)
            def _(step):
                spread_copy(index, step).wait_send()

    for index in range(2):
        spread_start(index)
    steps = ring_steps(
        [wires.ring(h, panel_piece, lambda h=h: panel_piece(col, h, 0)) for h in range(2)]
    )

    def join_inverse(tile):
        first, second, side = inv_ref[2 * tile], inv_ref[2 * tile + 1], side_ref[tile]
        full_ref[tile, NEAR, NEAR] = first
        full_ref[tile, NEAR, AWAY] = jnp.zeros((BLOCK, BLOCK), F32)
        full_ref[tile, AWAY, NEAR] = -product(second, product(side, first))
        full_ref[tile, AWAY, AWAY] = second

    def second_half(tile, below, corner):
        side = product_rows(below, inv_ref[2 * tile])
        side_ref[tile] = side
        block_ref[...] = corner - product_rows(side, side)

    def body(number, carry):
        @pl.when(number == 0)
        def _():
            block_ref[...] = lead_ref[NEAR, NEAR]

        @pl.when(number == 1)
        def _():
            second_half(0, lead_ref[AWAY, NEAR], lead_ref[AWAY, AWAY])

        @pl.when(number == 2)
        def _():
            for index in range(2):
                spread_wait(index)
            for run in steps[:4]:
                run()
            join_inverse(0)
            low = product_rows(lead_ref[TILE:, :TILE], full_ref[0])
            low_ref[...] = low
            work_ref[...] = lead_ref[TILE:, TILE:] - product_rows(low, low)
            block_ref[...] = work_ref[NEAR, NEAR]

        @pl.when(number == 3)
        def _():
            for run in steps[4:8]:
                run()
            second_half(1, work_ref[AWAY, NEAR], work_ref[AWAY, AWAY])

        eliminate(block_ref, upper_ref.at[number], inv_ref.at[number])
        return carry

    lax.fori_loop(0, 4, body, 0)
    for run in steps[8:12]:
        run()
    join_inverse(1)
    inverses = [halves(full_ref[t]) for t in range(2)]
    low = halves(low_ref[...])
    blank = jnp.zeros((BLOCK, BLOCK), F32)
    for part in range(PCT):
        for run in steps[12 + 2 * part : 14 + 2 * part]:
            run()
        lanes = slice(part * TILE, (part + 1) * TILE)
        first, second = triangular(inverses, low, top_ref[:, lanes])
        cols_ref[:TILE, lanes] = first
        cols_ref[TILE:, lanes] = second

    @pl.when(col == 0)
    def _():
        for t in range(2):
            for r, c, value in (
                (0, 0, upper_ref[2 * t]),
                (0, 1, side_ref[t].T),
                (1, 0, blank),
                (1, 1, upper_ref[2 * t + 1]),
            ):
                r0, c0 = t * TILE + r * BLOCK, t * TILE + c * BLOCK
                cols_ref[r0 : r0 + BLOCK, c0 : c0 + BLOCK] = value
        cols_ref[TILE:, :TILE] = jnp.zeros((TILE, TILE), F32)

    for run in steps[20:]:
        run()
    wires.drain()
    for index in range(2):
        spread_drain(index)


def gather_tiles(order, own_factor, front):
    anywhere = pl.BlockSpec(memory_space=pl.ANY)
    vmem = pl.BlockSpec(memory_space=pltpu.VMEM)
    return pl.pallas_call(
        gather_kernel,
        out_shape=(
            jax.ShapeDtypeStruct((COLS, TILE, TILE), F32),
            jax.ShapeDtypeStruct((LEAD, COL_WIDTH), F32),
            jax.ShapeDtypeStruct((COLS, 2, SLICE // 2, LEAD), F32),
        ),
        in_specs=[pl.BlockSpec(memory_space=pltpu.SMEM), vmem, anywhere],
        out_specs=(vmem,) * 3,
        scratch_shapes=[
            pltpu.VMEM((COLS, TILE, CW), F32),
            pltpu.VMEM((TILE, CW), BF16),
            pltpu.VMEM((TILE, CW), BF16),
            pltpu.VMEM((SLICE, LEAD), F32),
            pltpu.SemaphoreType.DMA((136,)),
            pltpu.SemaphoreType.DMA((136,)),
            pltpu.SemaphoreType.DMA((4,)),
        ],
        compiler_params=pltpu.CompilerParams(
            collective_id=0, has_side_effects=True, vmem_limit_bytes=56 * 2**20
        ),
        name="gather",
    )(order, own_factor, front)


def spread_panel(top, lead):
    vmem = pl.BlockSpec(memory_space=pltpu.VMEM)
    return pl.pallas_call(
        spread_kernel,
        out_shape=(
            jax.ShapeDtypeStruct((2, LEAD, COL_WIDTH), F32),
            jax.ShapeDtypeStruct((4, BLOCK, BLOCK), F32),
            jax.ShapeDtypeStruct((2, BLOCK, BLOCK), F32),
            jax.ShapeDtypeStruct((2, TILE, TILE), F32),
            jax.ShapeDtypeStruct((TILE, TILE), F32),
            jax.ShapeDtypeStruct((LEAD, COL_WIDTH), F32),
        ),
        in_specs=[vmem, vmem],
        out_specs=(vmem,) * 6,
        scratch_shapes=[
            pltpu.VMEM((BLOCK, BLOCK), F32),
            pltpu.VMEM((4, BLOCK, BLOCK), F32),
            pltpu.VMEM((TILE, TILE), F32),
            pltpu.SemaphoreType.DMA((80,)),
            pltpu.SemaphoreType.DMA((80,)),
            pltpu.SemaphoreType.DMA((3,)),
        ],
        compiler_params=pltpu.CompilerParams(
            collective_id=1, has_side_effects=True, vmem_limit_bytes=56 * 2**20
        ),
        cost_estimate=pl.CostEstimate(
            flops=30 * 10**9, bytes_accessed=20 * 2**20, transcendentals=0
        ),
        name="spread",
    )(top, lead)


def eliminate(block_ref, upper_ref, inverse_ref):
    shape = (GROUP, BLOCK)
    lanes = lax.broadcasted_iota(jnp.int32, shape, 1)
    sublanes = lax.broadcasted_iota(jnp.int32, shape, 0)
    left = [block_ref[GROUP * g : GROUP * (g + 1), :] for g in range(GROUPS)]
    right = [jnp.where(lanes == sublanes + GROUP * g, 1.0, 0.0) for g in range(GROUPS)]
    for g in range(GROUPS):
        base = GROUP * g
        row_l = [jnp.broadcast_to(left[g][s : s + 1, :], shape) for s in range(GROUP)]
        row_r = [jnp.broadcast_to(right[g][s : s + 1, :], shape) for s in range(GROUP)]
        entry = {}
        for s in range(GROUP):
            for t in range(s, GROUP):
                entry[s, t] = jnp.broadcast_to(row_l[s][:, base + t : base + t + 1], shape)
        recip = []
        ratio = {}
        for s in range(GROUP):
            recip.append(1.0 / entry[s, s])
            for t in range(s + 1, GROUP):
                ratio[t, s] = entry[s, t] * recip[s]
            for t in range(s + 1, GROUP):
                for u in range(t, GROUP):
                    entry[t, u] = entry[t, u] - ratio[t, s] * entry[s, u]
        for s in range(GROUP):
            for t in range(s):
                row_l[s] = row_l[s] - ratio[s, t] * row_l[t]
                row_r[s] = row_r[s] - ratio[s, t] * row_r[t]
        new_l, new_r, scale = row_l[0], row_r[0], recip[0]
        for s in range(1, GROUP):
            pick = sublanes == s
            new_l = jnp.where(pick, row_l[s], new_l)
            new_r = jnp.where(pick, row_r[s], new_r)
            scale = jnp.where(pick, recip[s], scale)
        for i in range(g + 1, GROUPS):
            plain = []
            for s in range(GROUP):
                value = jnp.broadcast_to(left[i][:, base + s : base + s + 1], shape)
                for t in range(s):
                    value = value - plain[t] * ratio[s, t]
                plain.append(value)
            for s in range(GROUP):
                scaled = plain[s] * recip[s]
                left[i] = left[i] - scaled * row_l[s]
                right[i] = right[i] - scaled * row_r[s]
        scale = jnp.sqrt(scale)
        upper = jnp.where(lanes >= sublanes + base, new_l * scale, 0.0)
        upper_ref[base : base + GROUP, :] = upper
        inverse_ref[base : base + GROUP, :] = new_r * scale


def final_kernel(
    rows_ref, cols_ref, front_ref, pan_ref, right_ref, upper_ref, side_ref, full_ref, low_ref,
    tiles_ref, panel_ref, out_ref, high_ref, small_ref,
):
    row = lax.axis_index("row")
    step = pl.program_id(0)
    inverses = [halves(full_ref[t]) for t in range(2)]
    low = halves(low_ref[...])
    blank = jnp.zeros((BLOCK, BLOCK), F32)

    @pl.when(step == 0)
    def _():
        high_ref[...], small_ref[...] = halves(right_ref[...])

    first, second = triangular(inverses, low, pan_ref[0])
    panel_ref[:, :TILE] = first.T
    panel_ref[:, TILE:] = second.T

    for t in range(2):

        @pl.when((row == 0) & (step == t))
        def _(t=t):
            for r, c, value in (
                (0, 0, upper_ref[2 * t].T),
                (0, 1, blank),
                (1, 0, side_ref[t]),
                (1, 1, upper_ref[2 * t + 1].T),
            ):
                r0, c0 = r * BLOCK, t * TILE + c * BLOCK
                panel_ref[r0 : r0 + BLOCK, c0 : c0 + BLOCK] = value
            if t == 0:
                panel_ref[:, TILE:] = jnp.zeros((TILE, TILE), F32)

    left = halves(panel_ref[...])
    for part in range(PCT):
        span = slice(part * TILE, (part + 1) * TILE)
        right = (high_ref[:, span], small_ref[:, span])
        out_ref[:, span] = front_ref[:, span] - three_pass(left, right, ((1,), (0,)))
    block = step // PCT
    for child in range(ROWS):

        @pl.when(rows_ref[child, block] == step)
        def _(child=child):
            start = pl.multiple_of(cols_ref[child] * TILE, TILE)
            out_ref[:, pl.ds(start, TILE)] -= tiles_ref[child, 0]


def finish(row_places, col_places, front, pan, top, upper, side, full, low, tiles):
    return pl.pallas_call(
        final_kernel,
        out_shape=(
            jax.ShapeDtypeStruct((PANEL_ROWS, LEAD), F32),
            jax.ShapeDtypeStruct((PANEL_ROWS, COL_WIDTH), F32),
        ),
        grid_spec=pltpu.PrefetchScalarGridSpec(
            num_scalar_prefetch=2,
            grid=(RT,),
            in_specs=[
                pl.BlockSpec((TILE, COL_WIDTH), lambda i, *_: (i, 0)),
                pl.BlockSpec((1, LEAD, TILE), lambda i, *_: (i // PCT, 0, lax.rem(i, PCT))),
                pl.BlockSpec((LEAD, COL_WIDTH), lambda i, *_: (0, 0)),
                pl.BlockSpec((4, BLOCK, BLOCK), lambda i, *_: (0, 0, 0)),
                pl.BlockSpec((2, BLOCK, BLOCK), lambda i, *_: (0, 0, 0)),
                pl.BlockSpec((2, TILE, TILE), lambda i, *_: (0, 0, 0)),
                pl.BlockSpec((TILE, TILE), lambda i, *_: (0, 0)),
                pl.BlockSpec((ROWS, 1, TILE, TILE), lambda i, *_: (0, i // PCT, 0, 0)),
            ],
            out_specs=(
                pl.BlockSpec((TILE, LEAD), lambda i, *_: (i, 0)),
                pl.BlockSpec((TILE, COL_WIDTH), lambda i, *_: (i, 0)),
            ),
            scratch_shapes=[
                pltpu.VMEM((LEAD, COL_WIDTH), BF16),
                pltpu.VMEM((LEAD, COL_WIDTH), BF16),
            ],
        ),
        compiler_params=pltpu.CompilerParams(vmem_limit_bytes=58 * 2**20),
        cost_estimate=pl.CostEstimate(
            flops=9 * PANEL_ROWS * COL_WIDTH * LEAD,
            bytes_accessed=30 * 2**20,
            transcendentals=0,
        ),
        name="finish",
    )(row_places, col_places, front, pan, top, upper, side, full, low, tiles)


def per_device(parent_front, child_panels, child_inverses, parent_index):
    here_row = lax.axis_index("row")
    here_col = lax.axis_index("col")
    own_factor = product_rows(child_panels[0], child_inverses[0])
    block_of = parent_index // PCT
    my_blocks = lax.dynamic_index_in_dim(block_of, here_row, 0, keepdims=False)
    ids = jnp.arange(COLS, dtype=jnp.int32)
    wanted = jnp.concatenate([ids, here_col[None].astype(jnp.int32)])
    order = jnp.sum(jnp.where(my_blocks[None, :] == wanted[:, None], ids[None, :], 0), axis=1)
    outgoing, top, lead = gather_tiles(order, own_factor, parent_front)
    lead = lead.reshape(LEAD, LEAD)
    outgoing = outgoing.reshape(ROWS, 2, TILE, TILE)
    tiles = lax.all_to_all(outgoing, "row", split_axis=0, concat_axis=0, tiled=True)

    row_blocks = 2 * here_row + jnp.arange(2, dtype=jnp.int32)
    row_places = (
        jnp.sum(
            jnp.where(
                block_of[:, None, :] == row_blocks[None, :, None], parent_index[:, None, :], 0
            ),
            axis=2,
        )
        - here_row * RT
    )
    col_places = (
        jnp.sum(jnp.where(block_of == here_col, parent_index, 0), axis=1) - here_col * PCT
    )

    top, lead, row_places, col_places = lax.optimization_barrier(
        (top, lead, row_places.astype(jnp.int32), col_places.astype(jnp.int32))
    )
    pan, upper, side, full, low, cols = spread_panel(top, lead)
    panel_out, schur = finish(
        row_places,
        col_places,
        parent_front,
        pan,
        cols,
        upper,
        side,
        full,
        low,
        tiles,
    )
    return (panel_out, schur)


def solution(mesh):
    placed = (P("row", "col"), P("row", "col", None), P("row", None, None), P())
    return jax.shard_map(
        per_device,
        mesh=mesh,
        in_specs=placed,
        out_specs=(P("row", None), P("row", "col")),
        check_vma=False,
    )
```

```python
import jax
import jax.numpy as jnp
from jax import lax
from jax.experimental import pallas as pl
from jax.experimental.pallas import tpu as pltpu
from jax.sharding import PartitionSpec as P

TILE = 256
CW = 512
PCT = 4
NSP = 2
ROWS = 8
COLS = 16
SIDE = 4
RT = 8
LEAD = NSP * TILE
PANEL_ROWS = RT * TILE
COL_WIDTH = PCT * TILE
SLICE = LEAD // COLS
TOP_PIECES = 8
MESH = pl.DeviceIdType.MESH
F32 = jnp.float32
BF16 = jnp.bfloat16


def product(matrix_a, matrix_b):
    return jnp.dot(
        matrix_a, matrix_b, precision=lax.Precision.HIGHEST, preferred_element_type=F32
    )


def product_rows(matrix_a, matrix_b):
    return lax.dot_general(
        matrix_a,
        matrix_b,
        (((1,), (1,)), ((), ())),
        precision=lax.Precision.HIGHEST,
        preferred_element_type=F32,
    )


def halves(value):
    high = value.astype(BF16)
    low = (value - high.astype(F32)).astype(BF16)
    return high, low


def three_pass(pair_a, pair_b, contract):
    def one(left, right):
        return lax.dot_general(left, right, (contract, ((), ())), preferred_element_type=F32)

    return one(pair_a[0], pair_b[0]) + (one(pair_a[0], pair_b[1]) + one(pair_a[1], pair_b[0]))


def wrap(value):
    return lax.rem(value + 2 * SIDE, SIDE)


class Wires:
    def __init__(self, send_sem, recv_sem):
        self.row = lax.axis_index("row")
        self.col = lax.axis_index("col")
        self.place_y = self.col // SIDE
        self.place_z = lax.rem(self.col, SIDE)
        self.chip = self.row // 2
        self.core = lax.rem(self.row, 2)
        self.send_sem = send_sem
        self.recv_sem = recv_sem
        self.used = 0
        self.started = []

    def fresh(self, count=1):
        self.used += count
        return self.used - count

    def at(self, step_y, step_z):
        return wrap(self.place_y + step_y) * SIDE + wrap(self.place_z + step_z)

    def remote(self, src, dst, send, recv, to_row, to_col):
        return pltpu.make_async_remote_copy(
            src_ref=src,
            dst_ref=dst,
            send_sem=self.send_sem.at[send],
            recv_sem=self.recv_sem.at[recv],
            device_id=(to_row, to_col),
            device_id_type=MESH,
        )

    def greet(self, devices):
        barrier = pltpu.get_barrier_semaphore()
        for who in devices:
            pl.semaphore_signal(barrier, inc=1, device_id=who, device_id_type=MESH)
        pl.semaphore_wait(barrier, len(devices))

    def col_others(self):
        return [(self.row, lax.rem(self.col + k, COLS)) for k in range(1, COLS)]

    def ring(self, half, piece, own):
        if half == 0:
            place = lambda i, j: self.at(j, i)
        else:
            place = lambda i, j: self.at(i, j)
        sem = {}

        def key(name):
            if name not in sem:
                sem[name] = self.fresh()
            return sem[name]

        pending = {}

        def go(name, i, j, part, to_i, to_j):
            number = key(name)

            def build():
                mine = (i, j) == (0, 0)
                source = own() if mine else piece(place(i, j), half, part)
                target = piece(place(i, j), half, part)
                return self.remote(source, target, number, number, self.row, place(to_i, to_j))

            build().start()
            pending[name] = build
            self.started.append(build)

        def arrived(name):
            pending[name]().wait_recv()

        def quarter(d):
            return 1 if d == 1 else 2

        def first():
            for d in (1, -1):
                go(("a", d), 0, 0, 0, d, 0)

        def second():
            for e in (1, -1):
                go(("b", 0, e), 0, 0, 0, 0, e)

        def near(d):
            arrived(("a", d))
            go(("af", d), -d, 0, quarter(d), d, 0)
            for e in (1, -1):
                go(("b", -d, e), -d, 0, 0, 0, e)

        def far():
            arrived(("af", 1))
            arrived(("af", -1))
            for e in (1, -1):
                go(("b", 2, e), 2, 0, 0, 0, e)

        def cross(i):
            for e in (1, -1):
                arrived(("b", i, e))
                go(("bf", i, e), i, -e, quarter(e), 0, e)

        def last(i):
            for e in (1, -1):
                arrived(("bf", i, e))

        return first, second, near, far, cross, last

    def drain(self):
        for build in self.started:
            build().wait_send()


def ring_steps(rings):
    def each(index, *args):
        return [lambda r=r: r[index](*args) for r in rings]

    steps = each(0) + each(1) + each(2, 1) + each(2, -1) + each(4, 0) + each(3)
    for i in (1, -1, 2):
        steps += each(4, i)
    for i in (0, 1, -1, 2):
        steps += each(5, i)
    return steps


def gather_kernel(
    order_ref, own_ref, front_ref, tiles_ref, top_ref, lead_ref,
    all_ref, high_ref, low_ref, corner_ref, send_sem, recv_sem, local_sem,
):
    wires = Wires(send_sem, recv_sem)
    row, col, chip, core = wires.row, wires.col, wires.chip, wires.core
    fresh, remote = wires.fresh, wires.remote
    load_top = pltpu.make_async_copy(front_ref.at[pl.ds(0, LEAD)], top_ref, local_sem.at[0])

    @pl.when(row == 0)
    def _():
        load_top.start()

    keep_own = pltpu.make_async_copy(own_ref, all_ref.at[col], local_sem.at[1])
    keep_own.start()
    wires.greet(
        wires.col_others()
        + [
            (lax.rem(row + k, ROWS), col) for k in range(1, ROWS)
        ]
    )

    def factor_piece(slot, half, part):
        if part == 0:
            return all_ref.at[slot, pl.ds(half * 128, 128)]
        return all_ref.at[slot, pl.ds(half * 128 + 64 * (part - 1), 64)]

    top_size = LEAD // TOP_PIECES
    half_pieces = TOP_PIECES // 2
    top_recv = fresh(TOP_PIECES)
    top_next = fresh(TOP_PIECES)
    top_side = fresh(TOP_PIECES)

    def top_copies(piece, way):
        block = top_ref.at[pl.ds(piece * top_size, top_size)]
        onward = lax.rem(row + (2 if way == 1 else 6), ROWS)
        return (
            remote(block, block, top_next + piece, top_recv + piece, onward, col),
            remote(block, block, top_side + piece, top_recv + piece, row + 1 - 2 * core, col),
        )

    def top_step(number):
        for way in (1, -1):
            depth = chip if way == 1 else lax.rem(SIDE - chip, SIDE)
            count = number - depth - core
            piece = 2 * count + (0 if way == 1 else 1)

            @pl.when((count >= 0) & (count < half_pieces))
            def _(piece=piece, way=way, depth=depth):
                onward, side = top_copies(piece, way)

                @pl.when(row != 0)
                def _():
                    side.wait_recv()

                @pl.when((core == 0) & (depth < SIDE - 1))
                def _():
                    onward.start()

                @pl.when(core == 0)
                def _():
                    side.start()

    def top_drain(number):
        for way in (1, -1):
            depth = chip if way == 1 else lax.rem(SIDE - chip, SIDE)
            onward, side = top_copies(2 * number + (0 if way == 1 else 1), way)

            @pl.when((core == 0) & (depth < SIDE - 1))
            def _():
                onward.wait_send()

            @pl.when(core == 0)
            def _():
                side.wait_send()

    corner_recv = fresh()
    along = fresh(COLS)
    down = fresh(ROWS)
    load_corner = pltpu.make_async_copy(
        front_ref.at[pl.ds(0, SLICE), pl.ds(0, LEAD)], corner_ref, local_sem.at[2]
    )

    def along_copy(step):
        return remote(
            front_ref.at[pl.ds(step * SLICE, SLICE), pl.ds(0, LEAD)],
            corner_ref,
            along + step,
            corner_recv,
            row,
            step,
        )

    def down_copy(step):
        start = pl.multiple_of(lax.rem(step, 2) * (SLICE // 2), SLICE // 2)
        part = corner_ref.at[pl.ds(start, SLICE // 2)]
        return remote(part, part, down + step, corner_recv, step, col)

    def each_along(act):
        @pl.when((row == 0) & (col == 0))
        def _():
            @pl.loop(1, COLS)
            def _(step):
                act(along_copy(step))

    def each_down(act):
        @pl.when(row == 0)
        def _():
            @pl.loop(1, ROWS)
            def _(step):
                act(down_copy(step))

    def corner_start():
        each_along(lambda copy: copy.start())

        @pl.when((row == 0) & (col == 0))
        def _():
            load_corner.start()

    def corner_pass():
        @pl.when((row == 0) & (col == 0))
        def _():
            load_corner.wait()

        @pl.when((row == 0) & (col != 0))
        def _():
            along_copy(1).wait_recv()

        each_down(lambda copy: copy.start())

    def corner_wait():
        @pl.when(row != 0)
        def _():
            down_copy(1).wait_recv()

    half_slice = SLICE // 2

    def lead_piece(slot, _, part):
        if part == 0:
            return lead_ref.at[slot, core]
        return lead_ref.at[slot, core, pl.ds((half_slice // 2) * (part - 1), half_slice // 2)]

    def own_corner():
        return corner_ref.at[pl.ds(pl.multiple_of(core * half_slice, half_slice), half_slice)]

    swap_sem = fresh()

    def swap_copy():
        mine = lead_ref.at[:, core]
        return remote(mine, mine, swap_sem, swap_sem, row + 1 - 2 * core, col)

    rings = [
        wires.ring(h, factor_piece, lambda h=h: own_ref.at[pl.ds(h * 128, 128)]) for h in range(2)
    ]
    lead_ring = wires.ring(0, lead_piece, own_corner)
    steps = ring_steps(rings)
    corner_start()
    for run in steps[:4]:
        run()

    @pl.when(row == 0)
    def _():
        load_top.wait()

    for run in steps[4:8]:
        run()
    corner_pass()
    for number in range(half_pieces + SIDE):
        top_step(number)
        for run in steps[8 + 2 * number : 10 + 2 * number]:
            run()
    for run in steps[8 + 2 * (half_pieces + SIDE) :]:
        run()
    corner_wait()
    keep_corner = pltpu.make_async_copy(own_corner(), lead_ref.at[col, core], local_sem.at[3])
    keep_corner.start()
    keep_own.wait()
    lead_steps = ring_steps([lead_ring])
    for run in lead_steps[:2]:
        run()
    high_ref[...], low_ref[...] = halves(all_ref[order_ref[COLS]])

    def tile(number):
        left = halves(all_ref[order_ref[number]])
        tiles_ref[number] = three_pass(left, (high_ref[...], low_ref[...]), ((1,), (1,)))

    for part in range(COLS // 2):
        pl.loop(2 * part, 2 * part + 2)(tile)
        for run in lead_steps[2 + 2 * part : 4 + 2 * part]:
            run()
        if part == COLS // 2 - 2:
            keep_corner.wait()
            swap_copy().start()
    swap_copy().wait_recv()
    swap_copy().wait_send()
    wires.drain()
    for number in range(half_pieces):
        top_drain(number)
    each_along(lambda copy: copy.wait_send())
    each_down(lambda copy: copy.wait_send())


BLOCK = 128
GROUP = 8
GROUPS = BLOCK // GROUP
NEAR = slice(0, BLOCK)
AWAY = slice(BLOCK, TILE)


def triangular(inverses, low, block):
    first = three_pass(inverses[0], halves(block[:TILE]), ((1,), (0,)))
    rest = block[TILE:] - three_pass(low, halves(first), ((1,), (0,)))
    return first, three_pass(inverses[1], halves(rest), ((1,), (0,)))


def spread_kernel(
    top_ref, lead_ref, pan_ref, upper_ref, side_ref, full_ref, low_ref, cols_ref,
    block_ref, inv_ref, work_ref, send_sem, recv_sem, local_sem,
):
    wires = Wires(send_sem, recv_sem)
    row, col = wires.row, wires.col
    fresh, remote = wires.fresh, wires.remote
    wires.greet(wires.col_others())

    def panel_piece(slot, half, part):
        if part == 0:
            return pan_ref.at[half, pl.ds(slot * SLICE, SLICE)]
        size = SLICE // 2
        return pan_ref.at[half, pl.ds(slot * SLICE + size * (part - 1), size)]

    spread = []
    for half in range(2):
        spread.append((half, 2 * row + half, pl.ds(0, COL_WIDTH), pl.ds(0, COL_WIDTH)))
    spread_recv = [fresh() for _ in spread]
    spread_send = [fresh(COLS) for _ in spread]

    def spread_copy(index, step):
        half, _, lanes, to_lanes = spread[index]
        to_col = lax.rem(col + step, COLS)
        rows = pl.ds(to_col * SLICE, SLICE)
        return remote(
            top_ref.at[rows, lanes],
            pan_ref.at[half, rows, to_lanes],
            spread_send[index] + step,
            spread_recv[index],
            row,
            to_col,
        )

    def spread_start(index):
        half, holder, lanes, to_lanes = spread[index]
        rows = pl.ds(col * SLICE, SLICE)

        @pl.when(col == holder)
        def _():
            keep = pltpu.make_async_copy(
                top_ref.at[rows, lanes], pan_ref.at[half, rows, to_lanes], local_sem.at[index]
            )
            keep.start()

            @pl.loop(1, COLS)
            def _(step):
                spread_copy(index, step).start()

            keep.wait()

    def spread_wait(index):
        @pl.when(col != spread[index][1])
        def _():
            spread_copy(index, 1).wait_recv()

    def spread_drain(index):
        @pl.when(col == spread[index][1])
        def _():
            @pl.loop(1, COLS)
            def _(step):
                spread_copy(index, step).wait_send()

    for index in range(2):
        spread_start(index)
    steps = ring_steps(
        [wires.ring(h, panel_piece, lambda h=h: panel_piece(col, h, 0)) for h in range(2)]
    )

    def join_inverse(tile):
        first, second, side = inv_ref[2 * tile], inv_ref[2 * tile + 1], side_ref[tile]
        full_ref[tile, NEAR, NEAR] = first
        full_ref[tile, NEAR, AWAY] = jnp.zeros((BLOCK, BLOCK), F32)
        full_ref[tile, AWAY, NEAR] = -product(second, product(side, first))
        full_ref[tile, AWAY, AWAY] = second

    def second_half(tile, below, corner):
        side = product_rows(below, inv_ref[2 * tile])
        side_ref[tile] = side
        block_ref[...] = corner - product_rows(side, side)

    def body(number, carry):
        @pl.when(number == 0)
        def _():
            block_ref[...] = lead_ref[NEAR, NEAR]

        @pl.when(number == 1)
        def _():
            second_half(0, lead_ref[AWAY, NEAR], lead_ref[AWAY, AWAY])

        @pl.when(number == 2)
        def _():
            for index in range(2):
                spread_wait(index)
            for run in steps[:4]:
                run()
            join_inverse(0)
            low = product_rows(lead_ref[TILE:, :TILE], full_ref[0])
            low_ref[...] = low
            work_ref[...] = lead_ref[TILE:, TILE:] - product_rows(low, low)
            block_ref[...] = work_ref[NEAR, NEAR]

        @pl.when(number == 3)
        def _():
            for run in steps[4:8]:
                run()
            second_half(1, work_ref[AWAY, NEAR], work_ref[AWAY, AWAY])

        eliminate(block_ref, upper_ref.at[number], inv_ref.at[number])
        return carry

    lax.fori_loop(0, 4, body, 0)
    for run in steps[8:12]:
        run()
    join_inverse(1)
    inverses = [halves(full_ref[t]) for t in range(2)]
    low = halves(low_ref[...])
    blank = jnp.zeros((BLOCK, BLOCK), F32)
    for part in range(PCT):
        for run in steps[12 + 2 * part : 14 + 2 * part]:
            run()
        lanes = slice(part * TILE, (part + 1) * TILE)
        first, second = triangular(inverses, low, top_ref[:, lanes])
        cols_ref[:TILE, lanes] = first
        cols_ref[TILE:, lanes] = second

    @pl.when(col == 0)
    def _():
        for t in range(2):
            for r, c, value in (
                (0, 0, upper_ref[2 * t]),
                (0, 1, side_ref[t].T),
                (1, 0, blank),
                (1, 1, upper_ref[2 * t + 1]),
            ):
                r0, c0 = t * TILE + r * BLOCK, t * TILE + c * BLOCK
                cols_ref[r0 : r0 + BLOCK, c0 : c0 + BLOCK] = value
        cols_ref[TILE:, :TILE] = jnp.zeros((TILE, TILE), F32)

    for run in steps[20:]:
        run()
    wires.drain()
    for index in range(2):
        spread_drain(index)


def gather_tiles(order, own_factor, front):
    anywhere = pl.BlockSpec(memory_space=pl.ANY)
    vmem = pl.BlockSpec(memory_space=pltpu.VMEM)
    return pl.pallas_call(
        gather_kernel,
        out_shape=(
            jax.ShapeDtypeStruct((COLS, TILE, TILE), F32),
            jax.ShapeDtypeStruct((LEAD, COL_WIDTH), F32),
            jax.ShapeDtypeStruct((COLS, 2, SLICE // 2, LEAD), F32),
        ),
        in_specs=[pl.BlockSpec(memory_space=pltpu.SMEM), vmem, anywhere],
        out_specs=(vmem,) * 3,
        scratch_shapes=[
            pltpu.VMEM((COLS, TILE, CW), F32),
            pltpu.VMEM((TILE, CW), BF16),
            pltpu.VMEM((TILE, CW), BF16),
            pltpu.VMEM((SLICE, LEAD), F32),
            pltpu.SemaphoreType.DMA((136,)),
            pltpu.SemaphoreType.DMA((136,)),
            pltpu.SemaphoreType.DMA((4,)),
        ],
        compiler_params=pltpu.CompilerParams(
            collective_id=0, has_side_effects=True, vmem_limit_bytes=56 * 2**20
        ),
        name="gather",
    )(order, own_factor, front)


def spread_panel(top, lead):
    vmem = pl.BlockSpec(memory_space=pltpu.VMEM)
    return pl.pallas_call(
        spread_kernel,
        out_shape=(
            jax.ShapeDtypeStruct((2, LEAD, COL_WIDTH), F32),
            jax.ShapeDtypeStruct((4, BLOCK, BLOCK), F32),
            jax.ShapeDtypeStruct((2, BLOCK, BLOCK), F32),
            jax.ShapeDtypeStruct((2, TILE, TILE), F32),
            jax.ShapeDtypeStruct((TILE, TILE), F32),
            jax.ShapeDtypeStruct((LEAD, COL_WIDTH), F32),
        ),
        in_specs=[vmem, vmem],
        out_specs=(vmem,) * 6,
        scratch_shapes=[
            pltpu.VMEM((BLOCK, BLOCK), F32),
            pltpu.VMEM((4, BLOCK, BLOCK), F32),
            pltpu.VMEM((TILE, TILE), F32),
            pltpu.SemaphoreType.DMA((80,)),
            pltpu.SemaphoreType.DMA((80,)),
            pltpu.SemaphoreType.DMA((3,)),
        ],
        compiler_params=pltpu.CompilerParams(
            collective_id=1, has_side_effects=True, vmem_limit_bytes=56 * 2**20
        ),
        cost_estimate=pl.CostEstimate(
            flops=30 * 10**9, bytes_accessed=20 * 2**20, transcendentals=0
        ),
        name="spread",
    )(top, lead)


def eliminate(block_ref, upper_ref, inverse_ref):
    shape = (GROUP, BLOCK)
    lanes = lax.broadcasted_iota(jnp.int32, shape, 1)
    sublanes = lax.broadcasted_iota(jnp.int32, shape, 0)
    left = [block_ref[GROUP * g : GROUP * (g + 1), :] for g in range(GROUPS)]
    right = [jnp.where(lanes == sublanes + GROUP * g, 1.0, 0.0) for g in range(GROUPS)]
    for g in range(GROUPS):
        base = GROUP * g
        row_l = [jnp.broadcast_to(left[g][s : s + 1, :], shape) for s in range(GROUP)]
        row_r = [jnp.broadcast_to(right[g][s : s + 1, :], shape) for s in range(GROUP)]
        entry = {}
        for s in range(GROUP):
            for t in range(s, GROUP):
                entry[s, t] = jnp.broadcast_to(row_l[s][:, base + t : base + t + 1], shape)
        recip = []
        ratio = {}
        for s in range(GROUP):
            recip.append(1.0 / entry[s, s])
            for t in range(s + 1, GROUP):
                ratio[t, s] = entry[s, t] * recip[s]
            for t in range(s + 1, GROUP):
                for u in range(t, GROUP):
                    entry[t, u] = entry[t, u] - ratio[t, s] * entry[s, u]
        for s in range(GROUP):
            for t in range(s):
                row_l[s] = row_l[s] - ratio[s, t] * row_l[t]
                row_r[s] = row_r[s] - ratio[s, t] * row_r[t]
        new_l, new_r, scale = row_l[0], row_r[0], recip[0]
        for s in range(1, GROUP):
            pick = sublanes == s
            new_l = jnp.where(pick, row_l[s], new_l)
            new_r = jnp.where(pick, row_r[s], new_r)
            scale = jnp.where(pick, recip[s], scale)
        for i in range(g + 1, GROUPS):
            plain = []
            for s in range(GROUP):
                value = jnp.broadcast_to(left[i][:, base + s : base + s + 1], shape)
                for t in range(s):
                    value = value - plain[t] * ratio[s, t]
                plain.append(value)
            for s in range(GROUP):
                scaled = plain[s] * recip[s]
                left[i] = left[i] - scaled * row_l[s]
                right[i] = right[i] - scaled * row_r[s]
        scale = jnp.sqrt(scale)
        upper = jnp.where(lanes >= sublanes + base, new_l * scale, 0.0)
        upper_ref[base : base + GROUP, :] = upper
        inverse_ref[base : base + GROUP, :] = new_r * scale


def final_kernel(
    rows_ref, cols_ref, front_ref, pan_ref, right_ref, upper_ref, side_ref, full_ref, low_ref,
    tiles_ref, panel_ref, out_ref, high_ref, small_ref,
):
    row = lax.axis_index("row")
    step = pl.program_id(0)
    inverses = [halves(full_ref[t]) for t in range(2)]
    low = halves(low_ref[...])
    blank = jnp.zeros((BLOCK, BLOCK), F32)

    @pl.when(step == 0)
    def _():
        high_ref[...], small_ref[...] = halves(right_ref[...])

    first, second = triangular(inverses, low, pan_ref[0])
    panel_ref[:, :TILE] = first.T
    panel_ref[:, TILE:] = second.T

    for t in range(2):

        @pl.when((row == 0) & (step == t))
        def _(t=t):
            for r, c, value in (
                (0, 0, upper_ref[2 * t].T),
                (0, 1, blank),
                (1, 0, side_ref[t]),
                (1, 1, upper_ref[2 * t + 1].T),
            ):
                r0, c0 = r * BLOCK, t * TILE + c * BLOCK
                panel_ref[r0 : r0 + BLOCK, c0 : c0 + BLOCK] = value
            if t == 0:
                panel_ref[:, TILE:] = jnp.zeros((TILE, TILE), F32)

    left = halves(panel_ref[...])
    for part in range(PCT):
        span = slice(part * TILE, (part + 1) * TILE)
        right = (high_ref[:, span], small_ref[:, span])
        out_ref[:, span] = front_ref[:, span] - three_pass(left, right, ((1,), (0,)))
    block = step // PCT
    for child in range(ROWS):

        @pl.when(rows_ref[child, block] == step)
        def _(child=child):
            start = pl.multiple_of(cols_ref[child] * TILE, TILE)
            out_ref[:, pl.ds(start, TILE)] -= tiles_ref[child, 0]


def finish(row_places, col_places, front, pan, top, upper, side, full, low, tiles):
    return pl.pallas_call(
        final_kernel,
        out_shape=(
            jax.ShapeDtypeStruct((PANEL_ROWS, LEAD), F32),
            jax.ShapeDtypeStruct((PANEL_ROWS, COL_WIDTH), F32),
        ),
        grid_spec=pltpu.PrefetchScalarGridSpec(
            num_scalar_prefetch=2,
            grid=(RT,),
            in_specs=[
                pl.BlockSpec((TILE, COL_WIDTH), lambda i, *_: (i, 0)),
                pl.BlockSpec((1, LEAD, TILE), lambda i, *_: (i // PCT, 0, lax.rem(i, PCT))),
                pl.BlockSpec((LEAD, COL_WIDTH), lambda i, *_: (0, 0)),
                pl.BlockSpec((4, BLOCK, BLOCK), lambda i, *_: (0, 0, 0)),
                pl.BlockSpec((2, BLOCK, BLOCK), lambda i, *_: (0, 0, 0)),
                pl.BlockSpec((2, TILE, TILE), lambda i, *_: (0, 0, 0)),
                pl.BlockSpec((TILE, TILE), lambda i, *_: (0, 0)),
                pl.BlockSpec((ROWS, 1, TILE, TILE), lambda i, *_: (0, i // PCT, 0, 0)),
            ],
            out_specs=(
                pl.BlockSpec((TILE, LEAD), lambda i, *_: (i, 0)),
                pl.BlockSpec((TILE, COL_WIDTH), lambda i, *_: (i, 0)),
            ),
            scratch_shapes=[
                pltpu.VMEM((LEAD, COL_WIDTH), BF16),
                pltpu.VMEM((LEAD, COL_WIDTH), BF16),
            ],
        ),
        compiler_params=pltpu.CompilerParams(vmem_limit_bytes=58 * 2**20),
        cost_estimate=pl.CostEstimate(
            flops=9 * PANEL_ROWS * COL_WIDTH * LEAD,
            bytes_accessed=30 * 2**20,
            transcendentals=0,
        ),
        name="finish",
    )(row_places, col_places, front, pan, top, upper, side, full, low, tiles)


def per_device(parent_front, child_panels, child_inverses, parent_index):
    here_row = lax.axis_index("row")
    here_col = lax.axis_index("col")
    own_factor = product_rows(child_panels[0], child_inverses[0])
    block_of = parent_index // PCT
    my_blocks = lax.dynamic_index_in_dim(block_of, here_row, 0, keepdims=False)
    ids = jnp.arange(COLS, dtype=jnp.int32)
    wanted = jnp.concatenate([ids, here_col[None].astype(jnp.int32)])
    order = jnp.sum(jnp.where(my_blocks[None, :] == wanted[:, None], ids[None, :], 0), axis=1)
    outgoing, top, lead = gather_tiles(order, own_factor, parent_front)
    lead = lead.reshape(LEAD, LEAD)
    outgoing = outgoing.reshape(ROWS, 2, TILE, TILE)
    tiles = lax.all_to_all(outgoing, "row", split_axis=0, concat_axis=0, tiled=True)

    row_blocks = 2 * here_row + jnp.arange(2, dtype=jnp.int32)
    row_places = (
        jnp.sum(
            jnp.where(
                block_of[:, None, :] == row_blocks[None, :, None], parent_index[:, None, :], 0
            ),
            axis=2,
        )
        - here_row * RT
    )
    col_places = (
        jnp.sum(jnp.where(block_of == here_col, parent_index, 0), axis=1) - here_col * PCT
    )

    top, lead, row_places, col_places = lax.optimization_barrier(
        (top, lead, row_places.astype(jnp.int32), col_places.astype(jnp.int32))
    )
    pan, upper, side, full, low, cols = spread_panel(top, lead)
    panel_out, schur = finish(
        row_places,
        col_places,
        parent_front,
        pan,
        cols,
        upper,
        side,
        full,
        low,
        tiles,
    )
    return (panel_out, schur)


def solution(mesh):
    placed = (P("row", "col"), P("row", "col", None), P("row", None, None), P())
    return jax.shard_map(
        per_device,
        mesh=mesh,
        in_specs=placed,
        out_specs=(P("row", None), P("row", "col")),
        check_vma=False,
    )
```
